128 devices in a mesh: seq: 8 (over x, core), head: 16 (over z, y).
Axes of the slice: x: 4, y: 4, z: 4, core: 2. Of those that a mesh axis runs over, the one named last changes fastest.
Arguments:
- moe_input: bfloat16 [16384, 1536], P(('seq', 'head')), may hold values from -6 to 6
- out_grad: bfloat16 [16384, 1536], P(('seq', 'head')), may hold values from -6 to 6
- route_ids: int32 [16384, 6], P(('seq', 'head')), may hold values from 0 to 63, all different within a row; in each aligned block of 128 rows (0 to 127, 128 to 255, ...) at most 16 rows name the same one
- route_gates: float32 [16384, 6], P(('seq', 'head')), may hold values from 0.05 to 0.35
- gate_halves: bfloat16 [128, 1536, 256], P(('seq', 'head')), may hold values from -0.15625 to 0.15625
- up_halves: bfloat16 [128, 1536, 256], P(('seq', 'head')), may hold values from -0.15625 to 0.15625
- down_halves: bfloat16 [128, 256, 1536], P(('seq', 'head')), may hold values from -0.25 to 0.25
- out_proj: bfloat16 [3072, 1536], P('head'), may hold values from -0.109375 to 0.109375
- ssd_x: float32 [16384, 3072], P('seq', 'head'), may hold values from -0.125 to 0.125
- b_proj: float32 [16384, 128], P('seq'), may hold values from -0.5 to 0.5
- c_proj: float32 [16384, 128], P('seq'), may hold values from -0.5 to 0.5
- log_decay: float32 [48, 16384], P('head', 'seq'), may hold values from -2.3 to 0, as said below
- skip_gain: float32 [48], P('head'), may hold values from 0.5 to 1.5
Outputs:
- resid_grad: bfloat16 [16384, 1536], P(('seq', 'head'))
- ssd_x_grad: float32 [16384, 3072], P('seq', 'head')
- b_grad: float32 [16384, 128], P(('seq', 'head'))
The draws below stay inside these ranges and needn't reach their ends.
Inputs may be any that keep to these rules, and one draw needn't show every extreme that they name: `route_ids`: each row names 6 different experts; the 128 rows of one device name any one expert at most 16 times, a bound that some block reaches. `log_decay`: negative.
All inputs are finite; a program needn't handle non-finite values.
Results may differ from the reference program's by a relative error of at most 0.0039.
Values may be sent and summed in bfloat16 or wider, within the bound.
No kernel may reach another device: no remote copies, remote signals or barrier semaphores. Data moves between devices by JAX's collectives and lax.ppermute only.
A program may use at most 128 MiB of HBM per device.

```python
import math
import jax
import jax.numpy as jnp
import numpy as np
from jax import lax

D = 1536
EXPERTS = 64
TOPK = 6
FFE = 512
SCAN_HEADS = 48
HEAD_DIM = 64
STATE = 128
BLOCK = 256
TOK_DEV = 128
HALF = 256
CAP = 16
SEQUENCE_TOKENS = 16384
N_SEQ = 8
N_HEAD = 16


def draw_log_decay(key, part):
    pick_key, fast_key, slow_key, span_key, rough_key, where_key, spike_depth_key = jax.random.split(key, 7)
    fast_share = 0.5
    is_fast = jax.random.uniform(pick_key, (SCAN_HEADS,), jnp.float32) < fast_share
    fast_rate = jnp.exp(jax.random.uniform(fast_key, (SCAN_HEADS,), jnp.float32, math.log(1.0 / 50.0), math.log(1.0 / 30.0)))
    slow_rate = jnp.exp(jax.random.uniform(slow_key, (SCAN_HEADS,), jnp.float32, math.log(0.1), math.log(0.8))) / SEQUENCE_TOKENS
    baseline_decay_rate = jnp.where(is_fast, fast_rate, slow_rate)
    span_count = SEQUENCE_TOKENS // BLOCK
    spread_multiplier = jnp.exp(jax.random.uniform(span_key, (SCAN_HEADS, span_count, 1), jnp.float32, math.log(0.5), math.log(2.0)))
    spread_multiplier = jnp.broadcast_to(spread_multiplier, (SCAN_HEADS, span_count, BLOCK)).reshape(SCAN_HEADS, SEQUENCE_TOKENS)
    jitter_level = jnp.exp(jax.random.uniform(rough_key, (SCAN_HEADS, SEQUENCE_TOKENS), jnp.float32, math.log(0.5), math.log(2.0)))
    spike_positions = jax.random.randint(where_key, (3,), 0, SEQUENCE_TOKENS)
    spike_depth = jax.random.uniform(spike_depth_key, (3, SCAN_HEADS), jnp.float32, 0.22, 0.69)
    spike_count = (jnp.arange(SEQUENCE_TOKENS, dtype=jnp.int32)[None, :] == spike_positions[:, None]).astype(jnp.float32)
    spike_events = jnp.einsum('dq,dc->qc', spike_depth, spike_count)
    return -(baseline_decay_rate[:, None] * spread_multiplier * jitter_level) - spike_events


def block_scale(own_key, dims, pieces, smallest, top_value):
    level, own = 1.0, jax.random.fold_in(own_key, 6)
    for dim, shards_of in pieces:
        heights = jnp.exp(jax.random.uniform(jax.random.fold_in(own, dim), (shards_of,), jnp.float32, smallest / len(pieces), top_value / len(pieces)))
        level = level * jnp.repeat(heights, dims[dim] // shards_of).reshape([-1 if axis == dim else 1 for axis in range(len(dims))])
    return level


def assign_block(stream_key, own, number, rows, amount, top, reach, lean):
    sequence = jax.random.permutation(stream_key, amount)
    crowded, ordinary = portions_of(amount, rows * top, reach, lean, True), portions_of(amount, rows * top, reach, lean, False)
    places = jnp.arange(amount)

    def named(lengths, offset_by):
        used = int((lengths > 0).sum())
        fixed = max(1, used // 4)
        passed = fixed + (places - fixed + offset_by * (used - fixed)) % max(1, amount - fixed)
        return jnp.zeros((amount,), jnp.int32).at[sequence[jnp.where(places < fixed, places, passed)]].set(jnp.asarray(lengths, jnp.int32))

    lengths = jnp.where(number % 4 == 0, named(crowded, number // 4), named(ordinary, number - number // 4 - 1))
    mixed = jax.random.permutation(jax.random.fold_in(own, 3), amount)
    source_of, sink = mixed[0:amount // 2 * 2:2], mixed[1:amount // 2 * 2:2]
    slack = jnp.minimum(lengths[source_of] - 1, reach - lengths[sink]) // 2
    slack = jnp.where((source_of == sequence[0]) | (sink == sequence[0]) | (lengths[sink] == 0), 0, jnp.maximum(slack, 0))
    passed = jax.random.randint(jax.random.fold_in(own, 4), (amount // 2,), 0, 1 << 20) % (slack + 1)
    lengths = lengths.at[source_of].add(-passed).at[sink].add(passed)
    members = jnp.searchsorted(jnp.cumsum(lengths), jnp.arange(rows * top), side="right").astype(jnp.int32)
    listing = members.reshape(top, rows).T
    listing = listing[jax.random.permutation(jax.random.fold_in(own, 1), rows)]
    offset_by = jax.random.randint(jax.random.fold_in(own, 2), (rows, 1), 0, top)
    return jnp.take_along_axis(listing, (jnp.arange(top)[None, :] + offset_by) % top, axis=1)


def portions_of(count, total, limit, slope, full):
    weights = [(1 << 20) // math.isqrt(rank ** slope) + 1 for rank in range(1, count + 1)]
    largest = limit if full else min(limit, max(-(-total // count), total * weights[0] // sum(weights)))
    least = 1 if total - largest >= count - 1 else 0
    holding, surplus = [largest] + [least] * (count - 1), total - largest - least * (count - 1)
    while surplus > 0:
        movable = [i for i in range(1, count) if holding[i] < largest] or [i for i in range(1, count) if holding[i] < limit]
        mass, remaining = sum([weights[i] for i in movable]), surplus
        for i in movable:
            more = min(limit - holding[i], max(1, remaining * weights[i] // mass), surplus)
            holding[i] = holding[i] + more
            surplus = surplus - more
    return np.array(holding)


def gaussian(stream_key, extent, deviation, reach, cuts=(), held_as=jnp.bfloat16):
    values = deviation * jax.random.normal(stream_key, extent, jnp.float32)
    if cuts:
        values = values * block_scale(stream_key, extent, cuts, -0.22, 0.18)
    return jnp.clip(values, -reach, reach).astype(held_as)


def setup_inputs(seed: int = 0) -> dict:
    splits = jax.random.split(jax.random.key(seed), 14)
    moe_input = gaussian(splits[0], (SEQUENCE_TOKENS, D), 1.0, 6.0, ((0, 128),))
    out_grad = gaussian(splits[1], (SEQUENCE_TOKENS, D), 1.0, 6.0, ((0, 128),))
    route_ids_keys = jax.random.split(jax.random.fold_in(splits[2], 1), SEQUENCE_TOKENS // TOK_DEV)
    route_ids_turns = jax.random.permutation(jax.random.fold_in(splits[2], 3), SEQUENCE_TOKENS // TOK_DEV)
    route_ids = jax.vmap(lambda own, number: assign_block(jax.random.fold_in(splits[2], 2), own, number, TOK_DEV, EXPERTS, TOPK, CAP, 2))(route_ids_keys, route_ids_turns).reshape((SEQUENCE_TOKENS, TOPK))
    route_gates = jnp.clip(0.05 + 0.29999999 * jax.random.uniform(splits[3], (SEQUENCE_TOKENS, TOPK), jnp.float32) ** block_scale(splits[3], (SEQUENCE_TOKENS, TOPK), ((0, 128),), -0.2, 0.2), 0.05, 0.35)
    gate_halves = gaussian(splits[4], (2 * EXPERTS, D, HALF), D ** -0.5, 0.15625, ((0, 128),))
    up_halves = gaussian(splits[5], (2 * EXPERTS, D, HALF), D ** -0.5, 0.15625, ((0, 128),))
    down_halves = gaussian(splits[6], (2 * EXPERTS, HALF, D), FFE ** -0.5, 0.25, ((0, 128),))
    out_proj = gaussian(splits[7], (SCAN_HEADS * HEAD_DIM, D), (SCAN_HEADS * HEAD_DIM) ** -0.5, 0.109375, ((0, 16),))
    ssd_x = gaussian(splits[8], (SEQUENCE_TOKENS, SCAN_HEADS * HEAD_DIM), 0.02, 0.125, ((0, 8), (1, 16)), jnp.float32)
    b_proj = gaussian(splits[9], (SEQUENCE_TOKENS, STATE), 0.09, 0.5, ((0, 8),), jnp.float32)
    c_proj = gaussian(splits[10], (SEQUENCE_TOKENS, STATE), 0.09, 0.5, ((0, 8),), jnp.float32)
    log_decay = draw_log_decay(jax.random.fold_in(splits[13], 71), 0)
    skip_gain = jnp.clip(0.5 + 1.0 * jax.random.uniform(splits[12], (SCAN_HEADS,), jnp.float32) ** block_scale(splits[12], (SCAN_HEADS,), ((0, 16),), -0.2, 0.2), 0.5, 1.5)
    return dict(moe_input=moe_input, out_grad=out_grad, route_ids=route_ids, route_gates=route_gates, gate_halves=gate_halves, up_halves=up_halves, down_halves=down_halves, out_proj=out_proj, ssd_x=ssd_x, b_proj=b_proj, c_proj=c_proj, log_decay=log_decay, skip_gain=skip_gain)


def reference(moe_input, out_grad, route_ids, route_gates, gate_halves, up_halves, down_halves, out_proj, ssd_x, b_proj, c_proj, log_decay, skip_gain):
    highest = lax.Precision.HIGHEST
    flat_ids = route_ids.reshape(-1)
    flat_gates = route_gates.reshape(-1)
    row_limit = N_SEQ * N_HEAD * CAP
    gate_full = gate_halves.reshape(EXPERTS, 2, D, HALF).transpose(0, 2, 1, 3).reshape(EXPERTS, D, FFE)
    up_full = up_halves.reshape(EXPERTS, 2, D, HALF).transpose(0, 2, 1, 3).reshape(EXPERTS, D, FFE)
    down_full = down_halves.reshape(EXPERTS, FFE, D)

    def one_expert(accumulated, expert):
        key_rank = jnp.where(flat_ids == expert, 0, 1).astype(jnp.int32)
        order = jnp.argsort(key_rank, stable=True)[:row_limit]
        matched = flat_ids[order] == expert
        token_index = (order // TOPK).astype(jnp.int32)
        zero_row = jnp.zeros((), moe_input.dtype)
        rows_in = jnp.where(matched[:, None], moe_input[token_index], zero_row)
        rows_grad = jnp.where(matched[:, None], out_grad[token_index], zero_row)
        gate_act = jnp.dot(rows_in, gate_full[expert], preferred_element_type=jnp.float32)
        up_act = jnp.dot(rows_in, up_full[expert], preferred_element_type=jnp.float32)
        hidden_grad = jnp.dot(rows_grad, down_full[expert].T, preferred_element_type=jnp.float32)
        sigmoid_act = jax.nn.sigmoid(gate_act)
        gate_grad = (hidden_grad * up_act * sigmoid_act * (1.0 + gate_act * (1.0 - sigmoid_act))).astype(jnp.bfloat16)
        up_grad = (hidden_grad * gate_act * sigmoid_act).astype(jnp.bfloat16)
        route_term = jnp.dot(gate_grad, gate_full[expert].T, preferred_element_type=jnp.float32)
        route_term = route_term + jnp.dot(up_grad, up_full[expert].T, preferred_element_type=jnp.float32)
        route_term = lax.optimization_barrier(route_term.astype(jnp.bfloat16))
        weight = jnp.where(matched, flat_gates[order], 0.0)
        accumulated = accumulated.at[token_index].add(weight[:, None] * route_term.astype(jnp.float32))
        return accumulated, None

    accumulated, _ = lax.scan(one_expert, jnp.zeros((SEQUENCE_TOKENS, D), jnp.float32), jnp.arange(EXPERTS, dtype=jnp.int32))
    resid_grad = (out_grad.astype(jnp.float32) + accumulated).astype(jnp.bfloat16)
    ssd_grad = jnp.dot(resid_grad, out_proj.T, preferred_element_type=jnp.float32)

    block_count = SEQUENCE_TOKENS // BLOCK
    grad_blocks = ssd_grad.reshape(block_count, BLOCK, SCAN_HEADS, HEAD_DIM)
    input_blocks = ssd_x.reshape(block_count, BLOCK, SCAN_HEADS, HEAD_DIM)
    b_blocks = b_proj.reshape(block_count, BLOCK, STATE)
    c_blocks = c_proj.reshape(block_count, BLOCK, STATE)
    decay_blocks = log_decay.reshape(SCAN_HEADS, block_count, BLOCK).transpose(1, 0, 2)
    causal = jnp.arange(BLOCK)[:, None] >= jnp.arange(BLOCK)[None, :]

    def block_step(carry, blocks_in):
        grad_block, input_block, b_block, c_block, decay_block = blocks_in
        within = jnp.cumsum(decay_block, axis=1)
        log_gap = within[:, :, None] - within[:, None, :]
        scores = jnp.dot(c_block, b_block.T, precision=highest)
        weights = jnp.where(causal[None], jnp.exp(jnp.where(causal[None], log_gap, 0.0)), 0.0) * scores[None]
        to_end = jnp.exp(within[:, -1:] - within)
        grad_x = jnp.einsum("hts,thp->shp", weights, grad_block, precision=highest)
        grad_x = grad_x + jnp.einsum("hs,sn,hpn->shp", to_end, b_block, carry, precision=highest)
        grad_x = grad_x + skip_gain[None, :, None] * grad_block
        inner_prod = jnp.einsum("thp,shp->hts", grad_block, input_block, precision=highest)
        grad_b = jnp.einsum("hts,tn->sn", weights * inner_prod, c_block, precision=highest)
        grad_b = grad_b + jnp.einsum("hs,shp,hpn->sn", to_end, input_block, carry, precision=highest)
        carry = jnp.exp(within[:, -1])[:, None, None] * carry + jnp.einsum("ht,thp,tn->hpn", jnp.exp(within), grad_block, c_block, precision=highest)
        return carry, (grad_x, grad_b)

    zero_state = jnp.zeros((SCAN_HEADS, HEAD_DIM, STATE), jnp.float32)
    _, (grad_x, grad_b) = lax.scan(block_step, zero_state, (grad_blocks, input_blocks, b_blocks, c_blocks, decay_blocks), reverse=True)
    return resid_grad, grad_x.reshape(SEQUENCE_TOKENS, SCAN_HEADS * HEAD_DIM), grad_b.reshape(SEQUENCE_TOKENS, STATE)
```

```python
import functools

import jax
import jax.numpy as jnp
from jax import lax
from jax.experimental import pallas as pl
from jax.experimental.pallas import tpu as pltpu
from jax.sharding import PartitionSpec as P

BLOCK = 256
SLOTS = 8
F32 = jnp.float32
BF16 = jnp.bfloat16
HIGHEST = lax.Precision.HIGHEST
NT = (((1,), (1,)), ((), ()))
NN = (((1,), (0,)), ((), ()))
TN = (((0,), (0,)), ((), ()))


def params(mib=48):
    return pltpu.CompilerParams(vmem_limit_bytes=mib << 20)


def cost(flops, bytes_accessed):
    return pl.CostEstimate(flops=int(flops), bytes_accessed=int(bytes_accessed), transcendentals=0)


def split(a):
    hi = a.astype(BF16)
    return hi, (a - hi.astype(F32)).astype(BF16)


def dot(a, b, dims):
    return lax.dot_general(a, b, dims, preferred_element_type=F32)


def dot_high(a, b, dims):
    return lax.dot_general(a, b, dims, precision=HIGHEST, preferred_element_type=F32)


def slot_experts(rows, toks):
    row = lax.broadcasted_iota(jnp.int32, (rows, toks), 0)
    dev, slot = row >> 3, row & 7
    x, core, z, y = dev >> 5, (dev >> 4) & 1, (dev >> 2) & 3, dev & 3
    expert = (2 * x + (y & 1)) * 8 + 2 * z + (y >> 1)
    return expert, 2 * slot + core


def select_kernel(ids_ref, rows_ref, sel_ref, out_ref):
    slots, toks = sel_ref.shape
    expert, rank = slot_experts(slots, toks)
    named = ids_ref[0:1, :] == expert
    for k in range(1, ids_ref.shape[0]):
        named = jnp.logical_or(named, ids_ref[k : k + 1, :] == expert)
    named = jnp.where(named, 1.0, 0.0)
    earlier = jnp.where(
        lax.broadcasted_iota(jnp.int32, (toks, toks), 0)
        < lax.broadcasted_iota(jnp.int32, (toks, toks), 1),
        1.0,
        0.0,
    )
    before = dot(named.astype(BF16), earlier.astype(BF16), NN)
    sel = jnp.where(before == rank.astype(F32), named, 0.0).astype(BF16)
    sel_ref[...] = sel
    out_ref[...] = dot(sel, rows_ref[...], NN).astype(BF16)


def second_kernel(ids_ref, gates_ref, sel_ref, rows_ref, out_ref, hi_ref, lo_ref):
    slots, toks = sel_ref.shape
    out_ref[...] = dot(sel_ref[...], rows_ref[...], NN).astype(BF16)
    expert, _ = slot_experts(slots, toks)
    gate = jnp.zeros((slots, toks), F32)
    for k in range(ids_ref.shape[0]):
        gate = jnp.where(ids_ref[k : k + 1, :] == expert, gates_ref[k : k + 1, :], gate)
    mix = (gate * sel_ref[...].astype(F32)).T
    hi, lo = split(mix)
    hi_ref[...] = hi
    lo_ref[...] = lo


def combine_kernel(hi_ref, lo_ref, rows_ref, grad_ref, out_ref):
    rows = rows_ref[...]
    total = dot(hi_ref[...], rows, NN) + dot(lo_ref[...], rows, NN)
    out_ref[...] = (grad_ref[...].astype(F32) + total).astype(BF16)


def load_weights(home, own, far, bufs, sem):
    def copies(sources):
        return [pltpu.make_async_copy(s, b, sem.at[i]) for i, (s, b) in enumerate(zip(sources, bufs))]

    @pl.when(pl.program_id(0) == 0)
    def _():
        @pl.when(home == 1)
        def _():
            for c in copies(own):
                c.start()

        @pl.when(home == 0)
        def _():
            for c in copies(far):
                c.start()

        for c in copies(own):
            c.wait()


def acts_kernel(home_ref, x_ref, *refs):
    own, far, (gate_ref, up_ref), bufs, sem = refs[:4], refs[4:8], refs[8:10], refs[10:14], refs[14]
    load_weights(home_ref[0], own, far, bufs, sem)
    x = x_ref[...]
    half = bufs[0].shape[2]
    for j in range(2):
        gate_ref[:, j * half : (j + 1) * half] = dot(x, bufs[j][0], NN)
        up_ref[:, j * half : (j + 1) * half] = dot(x, bufs[2 + j][0], NN)


def back_kernel(home_ref, g_ref, gate_ref, up_ref, *refs):
    own, far, out_ref, bufs, sem = refs[:6], refs[6:12], refs[12], refs[13:19], refs[19]
    load_weights(home_ref[0], own, far, bufs, sem)
    g = g_ref[...]
    half = bufs[0].shape[2]
    total = None
    for j in range(2):
        hidden = dot(g, bufs[4 + j][0], NT)
        gate_act = gate_ref[:, j * half : (j + 1) * half]
        up_act = up_ref[:, j * half : (j + 1) * half]
        sig = jax.nn.sigmoid(gate_act)
        gate_grad = (hidden * up_act * sig * (1.0 + gate_act * (1.0 - sig))).astype(BF16)
        up_grad = (hidden * gate_act * sig).astype(BF16)
        part = dot(gate_grad, bufs[j][0], NT) + dot(up_grad, bufs[2 + j][0], NT)
        total = part if total is None else total + part
    out_ref[...] = total.astype(BF16)


def prepare_kernel(d_ref, b_ref, c_ref, x_ref, w_ref, ts_ref, te_ref, xte_ref, bs_ref, tail_ref, tot_ref):
    heads, n = d_ref.shape
    dim = x_ref.shape[1] // heads
    row = lax.broadcasted_iota(jnp.int32, (n, n), 0)
    col = lax.broadcasted_iota(jnp.int32, (n, n), 1)
    tri = jnp.where(col <= row, 1.0, 0.0)
    spread = jnp.concatenate(
        [jnp.broadcast_to(d_ref[h : h + 1, :], (dim, n)) for h in range(heads)], axis=0
    )
    across = dot_high(spread, tri, NT)
    down = dot_high(tri, spread, NT)
    scores = dot_high(b_ref[...], c_ref[...], NT)
    later = col >= row
    for h in range(heads):
        gap = across[h * dim : h * dim + 1, :] - down[:, h * dim : h * dim + 1]
        w = jnp.where(later, jnp.exp(jnp.where(later, gap, 0.0)), 0.0) * scores
        w_ref[0, h] = w.astype(BF16)
    ts_ref[...] = jnp.exp(down)
    te = jnp.exp(down[n - 1 : n, :] - down)
    te_ref[...] = te
    xte_ref[...] = (x_ref[...] * te).astype(BF16)

    @pl.when(pl.program_id(0) == 0)
    def _():
        tot_ref[...] = jnp.zeros_like(tot_ref)

    block_sum = jnp.broadcast_to(across[:, n - 1 : n], tot_ref.shape)
    bs_ref[0] = block_sum
    tail_ref[0] = tot_ref[...]
    tot_ref[...] = tot_ref[...] + block_sum


def grad_kernel(r_ref, p_ref, c_ref, ts_ref, bs_ref, tot_ref, g_ref, fut_ref, pay_ref, carry_ref):
    @pl.when(pl.program_id(0) == 0)
    def _():
        carry_ref[...] = jnp.zeros_like(carry_ref)

    g = dot(r_ref[...], p_ref[...], NT)
    g_ref[...] = g
    ghi, glo = split(g * ts_ref[...])
    chi, clo = split(c_ref[...])
    state = dot(ghi, chi, TN) + dot(ghi, clo, TN) + dot(glo, chi, TN)
    carry = carry_ref[...]
    fut_ref[0] = carry
    carry = jnp.exp(bs_ref[0]) * carry + state
    carry_ref[...] = carry
    rows, lanes = carry.shape
    heads = 3
    dim = rows // heads
    pay_ref[0:rows, :] = carry
    pay_ref[rows:, :] = jnp.concatenate(
        [tot_ref[h * dim : h * dim + 1, :] for h in range(heads)]
        + [jnp.zeros((pay_ref.shape[0] - rows - heads, lanes), F32)],
        axis=0,
    )


def intra_kernel(w_ref, g_ref, x_ref, c_ref, skip_ref, gx_ref, ib_ref):
    heads = w_ref.shape[1]
    dim = g_ref.shape[1] // heads
    acc = None
    for h in range(heads):
        w = w_ref[0, h]
        cols = slice(h * dim, (h + 1) * dim)
        g = g_ref[:, cols]
        gb = g.astype(BF16)
        gx_ref[:, cols] = dot(w, gb, NN) + skip_ref[:, cols] * g
        inner = dot(x_ref[:, cols].astype(BF16), gb, NT)
        term = w.astype(F32) * inner
        acc = term if acc is None else acc + term
    ib_ref[...] = dot(acc.astype(BF16), c_ref[...].astype(BF16), NN)


def cross_b_kernel(*refs):
    pays, (fut_ref, tail_ref, xte_ref, ib_ref, pb_ref, all_ref, in_ref) = refs[:-7], refs[-7:]
    rows, lanes = in_ref.shape
    heads = 3
    dim = rows // heads

    @pl.when(pl.program_id(0) == 0)
    def _():
        acc = pays[0][0:rows, :]
        log = jnp.zeros((rows, lanes), F32)
        for prev, cur in zip(pays[:-1], pays[1:]):
            log = log + jnp.concatenate(
                [jnp.broadcast_to(prev[rows + h : rows + h + 1, :], (dim, lanes)) for h in range(heads)],
                axis=0,
            )
            acc = acc + jnp.exp(log) * cur[0:rows, :]
        in_ref[...] = acc

    future = fut_ref[0] + jnp.exp(tail_ref[0]) * in_ref[...]
    hi, lo = split(future)
    all_ref[0] = hi
    xte = xte_ref[...]
    pb_ref[...] = ib_ref[...] + dot(xte, hi, NN) + dot(xte, lo, NN)


def cross_x_kernel(all_ref, te_ref, b_ref, gx_ref, out_ref):
    bhi, blo = split(b_ref[...])
    fut = all_ref[0]
    out_ref[...] = gx_ref[...] + te_ref[...] * (dot(bhi, fut, NT) + dot(blo, fut, NT))


def whole(shape):
    zeros = (0,) * len(shape)
    return pl.BlockSpec(shape, lambda *_: zeros)


def shards(
    moe_input,
    out_grad,
    route_ids,
    route_gates,
    gate_halves,
    up_halves,
    down_halves,
    out_proj,
    ssd_x,
    b_proj,
    c_proj,
    log_decay,
    skip_gain,
):
    sds = jax.ShapeDtypeStruct
    toks, width = moe_input.shape
    n_seq, n_head = lax.axis_size("seq"), lax.axis_size("head")
    devices = n_seq * n_head
    slots = devices * SLOTS
    both = ("seq", "head")
    any_spec = pl.BlockSpec(memory_space=pl.ANY)
    smem_spec = pl.BlockSpec(memory_space=pltpu.SMEM)

    seq, head = lax.axis_index("seq"), lax.axis_index("head")
    home = ((seq & 1) == (head & 1)).astype(jnp.int32).reshape(1)
    over_y, over_core = [], []
    for s in range(n_seq):
        for h in range(n_head):
            if (s & 1) != (h & 1):
                over_y.append((s * n_head + h, s * n_head + (h ^ 1)))
            else:
                over_core.append((s * n_head + h, (s ^ 1) * n_head + h))
    halves = (gate_halves, up_halves, down_halves)
    y_halves = [lax.ppermute(a, both, over_y) for a in halves]
    far_own = [lax.ppermute(a, both, over_core) for a in halves]
    far_y = [lax.ppermute(a, both, over_core) for a in y_halves]

    ids_t, gates_t = route_ids.T, route_gates.T
    sel, send_input = pl.pallas_call(
        select_kernel,
        out_shape=(sds((slots, toks), BF16), sds((slots, width), BF16)),
        compiler_params=params(),
        cost_estimate=cost(2 * slots * toks * width, 4 << 20),
        name="select_rows",
    )(ids_t, moe_input)
    send_grad, mix_hi, mix_lo = pl.pallas_call(
        second_kernel,
        out_shape=(sds((slots, width), BF16), sds((toks, slots), BF16), sds((toks, slots), BF16)),
        compiler_params=params(),
        cost_estimate=cost(2 * slots * toks * width, 4 << 20),
        name="select_grads",
    )(ids_t, gates_t, sel, out_grad)

    def exchange(rows):
        shaped = rows.reshape(devices, SLOTS, width)
        return lax.all_to_all(shaped, both, split_axis=0, concat_axis=0, tiled=True).reshape(slots, width)

    recv_input = exchange(send_input)
    recv_grad = exchange(send_grad)

    tile = 256
    half = gate_halves.shape[2]
    hidden = 2 * half
    row_spec = pl.BlockSpec((tile, width), lambda i: (i, 0))
    act_spec = pl.BlockSpec((tile, hidden), lambda i: (i, 0))
    in_buf = pltpu.VMEM((1, width, half), BF16)
    out_buf = pltpu.VMEM((1, half, width), BF16)
    own = [a for o, y in zip(halves, y_halves) for a in (o, y)]
    far = [a for o, y in zip(far_own, far_y) for a in (o, y)]
    gate_act, up_act = pl.pallas_call(
        acts_kernel,
        grid=(slots // tile,),
        in_specs=[smem_spec, row_spec] + [any_spec] * 8,
        out_specs=(act_spec, act_spec),
        out_shape=(sds((slots, hidden), F32), sds((slots, hidden), F32)),
        scratch_shapes=[in_buf] * 4 + [pltpu.SemaphoreType.DMA((4,))],
        compiler_params=params(),
        cost_estimate=cost(4 * slots * width * hidden, 10 << 20),
        name="expert_acts",
    )(home, recv_input, *own[:4], *far[:4])
    expert_rows = pl.pallas_call(
        back_kernel,
        grid=(slots // tile,),
        in_specs=[smem_spec, row_spec, act_spec, act_spec] + [any_spec] * 12,
        out_specs=row_spec,
        out_shape=sds((slots, width), BF16),
        scratch_shapes=[in_buf] * 4 + [out_buf] * 2 + [pltpu.SemaphoreType.DMA((6,))],
        compiler_params=params(),
        cost_estimate=cost(6 * slots * width * hidden, 14 << 20),
        name="expert_back",
    )(home, recv_grad, gate_act, up_act, *own, *far)
    returned = exchange(expert_rows)
    resid_grad = pl.pallas_call(
        combine_kernel,
        out_shape=sds((toks, width), BF16),
        compiler_params=params(),
        cost_estimate=cost(4 * slots * toks * width, 4 << 20),
        name="combine_rows",
    )(mix_hi, mix_lo, returned, out_grad)

    heads = skip_gain.shape[0]
    inner = out_proj.shape[0]
    seq_rows, state = b_proj.shape
    blocks = seq_rows // BLOCK
    flip = lambda i: blocks - 1 - i
    tok_in = pl.BlockSpec((BLOCK, inner), lambda i: (flip(i), 0))
    tok_st = pl.BlockSpec((BLOCK, state), lambda i: (flip(i), 0))
    blk_st = pl.BlockSpec((1, inner, state), lambda i: (flip(i), 0, 0))
    blk_w = pl.BlockSpec((1, heads, BLOCK, BLOCK), lambda i: (flip(i), 0, 0, 0))
    weights, to_start, to_end, x_end, block_sum, tail, total = pl.pallas_call(
        prepare_kernel,
        grid=(blocks,),
        in_specs=[pl.BlockSpec((heads, BLOCK), lambda i: (0, flip(i))), tok_st, tok_st, tok_in],
        out_specs=(blk_w, tok_in, tok_in, tok_in, blk_st, blk_st, whole((inner, state))),
        out_shape=(
            sds((blocks, heads, BLOCK, BLOCK), BF16),
            sds((seq_rows, inner), F32),
            sds((seq_rows, inner), F32),
            sds((seq_rows, inner), BF16),
            sds((blocks, inner, state), F32),
            sds((blocks, inner, state), F32),
            sds((inner, state), F32),
        ),
        compiler_params=params(),
        cost_estimate=cost(4e9, 16 << 20),
        name="scan_prepare",
    )(log_decay, b_proj, c_proj, ssd_x)

    rows_all = lax.all_gather(resid_grad, "head", axis=0, tiled=True)
    pay_rows = inner + 8
    ssd_grad, future, payload = pl.pallas_call(
        grad_kernel,
        grid=(blocks,),
        in_specs=[
            pl.BlockSpec((BLOCK, width), lambda i: (flip(i), 0)),
            whole((inner, width)),
            tok_st,
            tok_in,
            blk_st,
            whole((inner, state)),
        ],
        out_specs=(tok_in, blk_st, whole((pay_rows, state))),
        out_shape=(
            sds((seq_rows, inner), F32),
            sds((blocks, inner, state), F32),
            sds((pay_rows, state), F32),
        ),
        scratch_shapes=[pltpu.VMEM((inner, state), F32)],
        compiler_params=params(),
        cost_estimate=cost(2 * seq_rows * width * inner, 12 << 20),
        name="scan_grad",
    )(rows_all, out_proj, c_proj, to_start, block_sum, total)

    pays = [
        lax.ppermute(payload, "seq", [(s, s - d) for s in range(d, n_seq)]) for d in range(1, n_seq)
    ]
    skip_row = jnp.repeat(skip_gain, inner // heads).reshape(1, inner)
    part_x, part_b = pl.pallas_call(
        intra_kernel,
        grid=(blocks,),
        in_specs=[blk_w, tok_in, tok_in, tok_st, whole((1, inner))],
        out_specs=(tok_in, tok_st),
        out_shape=(sds((seq_rows, inner), F32), sds((seq_rows, state), F32)),
        compiler_params=params(),
        cost_estimate=cost(4e9, 12 << 20),
        name="scan_intra",
    )(weights, ssd_grad, ssd_x, c_proj, skip_row)
    partial_b, future_all = pl.pallas_call(
        cross_b_kernel,
        grid=(blocks,),
        in_specs=[whole((pay_rows, state))] * (n_seq - 1) + [blk_st, blk_st, tok_in, tok_st],
        out_specs=(tok_st, blk_st),
        out_shape=(sds((seq_rows, state), F32), sds((blocks, inner, state), BF16)),
        scratch_shapes=[pltpu.VMEM((inner, state), F32)],
        compiler_params=params(),
        cost_estimate=cost(4e8, 8 << 20),
        name="scan_cross_b",
    )(*pays, future, tail, x_end, part_b)
    shares = lax.all_to_all(
        partial_b.reshape(n_head, seq_rows // n_head, state), "head", split_axis=0, concat_axis=0, tiled=True
    )
    grad_x = pl.pallas_call(
        cross_x_kernel,
        grid=(blocks,),
        in_specs=[blk_st, tok_in, tok_st, tok_in],
        out_specs=tok_in,
        out_shape=sds((seq_rows, inner), F32),
        compiler_params=params(),
        cost_estimate=cost(4e8, 8 << 20),
        name="scan_cross_x",
    )(future_all, to_end, b_proj, part_x)
    b_grad = jnp.sum(shares, axis=0)
    return (resid_grad, grad_x, b_grad)


def solution(mesh):
    return jax.shard_map(
        shards,
        mesh=mesh,
        in_specs=(
            P(("seq", "head"), None),
            P(("seq", "head"), None),
            P(("seq", "head"), None),
            P(("seq", "head"), None),
            P(("seq", "head"), None, None),
            P(("seq", "head"), None, None),
            P(("seq", "head"), None, None),
            P("head", None),
            P("seq", "head"),
            P("seq", None),
            P("seq", None),
            P("head", "seq"),
            P("head"),
        ),
        out_specs=(P(("seq", "head"), None), P("seq", "head"), P(("seq", "head"), None)),
        check_vma=False,
    )
```

```python
import functools

import jax
import jax.numpy as jnp
from jax import lax
from jax.experimental import pallas as pl
from jax.experimental.pallas import tpu as pltpu
from jax.sharding import PartitionSpec as P


BLOCK = 256
SLOTS = 8
F32 = jnp.float32
BF16 = jnp.bfloat16
HIGHEST = lax.Precision.HIGHEST
NT = (((1,), (1,)), ((), ()))
NN = (((1,), (0,)), ((), ()))


def params(limit=67043328):
    return pltpu.CompilerParams(vmem_limit_bytes=limit)


def cost(flops, bytes_accessed):
    return pl.CostEstimate(flops=int(flops), bytes_accessed=int(bytes_accessed), transcendentals=0)


def split(a):
    hi = a.astype(BF16)
    return hi, (a - hi.astype(F32)).astype(BF16)


def dot(a, b, dims):
    return lax.dot_general(a, b, dims, preferred_element_type=F32)


def dot_high(a, b, dims):
    return lax.dot_general(a, b, dims, precision=HIGHEST, preferred_element_type=F32)


def slot_experts(rows, toks):
    row = lax.broadcasted_iota(jnp.int32, (rows, toks), 0)
    dev, slot = row >> 3, row & 7
    x, core, z, y = dev >> 5, (dev >> 4) & 1, (dev >> 2) & 3, dev & 3
    expert = (2 * x + (y & 1)) * 8 + 2 * z + (y >> 1)
    return expert, 2 * slot + core


def select_kernel(ids_ref, rows_ref, sel_ref, out_ref):
    slots, toks = sel_ref.shape
    expert, rank = slot_experts(slots, toks)
    named = ids_ref[0:1, :] == expert
    for k in range(1, ids_ref.shape[0]):
        named = jnp.logical_or(named, ids_ref[k : k + 1, :] == expert)
    named = jnp.where(named, 1.0, 0.0)
    earlier = jnp.where(
        lax.broadcasted_iota(jnp.int32, (toks, toks), 0)
        < lax.broadcasted_iota(jnp.int32, (toks, toks), 1),
        1.0,
        0.0,
    )
    before = dot(named.astype(BF16), earlier.astype(BF16), NN)
    sel = jnp.where(before == rank.astype(F32), named, 0.0).astype(BF16)
    sel_ref[...] = sel
    out_ref[...] = dot(sel, rows_ref[...], NN).astype(BF16)


def second_kernel(ids_ref, gates_ref, sel_ref, rows_ref, out_ref, hi_ref, lo_ref):
    slots, toks = sel_ref.shape
    out_ref[...] = dot(sel_ref[...], rows_ref[...], NN).astype(BF16)
    expert, _ = slot_experts(slots, toks)
    gate = jnp.zeros((slots, toks), F32)
    for k in range(ids_ref.shape[0]):
        gate = jnp.where(ids_ref[k : k + 1, :] == expert, gates_ref[k : k + 1, :], gate)
    mix = (gate * sel_ref[...].astype(F32)).T
    hi, lo = split(mix)
    hi_ref[...] = hi
    lo_ref[...] = lo


def weights_kernel(home_ref, *refs):
    own, far, (cat_ref, cat_t_ref, down_t_ref), bufs, sem = refs[:6], refs[6:12], refs[12:15], refs[15:17], refs[17]
    half = bufs[0].shape[0]

    def copies(sources):
        targets = [cat_ref.at[:, pl.ds(k * half, half)] for k in range(4)] + list(bufs)
        return [
            pltpu.make_async_copy(s.at[0], t, sem.at[k]) for k, (s, t) in enumerate(zip(sources, targets))
        ]

    @pl.when(home_ref[0] == 1)
    def _():
        for c in copies(own):
            c.start()

    @pl.when(home_ref[0] == 0)
    def _():
        for c in copies(far):
            c.start()

    for k, c in enumerate(copies(own)):
        c.wait()
        if k < 4:
            cat_t_ref[k * half : (k + 1) * half, :] = cat_ref[:, k * half : (k + 1) * half].T
        else:
            down_t_ref[:, (k - 4) * half : (k - 3) * half] = bufs[k - 4][...].T


def acts_kernel(x_ref, w_ref, out_ref):
    act = dot(x_ref[...], w_ref[...], NN)
    hidden = act.shape[1] // 2
    gate, up = act[:, :hidden], act[:, hidden:]
    sig = jax.nn.sigmoid(gate)
    out_ref[:, :hidden] = up * sig * (1.0 + gate * (1.0 - sig))
    out_ref[:, hidden:] = gate * sig


def back_kernel(g_ref, act_ref, down_ref, cat_ref, out_ref, down_buf, cat_buf, sem):
    first = pl.program_id(0) == 0
    down_copy = pltpu.make_async_copy(down_ref, down_buf, sem.at[0])
    cat_copy = pltpu.make_async_copy(cat_ref, cat_buf, sem.at[1])

    @pl.when(first)
    def _():
        down_copy.start()
        cat_copy.start()
        down_copy.wait()

    grad = dot(g_ref[...], down_buf[...], NN)
    hidden = grad.shape[1]
    both = jnp.concatenate(
        [(grad * act_ref[:, :hidden]).astype(BF16), (grad * act_ref[:, hidden:]).astype(BF16)], axis=1
    )

    @pl.when(first)
    def _():
        cat_copy.wait()

    out_ref[...] = dot(both, cat_buf[...], NN).astype(BF16)


def combine_kernel(hi_ref, lo_ref, rows_ref, grad_ref, out_ref):
    rows = rows_ref[...]
    total = dot(hi_ref[...], rows, NN) + dot(lo_ref[...], rows, NN)
    out_ref[...] = (grad_ref[...].astype(F32) + total).astype(BF16)


def project_kernel(place_ref, own_ref, other_ref, near_ref, up_ref, far_a_ref, far_b_ref, dn_ref, out_ref, toks_ref, buf_ref, sem):
    core, z, y = place_ref[0], place_ref[1], place_ref[2]
    rows = near_ref.shape[0]
    copies = []
    at = 0
    for k, source in enumerate((near_ref, up_ref, far_a_ref, far_b_ref, dn_ref)):
        n = source.shape[0]
        copies.append(pltpu.make_async_copy(source, buf_ref.at[pl.ds(at, n)], sem.at[k]))
        at += n
    for c in copies:
        c.start()
    toks = own_ref.shape[0]
    toks_ref[pl.ds(pl.multiple_of(core * toks, toks), toks), :] = own_ref[...]
    toks_ref[pl.ds(pl.multiple_of((1 - core) * toks, toks), toks), :] = other_ref[...]
    both = toks_ref[...]
    part = out_ref.shape[2]
    waits = ((0,), (1,), (2, 3), (4,))
    for k, dz in enumerate((0, 3, 2, 1)):
        for w in waits[k]:
            copies[w].wait()
        g = dot(buf_ref[k * rows : (k + 1) * rows, :], both, NT).astype(BF16)
        for q, dy in enumerate((0, 3, 2, 1)):
            head = ((z + dz) & 3) * 4 + ((y + dy) & 3)
            for c in range(2):
                out_ref[c, head] = g[q * part : (q + 1) * part, c * toks : (c + 1) * toks]


def block_grads(g_ref, k):
    pieces = []
    for j in (2 * k, 2 * k + 1):
        pieces.append(jnp.concatenate([g_ref[0, j], g_ref[1, j]], axis=0))
    return jnp.concatenate(pieces, axis=1)


def head_rows(rows, heads, dim):
    n = rows.shape[1]
    return jnp.concatenate([jnp.broadcast_to(rows[h : h + 1, :], (dim, n)) for h in range(heads)], axis=0)


def prepare_kernel(
    d_ref, b_ref, c_ref, x_ref, wh_ref, wl_ref, ts_ref, te_ref, tt_ref, xh_ref, xl_ref, eh_ref, el_ref, th_ref, tl_ref,
    bs_ref, tot_ref,
):
    heads, n = d_ref.shape
    dim = x_ref.shape[0] // heads
    row = lax.broadcasted_iota(jnp.int32, (n, n), 0)
    col = lax.broadcasted_iota(jnp.int32, (n, n), 1)
    tri = jnp.where(col <= row, 1.0, 0.0)
    d = jnp.concatenate([d_ref[...], jnp.zeros((8 - heads, n), F32)], axis=0)
    across = dot_high(d, tri, NT)
    down = dot_high(tri, d, NT)
    scores = dot_high(b_ref[...], c_ref[...], NT)
    later = col >= row
    for h in range(heads):
        gap = across[h : h + 1, :] - down[:, h : h + 1]
        w = jnp.where(later, jnp.exp(jnp.where(later, gap, 0.0)), 0.0) * scores
        wh_ref[0, h], wl_ref[0, h] = split(w)

    @pl.when(pl.program_id(0) == 0)
    def _():
        tot_ref[...] = jnp.zeros_like(tot_ref)

    last = across[:, n - 1 : n]
    te = jnp.exp(last - across)
    tt = jnp.exp(last - across + tot_ref[:, 0:1])
    ts_ref[...] = jnp.exp(across)
    te_ref[...] = te
    tt_ref[...] = tt
    x = x_ref[...]
    xh_ref[...], xl_ref[...] = split(x.T)
    eh_ref[...], el_ref[...] = split((x * head_rows(te, heads, dim)).T)
    th_ref[...], tl_ref[...] = split((x * head_rows(tt, heads, dim)).T)
    block_sum = jnp.broadcast_to(last, tot_ref.shape)
    bs_ref[0] = block_sum
    tot_ref[...] = tot_ref[...] + block_sum


def state_kernel(heads, g_ref, c_ref, ts_ref, bs_ref, tot_ref, fut_ref, pay_ref):
    blocks, rows, lanes = fut_ref.shape
    dim = rows // heads
    n = c_ref.shape[0] // blocks
    states = []
    for k in range(blocks):
        at = slice(k * n, (k + 1) * n)
        g = block_grads(g_ref, k).astype(F32)
        ghi, glo = split(g * head_rows(ts_ref[:, at], heads, dim))
        chi, clo = split(c_ref[at, :])
        states.append(dot(ghi, chi, NN) + dot(ghi, clo, NN) + dot(glo, chi, NN))
    carry = jnp.zeros((rows, lanes), F32)
    for k in reversed(range(blocks)):
        fut_ref[k] = carry
        carry = head_rows(jnp.exp(bs_ref[k]), heads, dim) * carry + states[k]
    first = tot_ref[...]
    hi, _ = split(first)
    mid, low = split(first - hi.astype(F32))
    sent = jnp.concatenate([carry.astype(BF16), hi, mid, low, low], axis=0)
    for j in range(pay_ref.shape[0]):
        pay_ref[j] = sent


def intra_kernel(
    heads, skip_ref, wh_ref, wl_ref, g_ref, xh_ref, xl_ref, eh_ref, el_ref, te_ref, b_ref, c_ref, fut_ref, gx_ref, pb_ref
):
    n = wh_ref.shape[2]
    rows = gx_ref.shape[0]
    dim = rows // heads
    for k in range(wh_ref.shape[0]):
        at = slice(k * n, (k + 1) * n)
        fhi, flo = split(fut_ref[k])
        bhi, blo = split(b_ref[at, :])
        cross = dot(fhi, bhi, NT) + dot(flo, bhi, NT) + dot(fhi, blo, NT)
        cross = cross * head_rows(te_ref[:, at], heads, dim)
        acc = None
        grads = block_grads(g_ref, k)
        for h in range(heads):
            w = wh_ref[k, h]
            cols = slice(h * dim, (h + 1) * dim)
            g = grads[cols]
            gx_ref[cols, at] = dot(g, w, NT) + cross[cols] + skip_ref[h] * g.astype(F32)
            inner = dot(xh_ref[at, cols], g, NN) + dot(xl_ref[at, cols], g, NN)
            term = (w.astype(F32) + wl_ref[k, h].astype(F32)) * inner
            acc = term if acc is None else acc + term
        ahi, alo = split(acc)
        chi, clo = split(c_ref[at, :])
        eh = eh_ref[at, :]
        pb_ref[at, :] = (
            dot(ahi, chi, NN)
            + dot(alo, chi, NN)
            + dot(ahi, clo, NN)
            + dot(eh, fhi, NN)
            + dot(eh, flo, NN)
            + dot(el_ref[at, :], fhi, NN)
        )


def finish_b_kernel(heads, seq_ref, pay_ref, th_ref, tl_ref, pb_ref, out_ref, hi_ref, lo_ref):
    rows, lanes = hi_ref.shape
    dim = rows // heads

    @pl.when(pl.program_id(0) == 0)
    def _():
        place = seq_ref[0]
        acc = jnp.zeros((rows, lanes), F32)
        log = jnp.zeros((8, lanes), F32)
        for j in range(pay_ref.shape[0]):
            ahead = j > place
            factor = jnp.where(ahead, jnp.exp(log), 0.0)
            acc = acc + head_rows(factor, heads, dim) * pay_ref[j, 0:rows, :].astype(F32)
            tots = pay_ref[j, rows : rows + 32, :].astype(F32)
            log = log + jnp.where(ahead, tots[0:8] + tots[8:16] + tots[16:24], 0.0)
        hi_ref[...], lo_ref[...] = split(acc)

    hi = hi_ref[...]
    th = th_ref[...]
    total = pb_ref[...] + dot(th, hi, NN) + dot(th, lo_ref[...], NN) + dot(tl_ref[...], hi, NN)
    out_ref[...] = total.astype(out_ref.dtype)


def finish_x_kernel(heads, hi_ref, lo_ref, tt_ref, b_ref, gx_ref, out_ref):
    bhi, blo = split(b_ref[...])
    hi = hi_ref[...]
    tt = head_rows(tt_ref[...], heads, out_ref.shape[0] // heads)
    out_ref[...] = gx_ref[...] + tt * (dot(hi, bhi, NT) + dot(lo_ref[...], bhi, NT) + dot(hi, blo, NT))


def whole(shape):
    zeros = (0,) * len(shape)
    return pl.BlockSpec(shape, lambda *_: zeros)


def shards(
    moe_input,
    out_grad,
    route_ids,
    route_gates,
    gate_halves,
    up_halves,
    down_halves,
    out_proj,
    ssd_x,
    b_proj,
    c_proj,
    log_decay,
    skip_gain,
):
    sds = jax.ShapeDtypeStruct
    toks, width = moe_input.shape
    seq_axes = ("x", "core")
    n_seq, n_head = lax.axis_size(seq_axes), lax.axis_size("head")
    devices = n_seq * n_head
    slots = devices * SLOTS
    both = ("x", "core", "head")
    smem_spec = pl.BlockSpec(memory_space=pltpu.SMEM)
    any_spec = pl.BlockSpec(memory_space=pl.ANY)
    heads = skip_gain.shape[0]
    inner = out_proj.shape[0]
    seq_rows, state = b_proj.shape
    blocks = seq_rows // BLOCK
    seq, head = lax.axis_index(seq_axes), lax.axis_index("head")
    core = lax.axis_index("core")

    home = core == (head & 1)
    over_y, over_core = [], []
    for s in range(n_seq):
        for h in range(n_head):
            if (s & 1) != (h & 1):
                over_y.append((s * n_head + h, s * n_head + (h ^ 1)))
            else:
                over_core.append((s * n_head + h, (s ^ 1) * n_head + h))
    halves = (gate_halves, up_halves, down_halves)
    y_halves, far_own = [], []
    for a in halves:
        y_halves.append(lax.ppermute(a, both, over_y))
    for a in halves:
        far_own.append(lax.ppermute(a, both, over_core))
    far_y = [lax.ppermute(a, both, over_core) for a in y_halves]
    own = [a for o, y in zip(halves, y_halves) for a in (o, y)]
    far = [a for o, y in zip(far_own, far_y) for a in (o, y)]
    _, width, half = gate_halves.shape
    hidden = 2 * half
    expert_cat, expert_cat_t, expert_down_t = pl.pallas_call(
        weights_kernel,
        in_specs=[smem_spec] + [any_spec] * 12,
        out_shape=(sds((width, 2 * hidden), BF16), sds((2 * hidden, width), BF16), sds((width, hidden), BF16)),
        scratch_shapes=[pltpu.VMEM((half, width), BF16)] * 2 + [pltpu.SemaphoreType.DMA((6,))],
        compiler_params=params(),
        cost_estimate=cost(1e9, 12 << 20),
        name="expert_weights",
    )(home.astype(jnp.int32).reshape(1), *own, *far)

    ids_t, gates_t = route_ids.T, route_gates.T
    sel, send_input = pl.pallas_call(
        select_kernel,
        out_shape=(sds((slots, toks), BF16), sds((slots, width), BF16)),
        compiler_params=params(),
        cost_estimate=cost(2 * slots * toks * width, 4 << 20),
        name="select_rows",
    )(ids_t, moe_input)
    send_grad, mix_hi, mix_lo = pl.pallas_call(
        second_kernel,
        out_shape=(sds((slots, width), BF16), sds((toks, slots), BF16), sds((toks, slots), BF16)),
        compiler_params=params(),
        cost_estimate=cost(2 * slots * toks * width, 4 << 20),
        name="select_grads",
    )(ids_t, gates_t, sel, out_grad)

    def exchange(rows):
        shaped = rows.reshape(devices, SLOTS, width)
        return lax.all_to_all(shaped, both, split_axis=0, concat_axis=0, tiled=True).reshape(slots, width)

    recv_input = exchange(send_input)
    recv_grad = exchange(send_grad)

    part = inner // 2

    def shift(rows, dz, dy):
        pairs = [(z * 4 + y, (z + dz) % 4 * 4 + (y + dy) % 4) for z in range(4) for y in range(4)]
        return lax.ppermute(rows, "head", pairs)

    near = lax.dynamic_slice(out_proj, (core * part, 0), (part, width))
    up, dn = shift(near, 0, 1), shift(near, 0, -1)
    far_up = shift(up[: part // 2], 0, 1)
    far_dn = shift(dn[part // 2 :], 0, -1)
    line = jnp.concatenate([near, up, far_up, far_dn, dn], axis=0)
    z_up, z_dn = shift(line, 1, 0), shift(line, -1, 0)
    z_far_up = shift(z_up[: 2 * part], 1, 0)
    z_far_dn = shift(z_dn[2 * part :], -1, 0)

    flip = lambda i: blocks - 1 - i
    row_in = pl.BlockSpec((inner, BLOCK), lambda i: (0, flip(i)))
    tok_in = pl.BlockSpec((BLOCK, inner), lambda i: (flip(i), 0))
    tok_st = pl.BlockSpec((BLOCK, state), lambda i: (flip(i), 0))
    row_8 = pl.BlockSpec((8, BLOCK), lambda i: (0, flip(i)))
    blk_st = pl.BlockSpec((1, inner, state), lambda i: (flip(i), 0, 0))
    blk_8 = pl.BlockSpec((1, 8, state), lambda i: (flip(i), 0, 0))
    blk_w = pl.BlockSpec((1, heads, BLOCK, BLOCK), lambda i: (flip(i), 0, 0, 0))
    x_shape = sds((seq_rows, inner), BF16)
    w_shape = sds((blocks, heads, BLOCK, BLOCK), BF16)
    r_shape = sds((8, seq_rows), F32)
    w_hi, w_lo, to_start, to_end, to_last, x_hi, x_lo, e_hi, e_lo, t_hi, t_lo, block_sum, total = pl.pallas_call(
        prepare_kernel,
        grid=(blocks,),
        in_specs=[pl.BlockSpec((heads, BLOCK), lambda i: (0, flip(i))), tok_st, tok_st, row_in],
        out_specs=(blk_w,) * 2 + (row_8,) * 3 + (tok_in,) * 6 + (blk_8, whole((8, state))),
        out_shape=(w_shape,) * 2
        + (r_shape,) * 3
        + (x_shape,) * 6
        + (sds((blocks, 8, state), F32), sds((8, state), F32)),
        compiler_params=params(),
        cost_estimate=cost(4e9, 20 << 20),
        name="scan_prepare",
    )(log_decay, b_proj, c_proj, ssd_x.T)

    tile = 256
    row_spec = pl.BlockSpec((tile, width), lambda i: (i, 0))
    act_spec = pl.BlockSpec((tile, 2 * hidden), lambda i: (i, 0))
    factors = pl.pallas_call(
        acts_kernel,
        grid=(slots // tile,),
        in_specs=[row_spec, whole((width, 2 * hidden))],
        out_specs=act_spec,
        out_shape=sds((slots, 2 * hidden), F32),
        compiler_params=params(),
        cost_estimate=cost(4 * slots * width * hidden, 10 << 20),
        name="expert_acts",
    )(recv_input, expert_cat)
    expert_rows = pl.pallas_call(
        back_kernel,
        grid=(slots // tile,),
        in_specs=[row_spec, act_spec, any_spec, any_spec],
        out_specs=row_spec,
        out_shape=sds((slots, width), BF16),
        scratch_shapes=[
            pltpu.VMEM((width, hidden), BF16),
            pltpu.VMEM((2 * hidden, width), BF16),
            pltpu.SemaphoreType.DMA((2,)),
        ],
        compiler_params=params(),
        cost_estimate=cost(6 * slots * width * hidden, 14 << 20),
        name="expert_back",
    )(recv_grad, factors, expert_down_t, expert_cat_t)
    returned = exchange(expert_rows)

    resid_grad = pl.pallas_call(
        combine_kernel,
        out_shape=sds((toks, width), BF16),
        compiler_params=params(),
        cost_estimate=cost(4 * slots * toks * width, 4 << 20),
        name="combine_rows",
    )(mix_hi, mix_lo, returned, out_grad)
    resid_other = lax.ppermute(resid_grad, "core", [(0, 1), (1, 0)])
    grad_all = pl.pallas_call(
        project_kernel,
        grid=(1,),
        in_specs=[smem_spec] + [whole((toks, width))] * 2 + [any_spec] * 5,
        out_specs=whole((2, n_head, part, toks)),
        out_shape=sds((2, n_head, part, toks), BF16),
        scratch_shapes=[
            pltpu.VMEM((2 * toks, width), BF16),
            pltpu.VMEM((n_head * part, width), BF16),
            pltpu.SemaphoreType.DMA((5,)),
        ],
        compiler_params=params(),
        cost_estimate=cost(4 * n_head * part * toks * width, 7 << 20),
        name="project_rows",
    )(jnp.stack([core, head >> 2, head & 3]), resid_grad, resid_other, line, z_up, z_far_up, z_far_dn, z_dn)
    grads = lax.all_to_all(
        grad_all.reshape(2 * n_head, part, toks), ("core", "head"), split_axis=0, concat_axis=0, tiled=True
    ).reshape(2, n_head, part, toks)

    pay_rows = inner + 32
    future, payload = pl.pallas_call(
        functools.partial(state_kernel, heads),
        out_shape=(sds((blocks, inner, state), F32), sds((n_seq, pay_rows, state), BF16)),
        grid=(1,),
        in_specs=[
            whole((2, n_head, part, toks)),
            whole((seq_rows, state)),
            whole((8, seq_rows)),
            whole((blocks, 8, state)),
            whole((8, state)),
        ],
        out_specs=(whole((blocks, inner, state)), whole((n_seq, pay_rows, state))),
        compiler_params=params(),
        cost_estimate=cost(1e9, 4 << 20),
        name="scan_state",
    )(grads, c_proj, to_start, block_sum, total)
    pays = lax.all_to_all(payload, seq_axes, split_axis=0, concat_axis=0, tiled=True)
    pair = 2
    spec = lambda *shape: pl.BlockSpec(shape, lambda i: (i,) + (0,) * (len(shape) - 1))
    cols = lambda *shape: pl.BlockSpec(shape, lambda i: (0, i))
    tok_in2, tok_st2 = spec(pair * BLOCK, inner), spec(pair * BLOCK, state)
    row_in2, row_82 = cols(inner, pair * BLOCK), cols(8, pair * BLOCK)
    w_spec = spec(pair, heads, BLOCK, BLOCK)
    part_x, part_b = pl.pallas_call(
        functools.partial(intra_kernel, heads),
        grid=(blocks // pair,),
        in_specs=[smem_spec, w_spec, w_spec, pl.BlockSpec((2, pair * BLOCK // toks, part, toks), lambda i: (0, i, 0, 0))]
        + [tok_in2] * 4
        + [row_82, tok_st2, tok_st2, spec(pair, inner, state)],
        out_specs=(row_in2, tok_st2),
        out_shape=(sds((inner, seq_rows), F32), sds((seq_rows, state), F32)),
        compiler_params=params(),
        cost_estimate=cost(4e9, 16 << 20),
        name="scan_intra",
    )(skip_gain, w_hi, w_lo, grads, x_hi, x_lo, e_hi, e_lo, to_end, b_proj, c_proj, future)
    partial_b, in_hi, in_lo = pl.pallas_call(
        functools.partial(finish_b_kernel, heads),
        grid=(blocks // pair,),
        in_specs=[smem_spec, whole((n_seq, pay_rows, state)), tok_in2, tok_in2, tok_st2],
        out_specs=(tok_st2, whole((inner, state)), whole((inner, state))),
        out_shape=(sds((seq_rows, state), BF16), sds((inner, state), BF16), sds((inner, state), BF16)),
        compiler_params=params(),
        cost_estimate=cost(4e8, 6 << 20),
        name="scan_finish_b",
    )(seq.reshape(1), pays, t_hi, t_lo, part_b)
    shares = lax.all_to_all(
        partial_b.reshape(n_head, seq_rows // n_head, state), "head", split_axis=0, concat_axis=0, tiled=True
    )
    grad_x = pl.pallas_call(
        functools.partial(finish_x_kernel, heads),
        grid=(blocks // pair,),
        in_specs=[whole((inner, state)), whole((inner, state)), row_82, tok_st2, row_in2],
        out_specs=row_in2,
        out_shape=sds((inner, seq_rows), F32),
        compiler_params=params(),
        cost_estimate=cost(4e8, 6 << 20),
        name="scan_finish_x",
    )(in_hi, in_lo, to_last, b_proj, part_x)
    b_grad = jnp.sum(shares.astype(F32), axis=0)
    return (resid_grad, grad_x.T, b_grad)


def solution(mesh):
    n_seq, n_head = mesh.shape["seq"], mesh.shape["head"]
    fine = jax.sharding.Mesh(mesh.devices.reshape(n_seq // 2, 2, n_head), ("x", "core", "head"))

    seq, every = ("x", "core"), ("x", "core", "head")
    return jax.shard_map(
        shards,
        mesh=fine,
        in_specs=(
            P(every, None),
            P(every, None),
            P(every, None),
            P(every, None),
            P(every, None, None),
            P(every, None, None),
            P(every, None, None),
            P("head", None),
            P(seq, "head"),
            P(seq, None),
            P(seq, None),
            P("head", seq),
            P("head"),
        ),
        out_specs=(P(every, None), P(seq, "head"), P(every, None)),
        check_vma=False,
    )
```

```python
import functools

import jax
import jax.numpy as jnp
from jax import lax
from jax.experimental import pallas as pl
from jax.experimental.pallas import tpu as pltpu
from jax.sharding import PartitionSpec as P


BLOCK = 256
SLOTS = 8
F32 = jnp.float32
BF16 = jnp.bfloat16
HIGHEST = lax.Precision.HIGHEST
NT = (((1,), (1,)), ((), ()))
NN = (((1,), (0,)), ((), ()))


def params(limit=67043328):
    return pltpu.CompilerParams(vmem_limit_bytes=limit)


def cost(flops, bytes_accessed):
    return pl.CostEstimate(flops=int(flops), bytes_accessed=int(bytes_accessed), transcendentals=0)


def split(a):
    hi = a.astype(BF16)
    return hi, (a - hi.astype(F32)).astype(BF16)


def dot(a, b, dims):
    return lax.dot_general(a, b, dims, preferred_element_type=F32)


def dot_high(a, b, dims):
    return lax.dot_general(a, b, dims, precision=HIGHEST, preferred_element_type=F32)


def slot_experts(rows, toks):
    row = lax.broadcasted_iota(jnp.int32, (rows, toks), 0)
    dev, slot = row >> 3, row & 7
    x, core, z, y = dev >> 5, (dev >> 4) & 1, (dev >> 2) & 3, dev & 3
    expert = (2 * x + (y & 1)) * 8 + 2 * z + (y >> 1)
    return expert, 2 * slot + core


def select_kernel(ids_ref, rows_ref, sel_ref, out_ref):
    @pl.when(pl.program_id(0) == 0)
    def _():
        slots, toks = sel_ref.shape
        expert, rank = slot_experts(slots, toks)
        named = ids_ref[0:1, :] == expert
        for k in range(1, ids_ref.shape[0]):
            named = jnp.logical_or(named, ids_ref[k : k + 1, :] == expert)
        named = jnp.where(named, 1.0, 0.0)
        earlier = jnp.where(
            lax.broadcasted_iota(jnp.int32, (toks, toks), 0)
            < lax.broadcasted_iota(jnp.int32, (toks, toks), 1),
            1.0,
            0.0,
        )
        before = dot(named.astype(BF16), earlier.astype(BF16), NN)
        sel_ref[...] = jnp.where(before == rank.astype(F32), named, 0.0).astype(BF16)

    out_ref[...] = dot(sel_ref[...], rows_ref[...], NN).astype(BF16)


def second_kernel(ids_ref, gates_ref, sel_ref, rows_ref, out_ref, hi_ref, lo_ref):
    slots, toks = sel_ref.shape
    out_ref[...] = dot(sel_ref[...], rows_ref[...], NN).astype(BF16)
    expert, _ = slot_experts(slots, toks)
    gate = jnp.zeros((slots, toks), F32)
    for k in range(ids_ref.shape[0]):
        gate = jnp.where(ids_ref[k : k + 1, :] == expert, gates_ref[k : k + 1, :], gate)
    mix = (gate * sel_ref[...].astype(F32)).T
    hi, lo = split(mix)
    hi_ref[...] = hi
    lo_ref[...] = lo


def weights_kernel(home_ref, *refs):
    own, far, (cat_ref, cat_t_ref, down_t_ref), bufs, sem = refs[:6], refs[6:12], refs[12:15], refs[15:17], refs[17]
    half = bufs[0].shape[0]

    def copies(sources):
        targets = [cat_ref.at[:, pl.ds(k * half, half)] for k in range(4)] + list(bufs)
        return [
            pltpu.make_async_copy(s.at[0], t, sem.at[k]) for k, (s, t) in enumerate(zip(sources, targets))
        ]

    @pl.when(home_ref[0] == 1)
    def _():
        for c in copies(own):
            c.start()

    @pl.when(home_ref[0] == 0)
    def _():
        for c in copies(far):
            c.start()

    for k, c in enumerate(copies(own)):
        c.wait()
        if k < 4:
            cat_t_ref[k * half : (k + 1) * half, :] = cat_ref[:, k * half : (k + 1) * half].T
        else:
            down_t_ref[:, (k - 4) * half : (k - 3) * half] = bufs[k - 4][...].T


def acts_kernel(x_ref, w_ref, out_ref):
    act = dot(x_ref[...], w_ref[...], NN)
    hidden = act.shape[1] // 2
    gate, up = act[:, :hidden], act[:, hidden:]
    sig = jax.nn.sigmoid(gate)
    out_ref[:, :hidden] = up * sig * (1.0 + gate * (1.0 - sig))
    out_ref[:, hidden:] = gate * sig


def back_kernel(g_ref, act_ref, down_ref, cat_ref, out_ref, down_buf, cat_buf, sem):
    first = pl.program_id(0) == 0
    down_copy = pltpu.make_async_copy(down_ref, down_buf, sem.at[0])
    cat_copy = pltpu.make_async_copy(cat_ref, cat_buf, sem.at[1])

    @pl.when(first)
    def _():
        down_copy.start()
        cat_copy.start()
        down_copy.wait()

    grad = dot(g_ref[...], down_buf[...], NN)
    hidden = grad.shape[1]
    both = jnp.concatenate(
        [(grad * act_ref[:, :hidden]).astype(BF16), (grad * act_ref[:, hidden:]).astype(BF16)], axis=1
    )

    @pl.when(first)
    def _():
        cat_copy.wait()

    out_ref[...] = dot(both, cat_buf[...], NN).astype(BF16)


def combine_kernel(hi_ref, lo_ref, rows_ref, grad_ref, out_ref, first_ref, second_ref):
    rows = rows_ref[...]
    total = dot(hi_ref[...], rows, NN) + dot(lo_ref[...], rows, NN)
    resid = (grad_ref[...].astype(F32) + total).astype(BF16)
    out_ref[...] = resid
    half = first_ref.shape[0]
    first_ref[...] = resid[:half]
    second_ref[...] = resid[half:]


def project_kernel(y_ref, *refs):
    resids, projs, outs, toks_ref, buf_ref, sem = refs[:8], refs[8:13], refs[13:17], refs[17], refs[18], refs[19]
    copies = []
    at = 0
    for k, source in enumerate(projs):
        n = source.shape[0]
        copies.append(pltpu.make_async_copy(source, buf_ref.at[pl.ds(at, n)], sem.at[k]))
        at += n
    for c in copies:
        c.start()
    half = resids[0].shape[0]
    toks = 2 * half
    for k, source in enumerate(resids):
        place = ((y_ref[0] + (0, 3, 1, 2)[k // 2]) & 3) * toks + k % 2 * half
        toks_ref[pl.ds(pl.multiple_of(place, half), half), :] = source[...]
    line = toks_ref[...]
    rows = outs[0].shape[1]
    for k, waits in enumerate(((0,), (1,), (2, 3), (4,))):
        for w in waits:
            copies[w].wait()
        g = dot(buf_ref[k * rows : (k + 1) * rows, :], line, NT).astype(BF16)
        for q in range(4):
            outs[k][q] = g[:, q * toks : (q + 1) * toks]


def block_grads(g_ref, k):
    return jnp.concatenate([g_ref[2 * k], g_ref[2 * k + 1]], axis=1)


def head_rows(rows, heads, dim):
    n = rows.shape[1]
    return jnp.concatenate([jnp.broadcast_to(rows[h : h + 1, :], (dim, n)) for h in range(heads)], axis=0)


def prepare_kernel(
    d_ref, b_ref, c_ref, x_ref, wh_ref, wl_ref, ts_ref, te_ref, tt_ref, xh_ref, xl_ref, eh_ref, el_ref, th_ref, tl_ref,
    bs_ref, tot_ref,
):
    heads, n = d_ref.shape
    dim = x_ref.shape[0] // heads
    row = lax.broadcasted_iota(jnp.int32, (n, n), 0)
    col = lax.broadcasted_iota(jnp.int32, (n, n), 1)
    tri = jnp.where(col <= row, 1.0, 0.0)
    d = jnp.concatenate([d_ref[...], jnp.zeros((8 - heads, n), F32)], axis=0)
    across = dot_high(d, tri, NT)
    down = dot_high(tri, d, NT)
    scores = dot_high(b_ref[...], c_ref[...], NT)
    later = col >= row
    for h in range(heads):
        gap = across[h : h + 1, :] - down[:, h : h + 1]
        w = jnp.where(later, jnp.exp(jnp.where(later, gap, 0.0)), 0.0) * scores
        wh_ref[0, h], wl_ref[0, h] = split(w)

    @pl.when(pl.program_id(0) == 0)
    def _():
        tot_ref[...] = jnp.zeros_like(tot_ref)

    last = across[:, n - 1 : n]
    te = jnp.exp(last - across)
    tt = jnp.exp(last - across + tot_ref[:, 0:1])
    ts_ref[...] = jnp.exp(across)
    te_ref[...] = te
    tt_ref[...] = tt
    x = x_ref[...]
    xh_ref[...], xl_ref[...] = split(x.T)
    eh_ref[...], el_ref[...] = split((x * head_rows(te, heads, dim)).T)
    th_ref[...], tl_ref[...] = split((x * head_rows(tt, heads, dim)).T)
    block_sum = jnp.broadcast_to(last, tot_ref.shape)
    bs_ref[0] = block_sum
    tot_ref[...] = tot_ref[...] + block_sum


def state_kernel(heads, z_ref, g0_ref, g1_ref, g2_ref, g3_ref, c_ref, ts_ref, bs_ref, tot_ref, fut_ref, pay_ref, g_ref):
    blocks, rows, lanes = fut_ref.shape
    dim = rows // heads
    n = c_ref.shape[0] // blocks
    for dz, source in enumerate((g0_ref, g1_ref, g2_ref, g3_ref)):
        g_ref[pl.ds(((z_ref[0] + dz) & 3) * 4, 4)] = source[...]
    states = []
    for k in range(blocks):
        at = slice(k * n, (k + 1) * n)
        g = block_grads(g_ref, k).astype(F32)
        ghi, glo = split(g * head_rows(ts_ref[:, at], heads, dim))
        chi, clo = split(c_ref[at, :])
        states.append(dot(ghi, chi, NN) + dot(ghi, clo, NN) + dot(glo, chi, NN))
    carry = jnp.zeros((rows, lanes), F32)
    for k in reversed(range(blocks)):
        fut_ref[k] = carry
        carry = head_rows(jnp.exp(bs_ref[k]), heads, dim) * carry + states[k]
    first = tot_ref[...]
    hi, _ = split(first)
    mid, low = split(first - hi.astype(F32))
    sent = jnp.concatenate([carry.astype(BF16), hi, mid, low, low], axis=0)
    for j in range(pay_ref.shape[0]):
        pay_ref[j] = sent


def intra_kernel(heads, wh_ref, wl_ref, g_ref, xh_ref, xl_ref, eh_ref, el_ref, c_ref, fut_ref, pb_ref):
    n = wh_ref.shape[2]
    dim = fut_ref.shape[1] // heads
    for k in range(wh_ref.shape[0]):
        at = slice(k * n, (k + 1) * n)
        fhi, flo = split(fut_ref[k])
        acc = None
        grads = block_grads(g_ref, k)
        for h in range(heads):
            cols = slice(h * dim, (h + 1) * dim)
            g = grads[cols]
            inner = dot(xh_ref[at, cols], g, NN) + dot(xl_ref[at, cols], g, NN)
            term = (wh_ref[k, h].astype(F32) + wl_ref[k, h].astype(F32)) * inner
            acc = term if acc is None else acc + term
        ahi, alo = split(acc)
        chi, clo = split(c_ref[at, :])
        eh = eh_ref[at, :]
        pb_ref[at, :] = (
            dot(ahi, chi, NN)
            + dot(alo, chi, NN)
            + dot(ahi, clo, NN)
            + dot(eh, fhi, NN)
            + dot(eh, flo, NN)
            + dot(el_ref[at, :], fhi, NN)
        )


def finish_b_kernel(heads, seq_ref, pay_ref, th_ref, tl_ref, pb_ref, out_ref, in_ref, th_buf, tl_buf, pb_buf, sem):
    steps, n = th_buf.shape[0], th_buf.shape[1]
    copies = [
        [
            pltpu.make_async_copy(source.at[pl.ds(i * n, n)], buf.at[i], sem.at[k, i])
            for k, (source, buf) in enumerate(((th_ref, th_buf), (tl_ref, tl_buf), (pb_ref, pb_buf)))
        ]
        for i in range(steps)
    ]
    for step in copies:
        for c in step:
            c.start()
    rows, lanes = in_ref.shape
    dim = rows // heads
    place = seq_ref[0]
    acc = jnp.zeros((rows, lanes), F32)
    log = jnp.zeros((8, lanes), F32)
    for j in range(pay_ref.shape[0]):
        ahead = j > place
        factor = jnp.where(ahead, jnp.exp(log), 0.0)
        acc = acc + head_rows(factor, heads, dim) * pay_ref[j, 0:rows, :].astype(F32)
        tots = pay_ref[j, rows : rows + 32, :].astype(F32)
        log = log + jnp.where(ahead, tots[0:8] + tots[8:16] + tots[16:24], 0.0)
    in_ref[...] = acc
    hi, lo = split(acc)
    for i in range(steps):
        for c in copies[i]:
            c.wait()
        th = th_buf[i]
        total = pb_buf[i] + dot(th, hi, NN) + dot(th, lo, NN) + dot(tl_buf[i], hi, NN)
        out_ref[i * n : (i + 1) * n, :] = total.astype(out_ref.dtype)


def finish_x_kernel(heads, skip_ref, wh_ref, g_ref, te_ref, tt_ref, b_ref, fut_ref, in_ref, out_ref):
    n = wh_ref.shape[2]
    rows = out_ref.shape[0]
    dim = rows // heads
    ihi, ilo = split(in_ref[...])
    for k in range(wh_ref.shape[0]):
        at = slice(k * n, (k + 1) * n)
        fhi, flo = split(fut_ref[k])
        bhi, blo = split(b_ref[at, :])
        local = dot(fhi, bhi, NT) + dot(flo, bhi, NT) + dot(fhi, blo, NT)
        far = dot(ihi, bhi, NT) + dot(ilo, bhi, NT) + dot(ihi, blo, NT)
        cross = local * head_rows(te_ref[:, at], heads, dim) + far * head_rows(tt_ref[:, at], heads, dim)
        grads = block_grads(g_ref, k)
        for h in range(heads):
            cols = slice(h * dim, (h + 1) * dim)
            g = grads[cols]
            out_ref[cols, at] = dot(g, wh_ref[k, h], NT) + cross[cols] + skip_ref[h] * g.astype(F32)


def whole(shape):
    zeros = (0,) * len(shape)
    return pl.BlockSpec(shape, lambda *_: zeros)


def shards(
    moe_input,
    out_grad,
    route_ids,
    route_gates,
    gate_halves,
    up_halves,
    down_halves,
    out_proj,
    ssd_x,
    b_proj,
    c_proj,
    log_decay,
    skip_gain,
):
    sds = jax.ShapeDtypeStruct
    toks, width = moe_input.shape
    seq_axes = ("x", "core")
    n_seq, n_head = lax.axis_size(seq_axes), lax.axis_size("head")
    devices = n_seq * n_head
    slots = devices * SLOTS
    both = ("x", "core", "head")
    smem_spec = pl.BlockSpec(memory_space=pltpu.SMEM)
    any_spec = pl.BlockSpec(memory_space=pl.ANY)
    heads = skip_gain.shape[0]
    inner = out_proj.shape[0]
    seq_rows, state = b_proj.shape
    blocks = seq_rows // BLOCK
    seq, head = lax.axis_index(seq_axes), lax.axis_index("head")
    core = lax.axis_index("core")

    home = core == (head & 1)
    over_y, over_core = [], []
    for s in range(n_seq):
        for h in range(n_head):
            if (s & 1) != (h & 1):
                over_y.append((s * n_head + h, s * n_head + (h ^ 1)))
            else:
                over_core.append((s * n_head + h, (s ^ 1) * n_head + h))
    halves = (gate_halves, up_halves, down_halves)
    y_halves, far_own = [], []
    for a in halves:
        y_halves.append(lax.ppermute(a, both, over_y))
    for a in halves:
        far_own.append(lax.ppermute(a, both, over_core))
    far_y = [lax.ppermute(a, both, over_core) for a in y_halves]
    own = [a for o, y in zip(halves, y_halves) for a in (o, y)]
    far = [a for o, y in zip(far_own, far_y) for a in (o, y)]
    _, width, half = gate_halves.shape
    hidden = 2 * half
    expert_cat, expert_cat_t, expert_down_t = pl.pallas_call(
        weights_kernel,
        in_specs=[smem_spec] + [any_spec] * 12,
        out_shape=(sds((width, 2 * hidden), BF16), sds((2 * hidden, width), BF16), sds((width, hidden), BF16)),
        scratch_shapes=[pltpu.VMEM((half, width), BF16)] * 2 + [pltpu.SemaphoreType.DMA((6,))],
        compiler_params=params(),
        cost_estimate=cost(1e9, 12 << 20),
        name="expert_weights",
    )(home.astype(jnp.int32).reshape(1), *own, *far)

    strip = lambda rows: pl.BlockSpec((rows, width // 4), lambda i: (0, i))
    ids_t, gates_t = route_ids.T, route_gates.T
    sel, send_input = pl.pallas_call(
        select_kernel,
        grid=(4,),
        in_specs=[whole(ids_t.shape), strip(toks)],
        out_specs=(whole((slots, toks)), strip(slots)),
        out_shape=(sds((slots, toks), BF16), sds((slots, width), BF16)),
        compiler_params=params(),
        cost_estimate=cost(2 * slots * toks * width, 4 << 20),
        name="select_rows",
    )(ids_t, moe_input)
    send_grad, mix_hi, mix_lo = pl.pallas_call(
        second_kernel,
        out_shape=(sds((slots, width), BF16), sds((toks, slots), BF16), sds((toks, slots), BF16)),
        compiler_params=params(),
        cost_estimate=cost(2 * slots * toks * width, 4 << 20),
        name="select_grads",
    )(ids_t, gates_t, sel, out_grad)

    def exchange(rows):
        shaped = rows.reshape(devices, SLOTS, width)
        return lax.all_to_all(shaped, both, split_axis=0, concat_axis=0, tiled=True).reshape(slots, width)

    recv_input = exchange(send_input)
    recv_grad = exchange(send_grad)

    def shift(rows, dz, dy):
        pairs = [(z * 4 + y, (z + dz) % 4 * 4 + (y + dy) % 4) for z in range(4) for y in range(4)]
        return lax.ppermute(rows, "head", pairs)

    proj_up, proj_dn = shift(out_proj, 1, 0), shift(out_proj, -1, 0)
    proj_far_up = shift(proj_up[: inner // 2], 1, 0)
    proj_far_dn = shift(proj_dn[inner // 2 :], -1, 0)

    flip = lambda i: blocks - 1 - i
    row_in = pl.BlockSpec((inner, BLOCK), lambda i: (0, flip(i)))
    tok_in = pl.BlockSpec((BLOCK, inner), lambda i: (flip(i), 0))
    tok_st = pl.BlockSpec((BLOCK, state), lambda i: (flip(i), 0))
    row_8 = pl.BlockSpec((8, BLOCK), lambda i: (0, flip(i)))
    blk_st = pl.BlockSpec((1, inner, state), lambda i: (flip(i), 0, 0))
    blk_8 = pl.BlockSpec((1, 8, state), lambda i: (flip(i), 0, 0))
    blk_w = pl.BlockSpec((1, heads, BLOCK, BLOCK), lambda i: (flip(i), 0, 0, 0))
    x_shape = sds((seq_rows, inner), BF16)
    w_shape = sds((blocks, heads, BLOCK, BLOCK), BF16)
    r_shape = sds((8, seq_rows), F32)
    w_hi, w_lo, to_start, to_end, to_last, x_hi, x_lo, e_hi, e_lo, t_hi, t_lo, block_sum, total = pl.pallas_call(
        prepare_kernel,
        grid=(blocks,),
        in_specs=[pl.BlockSpec((heads, BLOCK), lambda i: (0, flip(i))), tok_st, tok_st, row_in],
        out_specs=(blk_w,) * 2 + (row_8,) * 3 + (tok_in,) * 6 + (blk_8, whole((8, state))),
        out_shape=(w_shape,) * 2
        + (r_shape,) * 3
        + (x_shape,) * 6
        + (sds((blocks, 8, state), F32), sds((8, state), F32)),
        compiler_params=params(),
        cost_estimate=cost(4e9, 20 << 20),
        name="scan_prepare",
    )(log_decay, b_proj, c_proj, ssd_x.T)

    tile = 256
    row_spec = pl.BlockSpec((tile, width), lambda i: (i, 0))
    act_spec = pl.BlockSpec((tile, 2 * hidden), lambda i: (i, 0))
    factors = pl.pallas_call(
        acts_kernel,
        grid=(slots // tile,),
        in_specs=[row_spec, whole((width, 2 * hidden))],
        out_specs=act_spec,
        out_shape=sds((slots, 2 * hidden), F32),
        compiler_params=params(),
        cost_estimate=cost(4 * slots * width * hidden, 10 << 20),
        name="expert_acts",
    )(recv_input, expert_cat)
    expert_rows = pl.pallas_call(
        back_kernel,
        grid=(slots // tile,),
        in_specs=[row_spec, act_spec, any_spec, any_spec],
        out_specs=row_spec,
        out_shape=sds((slots, width), BF16),
        scratch_shapes=[
            pltpu.VMEM((width, hidden), BF16),
            pltpu.VMEM((2 * hidden, width), BF16),
            pltpu.SemaphoreType.DMA((2,)),
        ],
        compiler_params=params(),
        cost_estimate=cost(6 * slots * width * hidden, 14 << 20),
        name="expert_back",
    )(recv_grad, factors, expert_down_t, expert_cat_t)
    returned = exchange(expert_rows)

    resid_grad, first, second = pl.pallas_call(
        combine_kernel,
        grid=(4,),
        in_specs=[whole((toks, slots))] * 2 + [strip(slots), strip(toks)],
        out_specs=(strip(toks), strip(toks // 2), strip(toks // 2)),
        out_shape=(sds((toks, width), BF16),) + (sds((toks // 2, width), BF16),) * 2,
        compiler_params=params(),
        cost_estimate=cost(4 * slots * toks * width, 4 << 20),
        name="combine_rows",
    )(mix_hi, mix_lo, returned, out_grad)
    up_first = shift(first, 0, 1)
    dn_second = shift(second, 0, -1)
    up_second = shift(second, 0, 1)
    dn_first = shift(first, 0, -1)
    far_first = shift(up_first, 0, 1)
    far_second = shift(dn_second, 0, -1)
    part_spec = whole((n_head // 4, inner, toks))
    part_shape = sds((n_head // 4, inner, toks), BF16)
    halves_spec = whole((toks // 2, width))
    to_0, to_3, to_2, to_1 = pl.pallas_call(
        project_kernel,
        grid=(1,),
        in_specs=[smem_spec] + [halves_spec] * 8 + [any_spec] * 5,
        out_specs=(part_spec,) * 4,
        out_shape=(part_shape,) * 4,
        scratch_shapes=[
            pltpu.VMEM((4 * toks, width), BF16),
            pltpu.VMEM((4 * inner, width), BF16),
            pltpu.SemaphoreType.DMA((5,)),
        ],
        compiler_params=params(24 << 20),
        cost_estimate=cost(32 * inner * toks * width, 7 << 20),
        name="project_rows",
    )(
        (head & 3).reshape(1),
        first,
        second,
        up_first,
        up_second,
        dn_first,
        dn_second,
        far_first,
        far_second,
        out_proj,
        proj_up,
        proj_far_up,
        proj_far_dn,
        proj_dn,
    )
    from_2 = shift(to_2, 2, 0)
    from_3 = shift(to_1, 1, 0)
    from_1 = shift(to_3, -1, 0)

    pay_rows = inner + 32
    future, payload, grads = pl.pallas_call(
        functools.partial(state_kernel, heads),
        out_shape=(
            sds((blocks, inner, state), F32),
            sds((n_seq, pay_rows, state), BF16),
            sds((n_head, inner, toks), BF16),
        ),
        grid=(1,),
        in_specs=[smem_spec]
        + [part_spec] * 4
        + [
            whole((seq_rows, state)),
            whole((8, seq_rows)),
            whole((blocks, 8, state)),
            whole((8, state)),
        ],
        out_specs=(
            whole((blocks, inner, state)),
            whole((n_seq, pay_rows, state)),
            whole((n_head, inner, toks)),
        ),
        compiler_params=params(),
        cost_estimate=cost(1e9, 4 << 20),
        name="scan_state",
    )((head >> 2).reshape(1), to_0, from_1, from_2, from_3, c_proj, to_start, block_sum, total)
    pays = lax.all_to_all(payload, seq_axes, split_axis=0, concat_axis=0, tiled=True)
    pair = 2
    spec = lambda *shape: pl.BlockSpec(shape, lambda i: (i,) + (0,) * (len(shape) - 1))
    cols = lambda *shape: pl.BlockSpec(shape, lambda i: (0, i))
    tok_in2, tok_st2 = spec(pair * BLOCK, inner), spec(pair * BLOCK, state)
    row_in2, row_82 = cols(inner, pair * BLOCK), cols(8, pair * BLOCK)
    w_spec = spec(pair, heads, BLOCK, BLOCK)
    g_spec = spec(pair * BLOCK // toks, inner, toks)
    f_spec = spec(pair, inner, state)
    part_b = pl.pallas_call(
        functools.partial(intra_kernel, heads),
        grid=(blocks // pair,),
        in_specs=[w_spec, w_spec, g_spec] + [tok_in2] * 4 + [tok_st2, f_spec],
        out_specs=tok_st2,
        out_shape=sds((seq_rows, state), F32),
        compiler_params=params(),
        cost_estimate=cost(4e9, 16 << 20),
        name="scan_intra",
    )(w_hi, w_lo, grads, x_hi, x_lo, e_hi, e_lo, c_proj, future)
    steps = 4
    partial_b, incoming = pl.pallas_call(
        functools.partial(finish_b_kernel, heads),
        grid=(1,),
        in_specs=[smem_spec, whole((n_seq, pay_rows, state))] + [any_spec] * 3,
        out_specs=(whole((seq_rows, state)), whole((inner, state))),
        out_shape=(sds((seq_rows, state), BF16), sds((inner, state), F32)),
        scratch_shapes=[pltpu.VMEM((steps, seq_rows // steps, inner), BF16)] * 2
        + [pltpu.VMEM((steps, seq_rows // steps, state), F32), pltpu.SemaphoreType.DMA((3, steps))],
        compiler_params=params(),
        cost_estimate=cost(4e8, 6 << 20),
        name="scan_finish_b",
    )(seq.reshape(1), pays, t_hi, t_lo, part_b)
    shares = lax.all_to_all(
        partial_b.reshape(n_head, seq_rows // n_head, state), "head", split_axis=0, concat_axis=0, tiled=True
    )
    grad_x = pl.pallas_call(
        functools.partial(finish_x_kernel, heads),
        grid=(blocks // pair,),
        in_specs=[smem_spec, w_spec, g_spec, row_82, row_82, tok_st2, f_spec, whole((inner, state))],
        out_specs=row_in2,
        out_shape=sds((inner, seq_rows), F32),
        compiler_params=params(),
        cost_estimate=cost(4e8, 6 << 20),
        name="scan_finish_x",
    )(skip_gain, w_hi, grads, to_end, to_last, b_proj, future, incoming)
    b_grad = jnp.sum(shares.astype(F32), axis=0)
    return (resid_grad, grad_x.T, b_grad)


def solution(mesh):
    n_seq, n_head = mesh.shape["seq"], mesh.shape["head"]
    fine = jax.sharding.Mesh(mesh.devices.reshape(n_seq // 2, 2, n_head), ("x", "core", "head"))

    seq, every = ("x", "core"), ("x", "core", "head")
    return jax.shard_map(
        shards,
        mesh=fine,
        in_specs=(
            P(every, None),
            P(every, None),
            P(every, None),
            P(every, None),
            P(every, None, None),
            P(every, None, None),
            P(every, None, None),
            P("head", None),
            P(seq, "head"),
            P(seq, None),
            P(seq, None),
            P("head", seq),
            P("head"),
        ),
        out_specs=(P(every, None), P(seq, "head"), P(every, None)),
        check_vma=False,
    )
```

```python
import functools

import jax
import jax.numpy as jnp
from jax import lax
from jax.experimental import pallas as pl
from jax.experimental.pallas import tpu as pltpu
from jax.sharding import PartitionSpec as P


BLOCK = 256
SLOTS = 8
F32 = jnp.float32
BF16 = jnp.bfloat16
HIGHEST = lax.Precision.HIGHEST
NT = (((1,), (1,)), ((), ()))
NN = (((1,), (0,)), ((), ()))


def params(limit=67043328):
    return pltpu.CompilerParams(vmem_limit_bytes=limit)


def cost(flops, bytes_accessed):
    return pl.CostEstimate(flops=int(flops), bytes_accessed=int(bytes_accessed), transcendentals=0)


def split(a):
    hi = a.astype(BF16)
    return hi, (a - hi.astype(F32)).astype(BF16)


def dot(a, b, dims):
    return lax.dot_general(a, b, dims, preferred_element_type=F32)


def dot_high(a, b, dims):
    return lax.dot_general(a, b, dims, precision=HIGHEST, preferred_element_type=F32)


def slot_experts(rows, toks):
    row = lax.broadcasted_iota(jnp.int32, (rows, toks), 0)
    dev, slot = row >> 3, row & 7
    x, core, z, y = dev >> 5, (dev >> 4) & 1, (dev >> 2) & 3, dev & 3
    expert = (2 * x + (y & 1)) * 8 + 2 * z + (y >> 1)
    return expert, 2 * slot + core


def select_kernel(ids_ref, rows_ref, sel_ref, out_ref):
    slots, toks = sel_ref.shape
    expert, rank = slot_experts(slots, toks)
    named = ids_ref[0:1, :] == expert
    for k in range(1, ids_ref.shape[0]):
        named = jnp.logical_or(named, ids_ref[k : k + 1, :] == expert)
    named = jnp.where(named, 1.0, 0.0)
    earlier = jnp.where(
        lax.broadcasted_iota(jnp.int32, (toks, toks), 0)
        < lax.broadcasted_iota(jnp.int32, (toks, toks), 1),
        1.0,
        0.0,
    )
    before = dot(named.astype(BF16), earlier.astype(BF16), NN)
    sel = jnp.where(before == rank.astype(F32), named, 0.0).astype(BF16)
    sel_ref[...] = sel
    out_ref[...] = dot(sel, rows_ref[...], NN).astype(BF16)


def second_kernel(ids_ref, gates_ref, sel_ref, rows_ref, out_ref, hi_ref, lo_ref):
    slots, toks = sel_ref.shape
    out_ref[...] = dot(sel_ref[...], rows_ref[...], NN).astype(BF16)
    expert, _ = slot_experts(slots, toks)
    gate = jnp.zeros((slots, toks), F32)
    for k in range(ids_ref.shape[0]):
        gate = jnp.where(ids_ref[k : k + 1, :] == expert, gates_ref[k : k + 1, :], gate)
    mix = (gate * sel_ref[...].astype(F32)).T
    hi, lo = split(mix)
    hi_ref[...] = hi
    lo_ref[...] = lo


def weights_kernel(home_ref, *refs):
    own, far, (cat_ref, cat_t_ref, down_t_ref), bufs, sem = refs[:6], refs[6:12], refs[12:15], refs[15:17], refs[17]
    half = bufs[0].shape[0]

    def copies(sources):
        targets = [cat_ref.at[:, pl.ds(k * half, half)] for k in range(4)] + list(bufs)
        return [
            pltpu.make_async_copy(s.at[0], t, sem.at[k]) for k, (s, t) in enumerate(zip(sources, targets))
        ]

    @pl.when(home_ref[0] == 1)
    def _():
        for c in copies(own):
            c.start()

    @pl.when(home_ref[0] == 0)
    def _():
        for c in copies(far):
            c.start()

    for k, c in enumerate(copies(own)):
        c.wait()
        if k < 4:
            cat_t_ref[k * half : (k + 1) * half, :] = cat_ref[:, k * half : (k + 1) * half].T
        else:
            down_t_ref[:, (k - 4) * half : (k - 3) * half] = bufs[k - 4][...].T


def acts_kernel(x_ref, w_ref, out_ref):
    act = dot(x_ref[...], w_ref[...], NN)
    hidden = act.shape[1] // 2
    gate, up = act[:, :hidden], act[:, hidden:]
    sig = jax.nn.sigmoid(gate)
    out_ref[:, :hidden] = up * sig * (1.0 + gate * (1.0 - sig))
    out_ref[:, hidden:] = gate * sig


def back_kernel(g_ref, act_ref, down_ref, cat_ref, out_ref, down_buf, cat_buf, sem):
    first = pl.program_id(0) == 0
    down_copy = pltpu.make_async_copy(down_ref, down_buf, sem.at[0])
    cat_copy = pltpu.make_async_copy(cat_ref, cat_buf, sem.at[1])

    @pl.when(first)
    def _():
        down_copy.start()
        cat_copy.start()
        down_copy.wait()

    grad = dot(g_ref[...], down_buf[...], NN)
    hidden = grad.shape[1]
    both = jnp.concatenate(
        [(grad * act_ref[:, :hidden]).astype(BF16), (grad * act_ref[:, hidden:]).astype(BF16)], axis=1
    )

    @pl.when(first)
    def _():
        cat_copy.wait()

    out_ref[...] = dot(both, cat_buf[...], NN).astype(BF16)


def combine_kernel(hi_ref, lo_ref, rows_ref, grad_ref, out_ref, first_ref, second_ref):
    rows = rows_ref[...]
    total = dot(hi_ref[...], rows, NN) + dot(lo_ref[...], rows, NN)
    resid = (grad_ref[...].astype(F32) + total).astype(BF16)
    out_ref[...] = resid
    half = first_ref.shape[0]
    first_ref[...] = resid[:half]
    second_ref[...] = resid[half:]


def project_kernel(y_ref, *refs):
    resids, projs, outs, toks_ref, buf_ref, sem = refs[:7], refs[7:12], refs[12:16], refs[16], refs[17], refs[18]
    copies = []
    at = 0
    for k, source in enumerate(projs):
        n = source.shape[0]
        copies.append(pltpu.make_async_copy(source, buf_ref.at[pl.ds(at, n)], sem.at[k]))
        at += n
    for c in copies:
        c.start()
    toks = resids[0].shape[0]
    half = toks // 2
    for source, (dy, at) in zip(resids, ((0, 0), (3, 0), (3, half), (1, 0), (1, half), (2, 0), (2, half))):
        place = ((y_ref[0] + dy) & 3) * toks + at
        toks_ref[pl.ds(pl.multiple_of(place, half), source.shape[0]), :] = source[...]
    line = toks_ref[...]
    rows = outs[0].shape[1]
    for k, waits in enumerate(((0,), (1,), (2, 3), (4,))):
        for w in waits:
            copies[w].wait()
        g = dot(buf_ref[k * rows : (k + 1) * rows, :], line, NT).astype(BF16)
        for q in range(4):
            outs[k][q] = g[:, q * toks : (q + 1) * toks]


def block_grads(g_ref, k):
    return jnp.concatenate([g_ref[2 * k], g_ref[2 * k + 1]], axis=1)


def head_rows(rows, heads, dim):
    n = rows.shape[1]
    return jnp.concatenate([jnp.broadcast_to(rows[h : h + 1, :], (dim, n)) for h in range(heads)], axis=0)


def prepare_kernel(
    d_ref, b_ref, c_ref, x_ref, wh_ref, wl_ref, ts_ref, te_ref, tt_ref, xh_ref, xl_ref, eh_ref, el_ref, th_ref, tl_ref,
    bs_ref, tot_ref,
):
    heads, n = d_ref.shape
    dim = x_ref.shape[0] // heads
    row = lax.broadcasted_iota(jnp.int32, (n, n), 0)
    col = lax.broadcasted_iota(jnp.int32, (n, n), 1)
    tri = jnp.where(col <= row, 1.0, 0.0)
    d = jnp.concatenate([d_ref[...], jnp.zeros((8 - heads, n), F32)], axis=0)
    across = dot_high(d, tri, NT)
    down = dot_high(tri, d, NT)
    scores = dot_high(b_ref[...], c_ref[...], NT)
    later = col >= row
    for h in range(heads):
        gap = across[h : h + 1, :] - down[:, h : h + 1]
        w = jnp.where(later, jnp.exp(jnp.where(later, gap, 0.0)), 0.0) * scores
        wh_ref[0, h], wl_ref[0, h] = split(w)

    @pl.when(pl.program_id(0) == 0)
    def _():
        tot_ref[...] = jnp.zeros_like(tot_ref)

    last = across[:, n - 1 : n]
    te = jnp.exp(last - across)
    tt = jnp.exp(last - across + tot_ref[:, 0:1])
    ts_ref[...] = jnp.exp(across)
    te_ref[...] = te
    tt_ref[...] = tt
    x = x_ref[...]
    xh_ref[...], xl_ref[...] = split(x.T)
    eh_ref[...], el_ref[...] = split((x * head_rows(te, heads, dim)).T)
    th_ref[...], tl_ref[...] = split((x * head_rows(tt, heads, dim)).T)
    block_sum = jnp.broadcast_to(last, tot_ref.shape)
    bs_ref[0] = block_sum
    tot_ref[...] = tot_ref[...] + block_sum


def state_kernel(heads, z_ref, g0_ref, g1_ref, g2_ref, g3_ref, c_ref, ts_ref, bs_ref, tot_ref, fut_ref, pay_ref, g_ref):
    blocks, rows, lanes = fut_ref.shape
    dim = rows // heads
    n = c_ref.shape[0] // blocks
    for dz, source in enumerate((g0_ref, g1_ref, g2_ref, g3_ref)):
        g_ref[pl.ds(((z_ref[0] + dz) & 3) * 4, 4)] = source[...]
    states = []
    for k in range(blocks):
        at = slice(k * n, (k + 1) * n)
        g = block_grads(g_ref, k).astype(F32)
        ghi, glo = split(g * head_rows(ts_ref[:, at], heads, dim))
        chi, clo = split(c_ref[at, :])
        states.append(dot(ghi, chi, NN) + dot(ghi, clo, NN) + dot(glo, chi, NN))
    carry = jnp.zeros((rows, lanes), F32)
    for k in reversed(range(blocks)):
        fut_ref[k] = carry
        carry = head_rows(jnp.exp(bs_ref[k]), heads, dim) * carry + states[k]
    first = tot_ref[...]
    hi, _ = split(first)
    mid, low = split(first - hi.astype(F32))
    sent = jnp.concatenate([carry.astype(BF16), hi, mid, low, low], axis=0)
    for j in range(pay_ref.shape[0]):
        pay_ref[j] = sent


def intra_kernel(
    heads, skip_ref, wh_ref, wl_ref, g_ref, xh_ref, xl_ref, eh_ref, el_ref, te_ref, b_ref, c_ref, fut_ref, gx_ref, pb_ref
):
    n = wh_ref.shape[2]
    rows = gx_ref.shape[0]
    dim = rows // heads
    for k in range(wh_ref.shape[0]):
        at = slice(k * n, (k + 1) * n)
        fhi, flo = split(fut_ref[k])
        bhi, blo = split(b_ref[at, :])
        cross = dot(fhi, bhi, NT) + dot(flo, bhi, NT) + dot(fhi, blo, NT)
        cross = cross * head_rows(te_ref[:, at], heads, dim)
        acc = None
        grads = block_grads(g_ref, k)
        for h in range(heads):
            w = wh_ref[k, h]
            cols = slice(h * dim, (h + 1) * dim)
            g = grads[cols]
            gx_ref[cols, at] = dot(g, w, NT) + cross[cols] + skip_ref[h] * g.astype(F32)
            inner = dot(xh_ref[at, cols], g, NN) + dot(xl_ref[at, cols], g, NN)
            term = (w.astype(F32) + wl_ref[k, h].astype(F32)) * inner
            acc = term if acc is None else acc + term
        ahi, alo = split(acc)
        chi, clo = split(c_ref[at, :])
        eh = eh_ref[at, :]
        pb_ref[at, :] = (
            dot(ahi, chi, NN)
            + dot(alo, chi, NN)
            + dot(ahi, clo, NN)
            + dot(eh, fhi, NN)
            + dot(eh, flo, NN)
            + dot(el_ref[at, :], fhi, NN)
        )


def finish_b_kernel(heads, seq_ref, pay_ref, th_ref, tl_ref, pb_ref, out_ref, hi_ref, lo_ref):
    rows, lanes = hi_ref.shape
    dim = rows // heads

    @pl.when(pl.program_id(0) == 0)
    def _():
        place = seq_ref[0]
        acc = jnp.zeros((rows, lanes), F32)
        log = jnp.zeros((8, lanes), F32)
        for j in range(pay_ref.shape[0]):
            ahead = j > place
            factor = jnp.where(ahead, jnp.exp(log), 0.0)
            acc = acc + head_rows(factor, heads, dim) * pay_ref[j, 0:rows, :].astype(F32)
            tots = pay_ref[j, rows : rows + 32, :].astype(F32)
            log = log + jnp.where(ahead, tots[0:8] + tots[8:16] + tots[16:24], 0.0)
        hi_ref[...], lo_ref[...] = split(acc)

    hi = hi_ref[...]
    th = th_ref[...]
    total = pb_ref[...] + dot(th, hi, NN) + dot(th, lo_ref[...], NN) + dot(tl_ref[...], hi, NN)
    out_ref[...] = total.astype(out_ref.dtype)


def finish_x_kernel(heads, hi_ref, lo_ref, tt_ref, b_ref, gx_ref, out_ref):
    bhi, blo = split(b_ref[...])
    hi = hi_ref[...]
    tt = head_rows(tt_ref[...], heads, out_ref.shape[0] // heads)
    out_ref[...] = gx_ref[...] + tt * (dot(hi, bhi, NT) + dot(lo_ref[...], bhi, NT) + dot(hi, blo, NT))


def whole(shape):
    zeros = (0,) * len(shape)
    return pl.BlockSpec(shape, lambda *_: zeros)


def shards(
    moe_input,
    out_grad,
    route_ids,
    route_gates,
    gate_halves,
    up_halves,
    down_halves,
    out_proj,
    ssd_x,
    b_proj,
    c_proj,
    log_decay,
    skip_gain,
):
    sds = jax.ShapeDtypeStruct
    toks, width = moe_input.shape
    seq_axes = ("x", "core")
    n_seq, n_head = lax.axis_size(seq_axes), lax.axis_size("head")
    devices = n_seq * n_head
    slots = devices * SLOTS
    both = ("x", "core", "head")
    smem_spec = pl.BlockSpec(memory_space=pltpu.SMEM)
    any_spec = pl.BlockSpec(memory_space=pl.ANY)
    heads = skip_gain.shape[0]
    inner = out_proj.shape[0]
    seq_rows, state = b_proj.shape
    blocks = seq_rows // BLOCK
    seq, head = lax.axis_index(seq_axes), lax.axis_index("head")
    core = lax.axis_index("core")

    home = core == (head & 1)
    over_y, over_core = [], []
    for s in range(n_seq):
        for h in range(n_head):
            if (s & 1) != (h & 1):
                over_y.append((s * n_head + h, s * n_head + (h ^ 1)))
            else:
                over_core.append((s * n_head + h, (s ^ 1) * n_head + h))
    halves = (gate_halves, up_halves, down_halves)
    y_halves, far_own = [], []
    for a in halves:
        y_halves.append(lax.ppermute(a, both, over_y))
    for a in halves:
        far_own.append(lax.ppermute(a, both, over_core))
    far_y = [lax.ppermute(a, both, over_core) for a in y_halves]
    own = [a for o, y in zip(halves, y_halves) for a in (o, y)]
    far = [a for o, y in zip(far_own, far_y) for a in (o, y)]
    _, width, half = gate_halves.shape
    hidden = 2 * half
    expert_cat, expert_cat_t, expert_down_t = pl.pallas_call(
        weights_kernel,
        in_specs=[smem_spec] + [any_spec] * 12,
        out_shape=(sds((width, 2 * hidden), BF16), sds((2 * hidden, width), BF16), sds((width, hidden), BF16)),
        scratch_shapes=[pltpu.VMEM((half, width), BF16)] * 2 + [pltpu.SemaphoreType.DMA((6,))],
        compiler_params=params(),
        cost_estimate=cost(1e9, 12 << 20),
        name="expert_weights",
    )(home.astype(jnp.int32).reshape(1), *own, *far)

    ids_t, gates_t = route_ids.T, route_gates.T
    sel, send_input = pl.pallas_call(
        select_kernel,
        out_shape=(sds((slots, toks), BF16), sds((slots, width), BF16)),
        compiler_params=params(),
        cost_estimate=cost(2 * slots * toks * width, 4 << 20),
        name="select_rows",
    )(ids_t, moe_input)
    send_grad, mix_hi, mix_lo = pl.pallas_call(
        second_kernel,
        out_shape=(sds((slots, width), BF16), sds((toks, slots), BF16), sds((toks, slots), BF16)),
        compiler_params=params(),
        cost_estimate=cost(2 * slots * toks * width, 4 << 20),
        name="select_grads",
    )(ids_t, gates_t, sel, out_grad)

    def exchange(rows):
        shaped = rows.reshape(devices, SLOTS, width)
        return lax.all_to_all(shaped, both, split_axis=0, concat_axis=0, tiled=True).reshape(slots, width)

    recv_input = exchange(send_input)
    recv_grad = exchange(send_grad)

    def shift(rows, dz, dy):
        pairs = [(z * 4 + y, (z + dz) % 4 * 4 + (y + dy) % 4) for z in range(4) for y in range(4)]
        return lax.ppermute(rows, "head", pairs)

    proj_up, proj_dn = shift(out_proj, 1, 0), shift(out_proj, -1, 0)
    proj_far_up = shift(proj_up[: inner // 2], 1, 0)
    proj_far_dn = shift(proj_dn[inner // 2 :], -1, 0)

    flip = lambda i: blocks - 1 - i
    row_in = pl.BlockSpec((inner, BLOCK), lambda i: (0, flip(i)))
    tok_in = pl.BlockSpec((BLOCK, inner), lambda i: (flip(i), 0))
    tok_st = pl.BlockSpec((BLOCK, state), lambda i: (flip(i), 0))
    row_8 = pl.BlockSpec((8, BLOCK), lambda i: (0, flip(i)))
    blk_st = pl.BlockSpec((1, inner, state), lambda i: (flip(i), 0, 0))
    blk_8 = pl.BlockSpec((1, 8, state), lambda i: (flip(i), 0, 0))
    blk_w = pl.BlockSpec((1, heads, BLOCK, BLOCK), lambda i: (flip(i), 0, 0, 0))
    x_shape = sds((seq_rows, inner), BF16)
    w_shape = sds((blocks, heads, BLOCK, BLOCK), BF16)
    r_shape = sds((8, seq_rows), F32)
    w_hi, w_lo, to_start, to_end, to_last, x_hi, x_lo, e_hi, e_lo, t_hi, t_lo, block_sum, total = pl.pallas_call(
        prepare_kernel,
        grid=(blocks,),
        in_specs=[pl.BlockSpec((heads, BLOCK), lambda i: (0, flip(i))), tok_st, tok_st, row_in],
        out_specs=(blk_w,) * 2 + (row_8,) * 3 + (tok_in,) * 6 + (blk_8, whole((8, state))),
        out_shape=(w_shape,) * 2
        + (r_shape,) * 3
        + (x_shape,) * 6
        + (sds((blocks, 8, state), F32), sds((8, state), F32)),
        compiler_params=params(),
        cost_estimate=cost(4e9, 20 << 20),
        name="scan_prepare",
    )(log_decay, b_proj, c_proj, ssd_x.T)

    tile = 256
    row_spec = pl.BlockSpec((tile, width), lambda i: (i, 0))
    act_spec = pl.BlockSpec((tile, 2 * hidden), lambda i: (i, 0))
    factors = pl.pallas_call(
        acts_kernel,
        grid=(slots // tile,),
        in_specs=[row_spec, whole((width, 2 * hidden))],
        out_specs=act_spec,
        out_shape=sds((slots, 2 * hidden), F32),
        compiler_params=params(),
        cost_estimate=cost(4 * slots * width * hidden, 10 << 20),
        name="expert_acts",
    )(recv_input, expert_cat)
    expert_rows = pl.pallas_call(
        back_kernel,
        grid=(slots // tile,),
        in_specs=[row_spec, act_spec, any_spec, any_spec],
        out_specs=row_spec,
        out_shape=sds((slots, width), BF16),
        scratch_shapes=[
            pltpu.VMEM((width, hidden), BF16),
            pltpu.VMEM((2 * hidden, width), BF16),
            pltpu.SemaphoreType.DMA((2,)),
        ],
        compiler_params=params(),
        cost_estimate=cost(6 * slots * width * hidden, 14 << 20),
        name="expert_back",
    )(recv_grad, factors, expert_down_t, expert_cat_t)
    returned = exchange(expert_rows)

    resid_grad, first, second = pl.pallas_call(
        combine_kernel,
        out_shape=(sds((toks, width), BF16),) + (sds((toks // 2, width), BF16),) * 2,
        compiler_params=params(),
        cost_estimate=cost(4 * slots * toks * width, 4 << 20),
        name="combine_rows",
    )(mix_hi, mix_lo, returned, out_grad)
    up_first = shift(first, 0, 1)
    dn_second = shift(second, 0, -1)
    up_second = shift(second, 0, 1)
    dn_first = shift(first, 0, -1)
    far_first = shift(up_first, 0, 1)
    far_second = shift(dn_second, 0, -1)
    part_spec = whole((n_head // 4, inner, toks))
    part_shape = sds((n_head // 4, inner, toks), BF16)
    halves_spec = whole((toks // 2, width))
    to_0, to_3, to_2, to_1 = pl.pallas_call(
        project_kernel,
        grid=(1,),
        in_specs=[smem_spec, whole((toks, width))] + [halves_spec] * 6 + [any_spec] * 5,
        out_specs=(part_spec,) * 4,
        out_shape=(part_shape,) * 4,
        scratch_shapes=[
            pltpu.VMEM((4 * toks, width), BF16),
            pltpu.VMEM((4 * inner, width), BF16),
            pltpu.SemaphoreType.DMA((5,)),
        ],
        compiler_params=params(60 << 20),
        cost_estimate=cost(32 * inner * toks * width, 7 << 20),
        name="project_rows",
    )(
        (head & 3).reshape(1),
        resid_grad,
        up_first,
        up_second,
        dn_first,
        dn_second,
        far_first,
        far_second,
        out_proj,
        proj_up,
        proj_far_up,
        proj_far_dn,
        proj_dn,
    )
    from_2 = shift(to_2, 2, 0)
    from_3 = shift(to_1, 1, 0)
    from_1 = shift(to_3, -1, 0)

    pay_rows = inner + 32
    future, payload, grads = pl.pallas_call(
        functools.partial(state_kernel, heads),
        out_shape=(
            sds((blocks, inner, state), F32),
            sds((n_seq, pay_rows, state), BF16),
            sds((n_head, inner, toks), BF16),
        ),
        grid=(1,),
        in_specs=[smem_spec]
        + [part_spec] * 4
        + [
            whole((seq_rows, state)),
            whole((8, seq_rows)),
            whole((blocks, 8, state)),
            whole((8, state)),
        ],
        out_specs=(
            whole((blocks, inner, state)),
            whole((n_seq, pay_rows, state)),
            whole((n_head, inner, toks)),
        ),
        compiler_params=params(),
        cost_estimate=cost(1e9, 4 << 20),
        name="scan_state",
    )((head >> 2).reshape(1), to_0, from_1, from_2, from_3, c_proj, to_start, block_sum, total)
    pays = lax.all_to_all(payload, seq_axes, split_axis=0, concat_axis=0, tiled=True)
    pair = 2
    spec = lambda *shape: pl.BlockSpec(shape, lambda i: (i,) + (0,) * (len(shape) - 1))
    cols = lambda *shape: pl.BlockSpec(shape, lambda i: (0, i))
    tok_in2, tok_st2 = spec(pair * BLOCK, inner), spec(pair * BLOCK, state)
    row_in2, row_82 = cols(inner, pair * BLOCK), cols(8, pair * BLOCK)
    w_spec = spec(pair, heads, BLOCK, BLOCK)
    part_x, part_b = pl.pallas_call(
        functools.partial(intra_kernel, heads),
        grid=(blocks // pair,),
        in_specs=[smem_spec, w_spec, w_spec, spec(pair * BLOCK // toks, inner, toks)]
        + [tok_in2] * 4
        + [row_82, tok_st2, tok_st2, spec(pair, inner, state)],
        out_specs=(row_in2, tok_st2),
        out_shape=(sds((inner, seq_rows), F32), sds((seq_rows, state), F32)),
        compiler_params=params(),
        cost_estimate=cost(4e9, 16 << 20),
        name="scan_intra",
    )(skip_gain, w_hi, w_lo, grads, x_hi, x_lo, e_hi, e_lo, to_end, b_proj, c_proj, future)
    partial_b, in_hi, in_lo = pl.pallas_call(
        functools.partial(finish_b_kernel, heads),
        grid=(blocks // pair,),
        in_specs=[smem_spec, whole((n_seq, pay_rows, state)), tok_in2, tok_in2, tok_st2],
        out_specs=(tok_st2, whole((inner, state)), whole((inner, state))),
        out_shape=(sds((seq_rows, state), BF16), sds((inner, state), BF16), sds((inner, state), BF16)),
        compiler_params=params(),
        cost_estimate=cost(4e8, 6 << 20),
        name="scan_finish_b",
    )(seq.reshape(1), pays, t_hi, t_lo, part_b)
    shares = lax.all_to_all(
        partial_b.reshape(n_head, seq_rows // n_head, state), "head", split_axis=0, concat_axis=0, tiled=True
    )
    grad_x = pl.pallas_call(
        functools.partial(finish_x_kernel, heads),
        grid=(blocks // pair,),
        in_specs=[whole((inner, state)), whole((inner, state)), row_82, tok_st2, row_in2],
        out_specs=row_in2,
        out_shape=sds((inner, seq_rows), F32),
        compiler_params=params(),
        cost_estimate=cost(4e8, 6 << 20),
        name="scan_finish_x",
    )(in_hi, in_lo, to_last, b_proj, part_x)
    b_grad = jnp.sum(shares.astype(F32), axis=0)
    return (resid_grad, grad_x.T, b_grad)


def solution(mesh):
    n_seq, n_head = mesh.shape["seq"], mesh.shape["head"]
    fine = jax.sharding.Mesh(mesh.devices.reshape(n_seq // 2, 2, n_head), ("x", "core", "head"))

    seq, every = ("x", "core"), ("x", "core", "head")
    return jax.shard_map(
        shards,
        mesh=fine,
        in_specs=(
            P(every, None),
            P(every, None),
            P(every, None),
            P(every, None),
            P(every, None, None),
            P(every, None, None),
            P(every, None, None),
            P("head", None),
            P(seq, "head"),
            P(seq, None),
            P(seq, None),
            P("head", seq),
            P("head"),
        ),
        out_specs=(P(every, None), P(seq, "head"), P(every, None)),
        check_vma=False,
    )
```

```python
import functools

import jax
import jax.numpy as jnp
from jax import lax
from jax.experimental import pallas as pl
from jax.experimental.pallas import tpu as pltpu
from jax.sharding import PartitionSpec as P


BLOCK = 256
SLOTS = 8
F32 = jnp.float32
BF16 = jnp.bfloat16
HIGHEST = lax.Precision.HIGHEST
NT = (((1,), (1,)), ((), ()))
NN = (((1,), (0,)), ((), ()))


def params(limit=67043328):
    return pltpu.CompilerParams(vmem_limit_bytes=limit)


def cost(flops, bytes_accessed):
    return pl.CostEstimate(flops=int(flops), bytes_accessed=int(bytes_accessed), transcendentals=0)


def split(a):
    hi = a.astype(BF16)
    return hi, (a - hi.astype(F32)).astype(BF16)


def dot(a, b, dims):
    return lax.dot_general(a, b, dims, preferred_element_type=F32)


def dot_high(a, b, dims):
    return lax.dot_general(a, b, dims, precision=HIGHEST, preferred_element_type=F32)


def slot_experts(rows, toks):
    row = lax.broadcasted_iota(jnp.int32, (rows, toks), 0)
    dev, slot = row >> 3, row & 7
    x, core, z, y = dev >> 5, (dev >> 4) & 1, (dev >> 2) & 3, dev & 3
    expert = (2 * x + (y & 1)) * 8 + 2 * z + (y >> 1)
    return expert, 2 * slot + core


def select_kernel(ids_ref, rows_ref, sel_ref, out_ref):
    slots, toks = sel_ref.shape
    expert, rank = slot_experts(slots, toks)
    named = ids_ref[0:1, :] == expert
    for k in range(1, ids_ref.shape[0]):
        named = jnp.logical_or(named, ids_ref[k : k + 1, :] == expert)
    named = jnp.where(named, 1.0, 0.0)
    earlier = jnp.where(
        lax.broadcasted_iota(jnp.int32, (toks, toks), 0)
        < lax.broadcasted_iota(jnp.int32, (toks, toks), 1),
        1.0,
        0.0,
    )
    before = dot(named.astype(BF16), earlier.astype(BF16), NN)
    sel = jnp.where(before == rank.astype(F32), named, 0.0).astype(BF16)
    sel_ref[...] = sel
    out_ref[...] = dot(sel, rows_ref[...], NN).astype(BF16)


def second_kernel(ids_ref, gates_ref, sel_ref, rows_ref, out_ref, hi_ref, lo_ref):
    slots, toks = sel_ref.shape
    out_ref[...] = dot(sel_ref[...], rows_ref[...], NN).astype(BF16)
    expert, _ = slot_experts(slots, toks)
    gate = jnp.zeros((slots, toks), F32)
    for k in range(ids_ref.shape[0]):
        gate = jnp.where(ids_ref[k : k + 1, :] == expert, gates_ref[k : k + 1, :], gate)
    mix = (gate * sel_ref[...].astype(F32)).T
    hi, lo = split(mix)
    hi_ref[...] = hi
    lo_ref[...] = lo


def copy_half(home_ref, own, far, targets, sem):
    def copies(sources):
        return [pltpu.make_async_copy(s.at[0], t, sem.at[k]) for k, (s, t) in enumerate(zip(sources, targets))]

    @pl.when(home_ref[0] == 1)
    def _():
        for c in copies(own):
            c.start()

    @pl.when(home_ref[0] == 0)
    def _():
        for c in copies(far):
            c.start()

    return copies(own)


def weights_kernel(home_ref, *refs):
    own, far, cat_ref, cat_t_ref, sem = refs[:4], refs[4:8], refs[8], refs[9], refs[10]
    half = cat_ref.shape[1] // 4
    targets = [cat_ref.at[:, pl.ds(k * half, half)] for k in range(4)]
    for k, c in enumerate(copy_half(home_ref, own, far, targets, sem)):
        c.wait()
        cat_t_ref[k * half : (k + 1) * half, :] = cat_ref[:, k * half : (k + 1) * half].T


def down_kernel(home_ref, *refs):
    own, far, down_t_ref, bufs, sem = refs[:2], refs[2:4], refs[4], refs[5:7], refs[7]
    half = bufs[0].shape[0]
    for k, c in enumerate(copy_half(home_ref, own, far, bufs, sem)):
        c.wait()
        down_t_ref[:, k * half : (k + 1) * half] = bufs[k][...].T


def acts_kernel(x_ref, w_ref, out_ref):
    act = dot(x_ref[...], w_ref[...], NN)
    hidden = act.shape[1] // 2
    gate, up = act[:, :hidden], act[:, hidden:]
    sig = jax.nn.sigmoid(gate)
    out_ref[:, :hidden] = up * sig * (1.0 + gate * (1.0 - sig))
    out_ref[:, hidden:] = gate * sig


def back_kernel(g_ref, act_ref, down_ref, cat_ref, out_ref, down_buf, cat_buf, sem):
    first = pl.program_id(0) == 0
    down_copy = pltpu.make_async_copy(down_ref, down_buf, sem.at[0])
    cat_copy = pltpu.make_async_copy(cat_ref, cat_buf, sem.at[1])

    @pl.when(first)
    def _():
        down_copy.start()
        cat_copy.start()
        down_copy.wait()

    grad = dot(g_ref[...], down_buf[...], NN)
    hidden = grad.shape[1]
    both = jnp.concatenate(
        [(grad * act_ref[:, :hidden]).astype(BF16), (grad * act_ref[:, hidden:]).astype(BF16)], axis=1
    )

    @pl.when(first)
    def _():
        cat_copy.wait()

    out_ref[...] = dot(both, cat_buf[...], NN).astype(BF16)


def combine_kernel(hi_ref, lo_ref, rows_ref, grad_ref, out_ref, first_ref, second_ref):
    rows = rows_ref[...]
    total = dot(hi_ref[...], rows, NN) + dot(lo_ref[...], rows, NN)
    resid = (grad_ref[...].astype(F32) + total).astype(BF16)
    out_ref[...] = resid
    half = first_ref.shape[0]
    first_ref[...] = resid[:half]
    second_ref[...] = resid[half:]


def project_kernel(y_ref, *refs):
    resids, projs, outs, toks_ref, buf_ref, sem = refs[:7], refs[7:12], refs[12:16], refs[16], refs[17], refs[18]
    copies = []
    at = 0
    for k, source in enumerate(projs):
        n = source.shape[0]
        copies.append(pltpu.make_async_copy(source, buf_ref.at[pl.ds(at, n)], sem.at[k]))
        at += n
    for c in copies:
        c.start()
    toks = resids[0].shape[0]
    half = toks // 2
    for source, (dy, at) in zip(resids, ((0, 0), (3, 0), (3, half), (1, 0), (1, half), (2, 0), (2, half))):
        place = ((y_ref[0] + dy) & 3) * toks + at
        toks_ref[pl.ds(pl.multiple_of(place, half), source.shape[0]), :] = source[...]
    line = toks_ref[...]
    rows = outs[0].shape[1]
    for k, waits in enumerate(((0,), (1,), (2, 3), (4,))):
        for w in waits:
            copies[w].wait()
        g = dot(buf_ref[k * rows : (k + 1) * rows, :], line, NT).astype(BF16)
        for q in range(4):
            outs[k][q] = g[:, q * toks : (q + 1) * toks]


def block_grads(g_ref, k):
    return jnp.concatenate([g_ref[2 * k], g_ref[2 * k + 1]], axis=1)


def head_rows(rows, heads, dim):
    n = rows.shape[1]
    return jnp.concatenate([jnp.broadcast_to(rows[h : h + 1, :], (dim, n)) for h in range(heads)], axis=0)


def prepare_kernel(
    d_ref, b_ref, c_ref, x_ref, wh_ref, wl_ref, ts_ref, te_ref, tt_ref, xh_ref, xl_ref, eh_ref, el_ref, th_ref, tl_ref,
    bs_ref, tot_ref,
):
    heads, n = d_ref.shape
    dim = x_ref.shape[0] // heads
    row = lax.broadcasted_iota(jnp.int32, (n, n), 0)
    col = lax.broadcasted_iota(jnp.int32, (n, n), 1)
    tri = jnp.where(col <= row, 1.0, 0.0)
    d = jnp.concatenate([d_ref[...], jnp.zeros((8 - heads, n), F32)], axis=0)
    across = dot_high(d, tri, NT)
    down = dot_high(tri, d, NT)
    scores = dot_high(b_ref[...], c_ref[...], NT)
    later = col >= row
    for h in range(heads):
        gap = across[h : h + 1, :] - down[:, h : h + 1]
        w = jnp.where(later, jnp.exp(jnp.where(later, gap, 0.0)), 0.0) * scores
        wh_ref[0, h], wl_ref[0, h] = split(w)

    @pl.when(pl.program_id(0) == 0)
    def _():
        tot_ref[...] = jnp.zeros_like(tot_ref)

    last = across[:, n - 1 : n]
    te = jnp.exp(last - across)
    tt = jnp.exp(last - across + tot_ref[:, 0:1])
    ts_ref[...] = jnp.exp(across)
    te_ref[...] = te
    tt_ref[...] = tt
    x = x_ref[...]
    xh_ref[...], xl_ref[...] = split(x.T)
    eh_ref[...], el_ref[...] = split((x * head_rows(te, heads, dim)).T)
    th_ref[...], tl_ref[...] = split((x * head_rows(tt, heads, dim)).T)
    block_sum = jnp.broadcast_to(last, tot_ref.shape)
    bs_ref[0] = block_sum
    tot_ref[...] = tot_ref[...] + block_sum


def state_kernel(heads, z_ref, g0_ref, g1_ref, g2_ref, g3_ref, c_ref, ts_ref, bs_ref, tot_ref, fut_ref, pay_ref, g_ref):
    blocks, rows, lanes = fut_ref.shape
    dim = rows // heads
    n = c_ref.shape[0] // blocks
    for dz, source in enumerate((g0_ref, g1_ref, g2_ref, g3_ref)):
        g_ref[pl.ds(((z_ref[0] + dz) & 3) * 4, 4)] = source[...]
    states = []
    for k in range(blocks):
        at = slice(k * n, (k + 1) * n)
        g = block_grads(g_ref, k).astype(F32)
        ghi, glo = split(g * head_rows(ts_ref[:, at], heads, dim))
        chi, clo = split(c_ref[at, :])
        states.append(dot(ghi, chi, NN) + dot(ghi, clo, NN) + dot(glo, chi, NN))
    carry = jnp.zeros((rows, lanes), F32)
    for k in reversed(range(blocks)):
        fut_ref[k] = carry
        carry = head_rows(jnp.exp(bs_ref[k]), heads, dim) * carry + states[k]
    first = tot_ref[...]
    hi, _ = split(first)
    mid, low = split(first - hi.astype(F32))
    sent = jnp.concatenate([carry.astype(BF16), hi, mid, low, low], axis=0)
    for j in range(pay_ref.shape[0]):
        pay_ref[j] = sent


def intra_kernel(
    heads, skip_ref, wh_ref, wl_ref, g_ref, xh_ref, xl_ref, eh_ref, el_ref, te_ref, b_ref, c_ref, fut_ref, gx_ref, pb_ref
):
    n = wh_ref.shape[2]
    rows = gx_ref.shape[0]
    dim = rows // heads
    for k in range(wh_ref.shape[0]):
        at = slice(k * n, (k + 1) * n)
        fhi, flo = split(fut_ref[k])
        bhi, blo = split(b_ref[at, :])
        cross = dot(fhi, bhi, NT) + dot(flo, bhi, NT) + dot(fhi, blo, NT)
        cross = cross * head_rows(te_ref[:, at], heads, dim)
        acc = None
        grads = block_grads(g_ref, k)
        for h in range(heads):
            w = wh_ref[k, h]
            cols = slice(h * dim, (h + 1) * dim)
            g = grads[cols]
            gx_ref[cols, at] = dot(g, w, NT) + cross[cols] + skip_ref[h] * g.astype(F32)
            inner = dot(xh_ref[at, cols], g, NN) + dot(xl_ref[at, cols], g, NN)
            term = (w.astype(F32) + wl_ref[k, h].astype(F32)) * inner
            acc = term if acc is None else acc + term
        ahi, alo = split(acc)
        chi, clo = split(c_ref[at, :])
        eh = eh_ref[at, :]
        pb_ref[at, :] = (
            dot(ahi, chi, NN)
            + dot(alo, chi, NN)
            + dot(ahi, clo, NN)
            + dot(eh, fhi, NN)
            + dot(eh, flo, NN)
            + dot(el_ref[at, :], fhi, NN)
        )


def finish_b_kernel(heads, seq_ref, pay_ref, th_ref, tl_ref, pb_ref, out_ref, hi_ref, lo_ref):
    rows, lanes = hi_ref.shape
    dim = rows // heads

    @pl.when(pl.program_id(0) == 0)
    def _():
        place = seq_ref[0]
        acc = jnp.zeros((rows, lanes), F32)
        log = jnp.zeros((8, lanes), F32)
        for j in range(pay_ref.shape[0]):
            ahead = j > place
            factor = jnp.where(ahead, jnp.exp(log), 0.0)
            acc = acc + head_rows(factor, heads, dim) * pay_ref[j, 0:rows, :].astype(F32)
            tots = pay_ref[j, rows : rows + 32, :].astype(F32)
            log = log + jnp.where(ahead, tots[0:8] + tots[8:16] + tots[16:24], 0.0)
        hi_ref[...], lo_ref[...] = split(acc)

    hi = hi_ref[...]
    th = th_ref[...]
    total = pb_ref[...] + dot(th, hi, NN) + dot(th, lo_ref[...], NN) + dot(tl_ref[...], hi, NN)
    out_ref[...] = total.astype(out_ref.dtype)


def finish_x_kernel(heads, hi_ref, lo_ref, tt_ref, b_ref, gx_ref, out_ref):
    bhi, blo = split(b_ref[...])
    hi = hi_ref[...]
    tt = head_rows(tt_ref[...], heads, out_ref.shape[0] // heads)
    out_ref[...] = gx_ref[...] + tt * (dot(hi, bhi, NT) + dot(lo_ref[...], bhi, NT) + dot(hi, blo, NT))


def whole(shape):
    zeros = (0,) * len(shape)
    return pl.BlockSpec(shape, lambda *_: zeros)


def shards(
    moe_input,
    out_grad,
    route_ids,
    route_gates,
    gate_halves,
    up_halves,
    down_halves,
    out_proj,
    ssd_x,
    b_proj,
    c_proj,
    log_decay,
    skip_gain,
):
    sds = jax.ShapeDtypeStruct
    toks, width = moe_input.shape
    seq_axes = ("x", "core")
    n_seq, n_head = lax.axis_size(seq_axes), lax.axis_size("head")
    devices = n_seq * n_head
    slots = devices * SLOTS
    both = ("x", "core", "head")
    smem_spec = pl.BlockSpec(memory_space=pltpu.SMEM)
    any_spec = pl.BlockSpec(memory_space=pl.ANY)
    heads = skip_gain.shape[0]
    inner = out_proj.shape[0]
    seq_rows, state = b_proj.shape
    blocks = seq_rows // BLOCK
    seq, head = lax.axis_index(seq_axes), lax.axis_index("head")
    core = lax.axis_index("core")

    home = core == (head & 1)
    over_y, over_core = [], []
    for s in range(n_seq):
        for h in range(n_head):
            if (s & 1) != (h & 1):
                over_y.append((s * n_head + h, s * n_head + (h ^ 1)))
            else:
                over_core.append((s * n_head + h, (s ^ 1) * n_head + h))
    halves = (gate_halves, up_halves, down_halves)
    y_halves, far_own = [], []
    for a in halves:
        y_halves.append(lax.ppermute(a, both, over_y))
    for a in halves:
        far_own.append(lax.ppermute(a, both, over_core))
    far_y = []
    for a in y_halves:
        far_y.append(lax.ppermute(a, both, over_core))
    own = [a for o, y in zip(halves, y_halves) for a in (o, y)]
    far = [a for o, y in zip(far_own, far_y) for a in (o, y)]
    _, width, half = gate_halves.shape
    hidden = 2 * half
    home_flag = home.astype(jnp.int32).reshape(1)
    expert_cat, expert_cat_t = pl.pallas_call(
        weights_kernel,
        in_specs=[smem_spec] + [any_spec] * 8,
        out_shape=(sds((width, 2 * hidden), BF16), sds((2 * hidden, width), BF16)),
        scratch_shapes=[pltpu.SemaphoreType.DMA((4,))],
        compiler_params=params(),
        cost_estimate=cost(1e9, 9 << 20),
        name="expert_weights",
    )(home_flag, *own[:4], *far[:4])
    expert_down_t = pl.pallas_call(
        down_kernel,
        in_specs=[smem_spec] + [any_spec] * 4,
        out_shape=sds((width, hidden), BF16),
        scratch_shapes=[pltpu.VMEM((half, width), BF16)] * 2 + [pltpu.SemaphoreType.DMA((2,))],
        compiler_params=params(),
        cost_estimate=cost(1e9, 3 << 20),
        name="expert_down",
    )(home_flag, *own[4:], *far[4:])

    ids_t, gates_t = route_ids.T, route_gates.T
    sel, send_input = pl.pallas_call(
        select_kernel,
        out_shape=(sds((slots, toks), BF16), sds((slots, width), BF16)),
        compiler_params=params(),
        cost_estimate=cost(2 * slots * toks * width, 4 << 20),
        name="select_rows",
    )(ids_t, moe_input)
    send_grad, mix_hi, mix_lo = pl.pallas_call(
        second_kernel,
        out_shape=(sds((slots, width), BF16), sds((toks, slots), BF16), sds((toks, slots), BF16)),
        compiler_params=params(),
        cost_estimate=cost(2 * slots * toks * width, 4 << 20),
        name="select_grads",
    )(ids_t, gates_t, sel, out_grad)

    def exchange(rows):
        shaped = rows.reshape(devices, SLOTS, width)
        return lax.all_to_all(shaped, both, split_axis=0, concat_axis=0, tiled=True).reshape(slots, width)

    recv_input = exchange(send_input)
    recv_grad = exchange(send_grad)

    def shift(rows, dz, dy):
        pairs = [(z * 4 + y, (z + dz) % 4 * 4 + (y + dy) % 4) for z in range(4) for y in range(4)]
        return lax.ppermute(rows, "head", pairs)

    proj_up, proj_dn = shift(out_proj, 1, 0), shift(out_proj, -1, 0)
    proj_far_up = shift(proj_up[: inner // 2], 1, 0)
    proj_far_dn = shift(proj_dn[inner // 2 :], -1, 0)

    flip = lambda i: blocks - 1 - i
    row_in = pl.BlockSpec((inner, BLOCK), lambda i: (0, flip(i)))
    tok_in = pl.BlockSpec((BLOCK, inner), lambda i: (flip(i), 0))
    tok_st = pl.BlockSpec((BLOCK, state), lambda i: (flip(i), 0))
    row_8 = pl.BlockSpec((8, BLOCK), lambda i: (0, flip(i)))
    blk_st = pl.BlockSpec((1, inner, state), lambda i: (flip(i), 0, 0))
    blk_8 = pl.BlockSpec((1, 8, state), lambda i: (flip(i), 0, 0))
    blk_w = pl.BlockSpec((1, heads, BLOCK, BLOCK), lambda i: (flip(i), 0, 0, 0))
    x_shape = sds((seq_rows, inner), BF16)
    w_shape = sds((blocks, heads, BLOCK, BLOCK), BF16)
    r_shape = sds((8, seq_rows), F32)
    w_hi, w_lo, to_start, to_end, to_last, x_hi, x_lo, e_hi, e_lo, t_hi, t_lo, block_sum, total = pl.pallas_call(
        prepare_kernel,
        grid=(blocks,),
        in_specs=[pl.BlockSpec((heads, BLOCK), lambda i: (0, flip(i))), tok_st, tok_st, row_in],
        out_specs=(blk_w,) * 2 + (row_8,) * 3 + (tok_in,) * 6 + (blk_8, whole((8, state))),
        out_shape=(w_shape,) * 2
        + (r_shape,) * 3
        + (x_shape,) * 6
        + (sds((blocks, 8, state), F32), sds((8, state), F32)),
        compiler_params=params(),
        cost_estimate=cost(4e9, 20 << 20),
        name="scan_prepare",
    )(log_decay, b_proj, c_proj, ssd_x.T)

    tile = 512
    row_spec = pl.BlockSpec((tile, width), lambda i: (i, 0))
    act_spec = pl.BlockSpec((tile, 2 * hidden), lambda i: (i, 0))
    factors = pl.pallas_call(
        acts_kernel,
        grid=(slots // tile,),
        in_specs=[row_spec, whole((width, 2 * hidden))],
        out_specs=act_spec,
        out_shape=sds((slots, 2 * hidden), F32),
        compiler_params=params(),
        cost_estimate=cost(4 * slots * width * hidden, 10 << 20),
        name="expert_acts",
    )(recv_input, expert_cat)
    expert_rows = pl.pallas_call(
        back_kernel,
        grid=(slots // tile,),
        in_specs=[row_spec, act_spec, any_spec, any_spec],
        out_specs=row_spec,
        out_shape=sds((slots, width), BF16),
        scratch_shapes=[
            pltpu.VMEM((width, hidden), BF16),
            pltpu.VMEM((2 * hidden, width), BF16),
            pltpu.SemaphoreType.DMA((2,)),
        ],
        compiler_params=params(),
        cost_estimate=cost(6 * slots * width * hidden, 14 << 20),
        name="expert_back",
    )(recv_grad, factors, expert_down_t, expert_cat_t)
    returned = exchange(expert_rows)

    resid_grad, first, second = pl.pallas_call(
        combine_kernel,
        out_shape=(sds((toks, width), BF16),) + (sds((toks // 2, width), BF16),) * 2,
        compiler_params=params(),
        cost_estimate=cost(4 * slots * toks * width, 4 << 20),
        name="combine_rows",
    )(mix_hi, mix_lo, returned, out_grad)
    up_first = shift(first, 0, 1)
    dn_second = shift(second, 0, -1)
    up_second = shift(second, 0, 1)
    dn_first = shift(first, 0, -1)
    far_first = shift(up_first, 0, 1)
    far_second = shift(dn_second, 0, -1)
    part_spec = whole((n_head // 4, inner, toks))
    part_shape = sds((n_head // 4, inner, toks), BF16)
    halves_spec = whole((toks // 2, width))
    to_0, to_3, to_2, to_1 = pl.pallas_call(
        project_kernel,
        grid=(1,),
        in_specs=[smem_spec, whole((toks, width))] + [halves_spec] * 6 + [any_spec] * 5,
        out_specs=(part_spec,) * 4,
        out_shape=(part_shape,) * 4,
        scratch_shapes=[
            pltpu.VMEM((4 * toks, width), BF16),
            pltpu.VMEM((4 * inner, width), BF16),
            pltpu.SemaphoreType.DMA((5,)),
        ],
        compiler_params=params(24 << 20),
        cost_estimate=cost(32 * inner * toks * width, 7 << 20),
        name="project_rows",
    )(
        (head & 3).reshape(1),
        resid_grad,
        up_first,
        up_second,
        dn_first,
        dn_second,
        far_first,
        far_second,
        out_proj,
        proj_up,
        proj_far_up,
        proj_far_dn,
        proj_dn,
    )
    from_2 = shift(to_2, 2, 0)
    from_3 = shift(to_1, 1, 0)
    from_1 = shift(to_3, -1, 0)

    pay_rows = inner + 32
    future, payload, grads = pl.pallas_call(
        functools.partial(state_kernel, heads),
        out_shape=(
            sds((blocks, inner, state), F32),
            sds((n_seq, pay_rows, state), BF16),
            sds((n_head, inner, toks), BF16),
        ),
        grid=(1,),
        in_specs=[smem_spec]
        + [part_spec] * 4
        + [
            whole((seq_rows, state)),
            whole((8, seq_rows)),
            whole((blocks, 8, state)),
            whole((8, state)),
        ],
        out_specs=(
            whole((blocks, inner, state)),
            whole((n_seq, pay_rows, state)),
            whole((n_head, inner, toks)),
        ),
        compiler_params=params(66000000),
        cost_estimate=cost(1e9, 4 << 20),
        name="scan_state",
    )((head >> 2).reshape(1), to_0, from_1, from_2, from_3, c_proj, to_start, block_sum, total)
    pays = lax.all_to_all(payload, seq_axes, split_axis=0, concat_axis=0, tiled=True)
    pair = 2
    spec = lambda *shape: pl.BlockSpec(shape, lambda i: (i,) + (0,) * (len(shape) - 1))
    cols = lambda *shape: pl.BlockSpec(shape, lambda i: (0, i))
    tok_in2, tok_st2 = spec(pair * BLOCK, inner), spec(pair * BLOCK, state)
    row_in2, row_82 = cols(inner, pair * BLOCK), cols(8, pair * BLOCK)
    w_spec = spec(pair, heads, BLOCK, BLOCK)
    part_x, part_b = pl.pallas_call(
        functools.partial(intra_kernel, heads),
        grid=(blocks // pair,),
        in_specs=[smem_spec, w_spec, w_spec, spec(pair * BLOCK // toks, inner, toks)]
        + [tok_in2] * 4
        + [row_82, tok_st2, tok_st2, spec(pair, inner, state)],
        out_specs=(row_in2, tok_st2),
        out_shape=(sds((inner, seq_rows), F32), sds((seq_rows, state), F32)),
        compiler_params=params(),
        cost_estimate=cost(4e9, 16 << 20),
        name="scan_intra",
    )(skip_gain, w_hi, w_lo, grads, x_hi, x_lo, e_hi, e_lo, to_end, b_proj, c_proj, future)
    partial_b, in_hi, in_lo = pl.pallas_call(
        functools.partial(finish_b_kernel, heads),
        grid=(blocks // pair,),
        in_specs=[smem_spec, whole((n_seq, pay_rows, state)), tok_in2, tok_in2, tok_st2],
        out_specs=(tok_st2, whole((inner, state)), whole((inner, state))),
        out_shape=(sds((seq_rows, state), BF16), sds((inner, state), BF16), sds((inner, state), BF16)),
        compiler_params=params(),
        cost_estimate=cost(4e8, 6 << 20),
        name="scan_finish_b",
    )(seq.reshape(1), pays, t_hi, t_lo, part_b)
    shares = lax.all_to_all(
        partial_b.reshape(n_head, seq_rows // n_head, state), "head", split_axis=0, concat_axis=0, tiled=True
    )
    grad_x = pl.pallas_call(
        functools.partial(finish_x_kernel, heads),
        grid=(blocks // pair,),
        in_specs=[whole((inner, state)), whole((inner, state)), row_82, tok_st2, row_in2],
        out_specs=row_in2,
        out_shape=sds((inner, seq_rows), F32),
        compiler_params=params(),
        cost_estimate=cost(4e8, 6 << 20),
        name="scan_finish_x",
    )(in_hi, in_lo, to_last, b_proj, part_x)
    b_grad = jnp.sum(shares.astype(F32), axis=0)
    return (resid_grad, grad_x.T, b_grad)


def solution(mesh):
    n_seq, n_head = mesh.shape["seq"], mesh.shape["head"]
    fine = jax.sharding.Mesh(mesh.devices.reshape(n_seq // 2, 2, n_head), ("x", "core", "head"))

    seq, every = ("x", "core"), ("x", "core", "head")
    return jax.shard_map(
        shards,
        mesh=fine,
        in_specs=(
            P(every, None),
            P(every, None),
            P(every, None),
            P(every, None),
            P(every, None, None),
            P(every, None, None),
            P(every, None, None),
            P("head", None),
            P(seq, "head"),
            P(seq, None),
            P(seq, None),
            P("head", seq),
            P("head"),
        ),
        out_specs=(P(every, None), P(seq, "head"), P(every, None)),
        check_vma=False,
    )
```

```python
import functools

import jax
import jax.numpy as jnp
from jax import lax
from jax.experimental import pallas as pl
from jax.experimental.pallas import tpu as pltpu
from jax.sharding import PartitionSpec as P


BLOCK = 256
SLOTS = 8
F32 = jnp.float32
BF16 = jnp.bfloat16
HIGHEST = lax.Precision.HIGHEST
NT = (((1,), (1,)), ((), ()))
NN = (((1,), (0,)), ((), ()))


def params(limit=67043328):
    return pltpu.CompilerParams(vmem_limit_bytes=limit)


def cost(flops, bytes_accessed):
    return pl.CostEstimate(flops=int(flops), bytes_accessed=int(bytes_accessed), transcendentals=0)


def split(a):
    hi = a.astype(BF16)
    return hi, (a - hi.astype(F32)).astype(BF16)


def dot(a, b, dims):
    return lax.dot_general(a, b, dims, preferred_element_type=F32)


def dot_high(a, b, dims):
    return lax.dot_general(a, b, dims, precision=HIGHEST, preferred_element_type=F32)


def slot_experts(rows, toks):
    row = lax.broadcasted_iota(jnp.int32, (rows, toks), 0)
    dev, slot = row >> 3, row & 7
    x, core, z, y = dev >> 5, (dev >> 4) & 1, (dev >> 2) & 3, dev & 3
    expert = (2 * x + (y & 1)) * 8 + 2 * z + (y >> 1)
    return expert, 2 * slot + core


def send_chunks(sel, rows, out_ref, buf_ref, sem):
    n = buf_ref.shape[1]
    copies = []
    for k in range(buf_ref.shape[0]):
        buf_ref[k] = dot(sel[k * n : (k + 1) * n], rows, NN).astype(BF16)
        copies.append(pltpu.make_async_copy(buf_ref.at[k], out_ref.at[pl.ds(k * n, n)], sem.at[k]))
        copies[-1].start()
    for c in copies:
        c.wait()


def select_kernel(ids_ref, rows_ref, sel_ref, out_ref, buf_ref, sem):
    slots, toks = sel_ref.shape
    expert, rank = slot_experts(slots, toks)
    named = ids_ref[0:1, :] == expert
    for k in range(1, ids_ref.shape[0]):
        named = jnp.logical_or(named, ids_ref[k : k + 1, :] == expert)
    named = jnp.where(named, 1.0, 0.0)
    earlier = jnp.where(
        lax.broadcasted_iota(jnp.int32, (toks, toks), 0)
        < lax.broadcasted_iota(jnp.int32, (toks, toks), 1),
        1.0,
        0.0,
    )
    before = dot(named.astype(BF16), earlier.astype(BF16), NN)
    sel = jnp.where(before == rank.astype(F32), named, 0.0).astype(BF16)
    sel_ref[...] = sel
    send_chunks(sel, rows_ref[...], out_ref, buf_ref, sem)


def second_kernel(ids_ref, gates_ref, sel_ref, rows_ref, out_ref, mix_ref):
    slots, toks = sel_ref.shape
    out_ref[...] = dot(sel_ref[...], rows_ref[...], NN).astype(BF16)
    expert, _ = slot_experts(slots, toks)
    gate = jnp.zeros((slots, toks), F32)
    for k in range(ids_ref.shape[0]):
        gate = jnp.where(ids_ref[k : k + 1, :] == expert, gates_ref[k : k + 1, :], gate)
    mix = (gate * sel_ref[...].astype(F32)).T
    mix_ref[:toks, :], mix_ref[toks:, :] = split(mix)


def copy_half(home_ref, own, far, targets, sem):
    def copies(sources):
        return [pltpu.make_async_copy(s.at[0], t, sem.at[k]) for k, (s, t) in enumerate(zip(sources, targets))]

    @pl.when(home_ref[0] == 1)
    def _():
        for c in copies(own):
            c.start()

    @pl.when(home_ref[0] == 0)
    def _():
        for c in copies(far):
            c.start()

    return copies(own)


def weights_kernel(home_ref, *refs):
    own, far, cat_ref, cat_t_ref, sem = refs[:4], refs[4:8], refs[8], refs[9], refs[10]
    half = cat_ref.shape[1] // 4
    targets = [cat_ref.at[:, pl.ds(k * half, half)] for k in range(4)]
    for k, c in enumerate(copy_half(home_ref, own, far, targets, sem)):
        c.wait()
        cat_t_ref[k * half : (k + 1) * half, :] = cat_ref[:, k * half : (k + 1) * half].T


def acts_kernel(x_ref, w_ref, out_ref):
    act = dot(x_ref[...], w_ref[...], NN)
    hidden = act.shape[1] // 2
    gate, up = act[:, :hidden], act[:, hidden:]
    sig = jax.nn.sigmoid(gate)
    out_ref[:, :hidden] = up * sig * (1.0 + gate * (1.0 - sig))
    out_ref[:, hidden:] = gate * sig


def back_kernel(home_ref, g_ref, act_ref, cat_ref, *refs):
    own, far, out_ref, down_buf, cat_buf, sem, cat_sem = refs[:2], refs[2:4], *refs[4:]
    first = pl.program_id(0) == 0
    half = down_buf.shape[0] // 2
    targets = [down_buf.at[pl.ds(k * half, half)] for k in range(2)]
    cat_copy = pltpu.make_async_copy(cat_ref, cat_buf, cat_sem)

    @pl.when(first)
    def _():
        waits = copy_half(home_ref, own, far, targets, sem)
        cat_copy.start()
        for c in waits:
            c.wait()

    grad = dot(g_ref[...], down_buf[...], NT)
    hidden = grad.shape[1]
    both = jnp.concatenate(
        [(grad * act_ref[:, :hidden]).astype(BF16), (grad * act_ref[:, hidden:]).astype(BF16)], axis=1
    )

    @pl.when(first)
    def _():
        cat_copy.wait()

    out_ref[...] = dot(both, cat_buf[...], NN).astype(BF16)


def combine_kernel(mix_ref, rows_ref, grad_ref, out_ref, first_ref, second_ref, buf_ref, sem):
    n = buf_ref.shape[1]
    copies = [
        pltpu.make_async_copy(rows_ref.at[pl.ds(k * n, n)], buf_ref.at[k], sem.at[k]) for k in range(buf_ref.shape[0])
    ]
    for c in copies:
        c.start()
    total = None
    for k, c in enumerate(copies):
        c.wait()
        part = dot(mix_ref[:, k * n : (k + 1) * n], buf_ref[k], NN)
        total = part if total is None else total + part
    toks = out_ref.shape[0]
    resid = (grad_ref[...].astype(F32) + total[:toks] + total[toks:]).astype(BF16)
    out_ref[...] = resid
    first_ref[...] = resid[: toks // 2]
    second_ref[...] = resid[toks // 2 :]


def project_kernel(y_ref, *refs):
    resids, projs, outs, toks_ref, buf_ref, sem = refs[:7], refs[7:12], refs[12:16], refs[16], refs[17], refs[18]
    copies = []
    at = 0
    for k, source in enumerate(projs):
        n = source.shape[0]
        copies.append(pltpu.make_async_copy(source, buf_ref.at[pl.ds(at, n)], sem.at[k]))
        at += n
    for c in copies:
        c.start()
    toks = resids[0].shape[0]
    half = toks // 2
    for source, (dy, at) in zip(resids, ((0, 0), (3, 0), (3, half), (1, 0), (1, half), (2, 0), (2, half))):
        place = ((y_ref[0] + dy) & 3) * toks + at
        toks_ref[pl.ds(pl.multiple_of(place, half), source.shape[0]), :] = source[...]
    line = toks_ref[...]
    rows = outs[0].shape[1]
    for k, waits in enumerate(((0, 1), (2, 3, 4))):
        for w in waits:
            copies[w].wait()
        g = dot(buf_ref[2 * k * rows : 2 * (k + 1) * rows, :], line, NT).astype(BF16)
        for i in range(2):
            for q in range(4):
                outs[2 * k + i][q] = g[i * rows : (i + 1) * rows, q * toks : (q + 1) * toks]


def block_grads(g_ref, k):
    return jnp.concatenate([g_ref[2 * k], g_ref[2 * k + 1]], axis=1)


def head_rows(rows, heads, dim):
    n = rows.shape[1]
    return jnp.concatenate([jnp.broadcast_to(rows[h : h + 1, :], (dim, n)) for h in range(heads)], axis=0)


def prepare_kernel(
    d_ref, b_ref, c_ref, x_ref, wh_ref, wl_ref, ts_ref, te_ref, tt_ref, xh_ref, xl_ref, eh_ref, el_ref, th_ref, tl_ref,
    bs_ref, tot_ref,
):
    heads, n = d_ref.shape
    dim = x_ref.shape[0] // heads
    row = lax.broadcasted_iota(jnp.int32, (n, n), 0)
    col = lax.broadcasted_iota(jnp.int32, (n, n), 1)
    tri = jnp.where(col <= row, 1.0, 0.0)
    d = jnp.concatenate([d_ref[...], jnp.zeros((8 - heads, n), F32)], axis=0)
    across = dot_high(d, tri, NT)
    down = dot_high(tri, d, NT)
    scores = dot_high(b_ref[...], c_ref[...], NT)
    later = col >= row
    for h in range(heads):
        gap = across[h : h + 1, :] - down[:, h : h + 1]
        w = jnp.where(later, jnp.exp(jnp.where(later, gap, 0.0)), 0.0) * scores
        wh_ref[0, h], wl_ref[0, h] = split(w)

    @pl.when(pl.program_id(0) == 0)
    def _():
        tot_ref[...] = jnp.zeros_like(tot_ref)

    last = across[:, n - 1 : n]
    te = jnp.exp(last - across)
    tt = jnp.exp(last - across + tot_ref[:, 0:1])
    ts_ref[...] = jnp.exp(across)
    te_ref[...] = te
    tt_ref[...] = tt
    x = x_ref[...]
    xh_ref[...], xl_ref[...] = split(x.T)
    eh_ref[...], el_ref[...] = split((x * head_rows(te, heads, dim)).T)
    th_ref[...], tl_ref[...] = split((x * head_rows(tt, heads, dim)).T)
    block_sum = jnp.broadcast_to(last, tot_ref.shape)
    bs_ref[0] = block_sum
    tot_ref[...] = tot_ref[...] + block_sum


def state_kernel(heads, z_ref, g0_ref, g1_ref, g2_ref, g3_ref, c_ref, ts_ref, bs_ref, tot_ref, fut_ref, pay_ref, g_ref):
    blocks, rows, lanes = fut_ref.shape
    dim = rows // heads
    n = c_ref.shape[0] // blocks
    for dz, source in enumerate((g0_ref, g1_ref, g2_ref, g3_ref)):
        g_ref[pl.ds(((z_ref[0] + dz) & 3) * 4, 4)] = source[...]
    states = []
    for k in range(blocks):
        at = slice(k * n, (k + 1) * n)
        g = block_grads(g_ref, k).astype(F32)
        ghi, glo = split(g * head_rows(ts_ref[:, at], heads, dim))
        chi, clo = split(c_ref[at, :])
        wide = dot(ghi, jnp.concatenate([chi, clo], axis=1), NN)
        states.append(wide[:, :lanes] + wide[:, lanes:] + dot(glo, chi, NN))
    carry = jnp.zeros((rows, lanes), F32)
    for k in reversed(range(blocks)):
        fut_ref[k] = carry
        carry = head_rows(jnp.exp(bs_ref[k]), heads, dim) * carry + states[k]
    first = tot_ref[...]
    hi, _ = split(first)
    mid, low = split(first - hi.astype(F32))
    sent = jnp.concatenate([carry.astype(BF16), hi, mid, low, low], axis=0)
    for j in range(pay_ref.shape[0]):
        pay_ref[j] = sent


def intra_kernel(
    heads, skip_ref, wh_ref, wl_ref, g_ref, xh_ref, xl_ref, eh_ref, el_ref, te_ref, b_ref, c_ref, fut_ref, gx_ref, pb_ref
):
    n = wh_ref.shape[2]
    rows = gx_ref.shape[0]
    dim = rows // heads
    for k in range(wh_ref.shape[0]):
        at = slice(k * n, (k + 1) * n)
        fhi, flo = split(fut_ref[k])
        bhi, blo = split(b_ref[at, :])
        cross = dot(fhi, bhi, NT) + dot(flo, bhi, NT) + dot(fhi, blo, NT)
        cross = cross * head_rows(te_ref[:, at], heads, dim)
        acc = None
        grads = block_grads(g_ref, k)
        for h in range(heads):
            w = wh_ref[k, h]
            cols = slice(h * dim, (h + 1) * dim)
            g = grads[cols]
            gx_ref[cols, at] = dot(g, w, NT) + cross[cols] + skip_ref[h] * g.astype(F32)
            inner = dot(xh_ref[at, cols], g, NN) + dot(xl_ref[at, cols], g, NN)
            term = (w.astype(F32) + wl_ref[k, h].astype(F32)) * inner
            acc = term if acc is None else acc + term
        ahi, alo = split(acc)
        chi, clo = split(c_ref[at, :])
        eh = eh_ref[at, :]
        pb_ref[at, :] = (
            dot(ahi, chi, NN)
            + dot(alo, chi, NN)
            + dot(ahi, clo, NN)
            + dot(eh, fhi, NN)
            + dot(eh, flo, NN)
            + dot(el_ref[at, :], fhi, NN)
        )


def finish_b_kernel(heads, seq_ref, pay_ref, th_ref, tl_ref, pb_ref, out_ref, hi_ref, lo_ref):
    rows, lanes = hi_ref.shape
    dim = rows // heads

    @pl.when(pl.program_id(0) == 0)
    def _():
        place = seq_ref[0]
        acc = jnp.zeros((rows, lanes), F32)
        log = jnp.zeros((8, lanes), F32)
        for j in range(pay_ref.shape[0]):
            ahead = j > place
            factor = jnp.where(ahead, jnp.exp(log), 0.0)
            acc = acc + head_rows(factor, heads, dim) * pay_ref[j, 0:rows, :].astype(F32)
            tots = pay_ref[j, rows : rows + 32, :].astype(F32)
            log = log + jnp.where(ahead, tots[0:8] + tots[8:16] + tots[16:24], 0.0)
        hi_ref[...], lo_ref[...] = split(acc)

    hi = hi_ref[...]
    th = th_ref[...]
    wide = dot(th, jnp.concatenate([hi, lo_ref[...]], axis=1), NN)
    total = pb_ref[...] + wide[:, :lanes] + wide[:, lanes:] + dot(tl_ref[...], hi, NN)
    out_ref[...] = total.astype(out_ref.dtype)


def finish_x_kernel(heads, hi_ref, lo_ref, tt_ref, b_ref, gx_ref, out_ref):
    bhi, blo = split(b_ref[...])
    hi = hi_ref[...]
    tt = head_rows(tt_ref[...], heads, out_ref.shape[0] // heads)
    out_ref[...] = gx_ref[...] + tt * (dot(hi, bhi, NT) + dot(lo_ref[...], bhi, NT) + dot(hi, blo, NT))


def whole(shape):
    zeros = (0,) * len(shape)
    return pl.BlockSpec(shape, lambda *_: zeros)


def shards(
    moe_input,
    out_grad,
    route_ids,
    route_gates,
    gate_halves,
    up_halves,
    down_halves,
    out_proj,
    ssd_x,
    b_proj,
    c_proj,
    log_decay,
    skip_gain,
):
    sds = jax.ShapeDtypeStruct
    toks, width = moe_input.shape
    seq_axes = ("x", "core")
    n_seq, n_head = lax.axis_size(seq_axes), lax.axis_size("head")
    devices = n_seq * n_head
    slots = devices * SLOTS
    both = ("x", "core", "head")
    smem_spec = pl.BlockSpec(memory_space=pltpu.SMEM)
    any_spec = pl.BlockSpec(memory_space=pl.ANY)
    heads = skip_gain.shape[0]
    inner = out_proj.shape[0]
    seq_rows, state = b_proj.shape
    blocks = seq_rows // BLOCK
    seq, head = lax.axis_index(seq_axes), lax.axis_index("head")
    core = lax.axis_index("core")

    home = core == (head & 1)
    over_y, over_core = [], []
    for s in range(n_seq):
        for h in range(n_head):
            if (s & 1) != (h & 1):
                over_y.append((s * n_head + h, s * n_head + (h ^ 1)))
            else:
                over_core.append((s * n_head + h, (s ^ 1) * n_head + h))
    halves = (gate_halves, up_halves, down_halves)
    y_halves, far_own = [], []
    for a in halves:
        y_halves.append(lax.ppermute(a, both, over_y))
    for a in halves:
        far_own.append(lax.ppermute(a, both, over_core))
    far_y = []
    for a in y_halves:
        far_y.append(lax.ppermute(a, both, over_core))
    own = [a for o, y in zip(halves, y_halves) for a in (o, y)]
    far = [a for o, y in zip(far_own, far_y) for a in (o, y)]
    _, width, half = gate_halves.shape
    hidden = 2 * half
    home_flag = home.astype(jnp.int32).reshape(1)
    expert_cat, expert_cat_t = pl.pallas_call(
        weights_kernel,
        in_specs=[smem_spec] + [any_spec] * 8,
        out_shape=(sds((width, 2 * hidden), BF16), sds((2 * hidden, width), BF16)),
        scratch_shapes=[pltpu.SemaphoreType.DMA((4,))],
        compiler_params=params(),
        cost_estimate=cost(1e9, 9 << 20),
        name="expert_weights",
    )(home_flag, *own[:4], *far[:4])
    ids_t, gates_t = route_ids.T, route_gates.T
    sel, send_input = pl.pallas_call(
        select_kernel,
        grid=(1,),
        in_specs=[whole(ids_t.shape), whole((toks, width))],
        out_specs=(whole((slots, toks)), any_spec),
        out_shape=(sds((slots, toks), BF16), sds((slots, width), BF16)),
        scratch_shapes=[pltpu.VMEM((4, slots // 4, width), BF16), pltpu.SemaphoreType.DMA((4,))],
        compiler_params=params(),
        cost_estimate=cost(2 * slots * toks * width, 4 << 20),
        name="select_rows",
    )(ids_t, moe_input)
    send_grad, mix = pl.pallas_call(
        second_kernel,
        out_shape=(sds((slots, width), BF16), sds((2 * toks, slots), BF16)),
        compiler_params=params(),
        cost_estimate=cost(2 * slots * toks * width, 4 << 20),
        name="select_grads",
    )(ids_t, gates_t, sel, out_grad)

    def exchange(rows):
        shaped = rows.reshape(devices, SLOTS, width)
        return lax.all_to_all(shaped, both, split_axis=0, concat_axis=0, tiled=True).reshape(slots, width)

    recv_input = exchange(send_input)
    recv_grad = exchange(send_grad)

    def shift(rows, dz, dy):
        pairs = [(z * 4 + y, (z + dz) % 4 * 4 + (y + dy) % 4) for z in range(4) for y in range(4)]
        return lax.ppermute(rows, "head", pairs)

    proj_up, proj_dn = shift(out_proj, 1, 0), shift(out_proj, -1, 0)
    proj_far_up = shift(proj_up[: inner // 2], 1, 0)
    proj_far_dn = shift(proj_dn[inner // 2 :], -1, 0)

    flip = lambda i: blocks - 1 - i
    row_in = pl.BlockSpec((inner, BLOCK), lambda i: (0, flip(i)))
    tok_in = pl.BlockSpec((BLOCK, inner), lambda i: (flip(i), 0))
    tok_st = pl.BlockSpec((BLOCK, state), lambda i: (flip(i), 0))
    row_8 = pl.BlockSpec((8, BLOCK), lambda i: (0, flip(i)))
    blk_st = pl.BlockSpec((1, inner, state), lambda i: (flip(i), 0, 0))
    blk_8 = pl.BlockSpec((1, 8, state), lambda i: (flip(i), 0, 0))
    blk_w = pl.BlockSpec((1, heads, BLOCK, BLOCK), lambda i: (flip(i), 0, 0, 0))
    x_shape = sds((seq_rows, inner), BF16)
    w_shape = sds((blocks, heads, BLOCK, BLOCK), BF16)
    r_shape = sds((8, seq_rows), F32)
    w_hi, w_lo, to_start, to_end, to_last, x_hi, x_lo, e_hi, e_lo, t_hi, t_lo, block_sum, total = pl.pallas_call(
        prepare_kernel,
        grid=(blocks,),
        in_specs=[pl.BlockSpec((heads, BLOCK), lambda i: (0, flip(i))), tok_st, tok_st, row_in],
        out_specs=(blk_w,) * 2 + (row_8,) * 3 + (tok_in,) * 6 + (blk_8, whole((8, state))),
        out_shape=(w_shape,) * 2
        + (r_shape,) * 3
        + (x_shape,) * 6
        + (sds((blocks, 8, state), F32), sds((8, state), F32)),
        compiler_params=params(),
        cost_estimate=cost(4e9, 20 << 20),
        name="scan_prepare",
    )(log_decay, b_proj, c_proj, ssd_x.T)

    tile = 512
    row_spec = pl.BlockSpec((tile, width), lambda i: (i, 0))
    act_spec = pl.BlockSpec((tile, 2 * hidden), lambda i: (i, 0))
    factors = pl.pallas_call(
        acts_kernel,
        grid=(slots // tile,),
        in_specs=[row_spec, whole((width, 2 * hidden))],
        out_specs=act_spec,
        out_shape=sds((slots, 2 * hidden), F32),
        compiler_params=params(),
        cost_estimate=cost(4 * slots * width * hidden, 10 << 20),
        name="expert_acts",
    )(recv_input, expert_cat)
    expert_rows = pl.pallas_call(
        back_kernel,
        grid=(slots // tile,),
        in_specs=[smem_spec, row_spec, act_spec] + [any_spec] * 5,
        out_specs=row_spec,
        out_shape=sds((slots, width), BF16),
        scratch_shapes=[
            pltpu.VMEM((hidden, width), BF16),
            pltpu.VMEM((2 * hidden, width), BF16),
            pltpu.SemaphoreType.DMA((2,)),
            pltpu.SemaphoreType.DMA,
        ],
        compiler_params=params(),
        cost_estimate=cost(6 * slots * width * hidden, 14 << 20),
        name="expert_back",
    )(home_flag, recv_grad, factors, expert_cat_t, *own[4:], *far[4:])
    returned = exchange(expert_rows)

    resid_grad, first, second = pl.pallas_call(
        combine_kernel,
        grid=(1,),
        in_specs=[whole((2 * toks, slots)), any_spec, whole((toks, width))],
        out_specs=(whole((toks, width)),) + (whole((toks // 2, width)),) * 2,
        out_shape=(sds((toks, width), BF16),) + (sds((toks // 2, width), BF16),) * 2,
        scratch_shapes=[pltpu.VMEM((2, slots // 2, width), BF16), pltpu.SemaphoreType.DMA((2,))],
        compiler_params=params(),
        cost_estimate=cost(4 * slots * toks * width, 4 << 20),
        name="combine_rows",
    )(mix, returned, out_grad)
    up_first = shift(first, 0, 1)
    dn_second = shift(second, 0, -1)
    up_second = shift(second, 0, 1)
    dn_first = shift(first, 0, -1)
    far_first = shift(up_first, 0, 1)
    far_second = shift(dn_second, 0, -1)
    part_spec = whole((n_head // 4, inner, toks))
    part_shape = sds((n_head // 4, inner, toks), BF16)
    halves_spec = whole((toks // 2, width))
    to_0, to_3, to_2, to_1 = pl.pallas_call(
        project_kernel,
        grid=(1,),
        in_specs=[smem_spec, whole((toks, width))] + [halves_spec] * 6 + [any_spec] * 5,
        out_specs=(part_spec,) * 4,
        out_shape=(part_shape,) * 4,
        scratch_shapes=[
            pltpu.VMEM((4 * toks, width), BF16),
            pltpu.VMEM((4 * inner, width), BF16),
            pltpu.SemaphoreType.DMA((5,)),
        ],
        compiler_params=params(24 << 20),
        cost_estimate=cost(32 * inner * toks * width, 7 << 20),
        name="project_rows",
    )(
        (head & 3).reshape(1),
        resid_grad,
        up_first,
        up_second,
        dn_first,
        dn_second,
        far_first,
        far_second,
        out_proj,
        proj_up,
        proj_far_up,
        proj_far_dn,
        proj_dn,
    )
    from_2 = shift(to_2, 2, 0)
    from_3 = shift(to_1, 1, 0)
    from_1 = shift(to_3, -1, 0)

    pay_rows = inner + 32
    future, payload, grads = pl.pallas_call(
        functools.partial(state_kernel, heads),
        out_shape=(
            sds((blocks, inner, state), F32),
            sds((n_seq, pay_rows, state), BF16),
            sds((n_head, inner, toks), BF16),
        ),
        grid=(1,),
        in_specs=[smem_spec]
        + [part_spec] * 4
        + [
            whole((seq_rows, state)),
            whole((8, seq_rows)),
            whole((blocks, 8, state)),
            whole((8, state)),
        ],
        out_specs=(
            whole((blocks, inner, state)),
            whole((n_seq, pay_rows, state)),
            whole((n_head, inner, toks)),
        ),
        compiler_params=params(66000000),
        cost_estimate=cost(1e9, 4 << 20),
        name="scan_state",
    )((head >> 2).reshape(1), to_0, from_1, from_2, from_3, c_proj, to_start, block_sum, total)
    pays = lax.all_to_all(payload, seq_axes, split_axis=0, concat_axis=0, tiled=True)
    pair = 2
    spec = lambda *shape: pl.BlockSpec(shape, lambda i: (i,) + (0,) * (len(shape) - 1))
    cols = lambda *shape: pl.BlockSpec(shape, lambda i: (0, i))
    tok_in2, tok_st2 = spec(pair * BLOCK, inner), spec(pair * BLOCK, state)
    row_in2, row_82 = cols(inner, pair * BLOCK), cols(8, pair * BLOCK)
    w_spec = spec(pair, heads, BLOCK, BLOCK)
    part_x, part_b = pl.pallas_call(
        functools.partial(intra_kernel, heads),
        grid=(blocks // pair,),
        in_specs=[smem_spec, w_spec, w_spec, spec(pair * BLOCK // toks, inner, toks)]
        + [tok_in2] * 4
        + [row_82, tok_st2, tok_st2, spec(pair, inner, state)],
        out_specs=(row_in2, tok_st2),
        out_shape=(sds((inner, seq_rows), F32), sds((seq_rows, state), F32)),
        compiler_params=params(),
        cost_estimate=cost(4e9, 16 << 20),
        name="scan_intra",
    )(skip_gain, w_hi, w_lo, grads, x_hi, x_lo, e_hi, e_lo, to_end, b_proj, c_proj, future)
    partial_b, in_hi, in_lo = pl.pallas_call(
        functools.partial(finish_b_kernel, heads),
        grid=(2,),
        in_specs=[
            smem_spec,
            whole((n_seq, pay_rows, state)),
            spec(seq_rows // 2, inner),
            spec(seq_rows // 2, inner),
            spec(seq_rows // 2, state),
        ],
        out_specs=(spec(seq_rows // 2, state), whole((inner, state)), whole((inner, state))),
        out_shape=(sds((seq_rows, state), BF16), sds((inner, state), BF16), sds((inner, state), BF16)),
        compiler_params=params(),
        cost_estimate=cost(4e8, 6 << 20),
        name="scan_finish_b",
    )(seq.reshape(1), pays, t_hi, t_lo, part_b)
    shares = lax.all_to_all(
        partial_b.reshape(n_head, seq_rows // n_head, state), "head", split_axis=0, concat_axis=0, tiled=True
    )
    grad_x = pl.pallas_call(
        functools.partial(finish_x_kernel, heads),
        grid=(blocks // pair,),
        in_specs=[whole((inner, state)), whole((inner, state)), row_82, tok_st2, row_in2],
        out_specs=row_in2,
        out_shape=sds((inner, seq_rows), F32),
        compiler_params=params(),
        cost_estimate=cost(4e8, 6 << 20),
        name="scan_finish_x",
    )(in_hi, in_lo, to_last, b_proj, part_x)
    b_grad = jnp.sum(shares.astype(F32), axis=0)
    return (resid_grad, grad_x.T, b_grad)


def solution(mesh):
    n_seq, n_head = mesh.shape["seq"], mesh.shape["head"]
    fine = jax.sharding.Mesh(mesh.devices.reshape(n_seq // 2, 2, n_head), ("x", "core", "head"))

    seq, every = ("x", "core"), ("x", "core", "head")
    return jax.shard_map(
        shards,
        mesh=fine,
        in_specs=(
            P(every, None),
            P(every, None),
            P(every, None),
            P(every, None),
            P(every, None, None),
            P(every, None, None),
            P(every, None, None),
            P("head", None),
            P(seq, "head"),
            P(seq, None),
            P(seq, None),
            P("head", seq),
            P("head"),
        ),
        out_specs=(P(every, None), P(seq, "head"), P(every, None)),
        check_vma=False,
    )
```

```python
import functools

import jax
import jax.numpy as jnp
from jax import lax
from jax.experimental import pallas as pl
from jax.experimental.pallas import tpu as pltpu
from jax.sharding import PartitionSpec as P


BLOCK = 256
SLOTS = 8
F32 = jnp.float32
BF16 = jnp.bfloat16
HIGHEST = lax.Precision.HIGHEST
NT = (((1,), (1,)), ((), ()))
NN = (((1,), (0,)), ((), ()))


def params(limit=67043328):
    return pltpu.CompilerParams(vmem_limit_bytes=limit)


def cost(flops, bytes_accessed):
    return pl.CostEstimate(flops=int(flops), bytes_accessed=int(bytes_accessed), transcendentals=0)


def split(a):
    hi = a.astype(BF16)
    return hi, (a - hi.astype(F32)).astype(BF16)


def dot(a, b, dims):
    return lax.dot_general(a, b, dims, preferred_element_type=F32)


def dot_high(a, b, dims):
    return lax.dot_general(a, b, dims, precision=HIGHEST, preferred_element_type=F32)


def slot_experts(rows, toks, at=0):
    row = lax.broadcasted_iota(jnp.int32, (rows, toks), 0) + at
    dev, slot = row >> 3, row & 7
    x, core, z, y = dev >> 5, (dev >> 4) & 1, (dev >> 2) & 3, dev & 3
    expert = (2 * x + (y & 1)) * 8 + 2 * z + (y >> 1)
    return expert, 2 * slot + core


def select_kernel(ids_ref, rows_ref, sel_ref, out_ref):
    slots, toks = sel_ref.shape
    expert, rank = slot_experts(slots, toks, pl.program_id(0) * slots)
    named = ids_ref[0:1, :] == expert
    for k in range(1, ids_ref.shape[0]):
        named = jnp.logical_or(named, ids_ref[k : k + 1, :] == expert)
    named = jnp.where(named, 1.0, 0.0)
    earlier = jnp.where(
        lax.broadcasted_iota(jnp.int32, (toks, toks), 0)
        < lax.broadcasted_iota(jnp.int32, (toks, toks), 1),
        1.0,
        0.0,
    )
    before = dot(named.astype(BF16), earlier.astype(BF16), NN)
    sel = jnp.where(before == rank.astype(F32), named, 0.0).astype(BF16)
    sel_ref[...] = sel
    out_ref[...] = dot(sel, rows_ref[...], NN).astype(BF16)


def second_kernel(ids_ref, gates_ref, sel_ref, rows_ref, out_ref, hi_ref, lo_ref):
    slots, toks = sel_ref.shape
    out_ref[...] = dot(sel_ref[...], rows_ref[...], NN).astype(BF16)
    expert, _ = slot_experts(slots, toks)
    gate = jnp.zeros((slots, toks), F32)
    for k in range(ids_ref.shape[0]):
        gate = jnp.where(ids_ref[k : k + 1, :] == expert, gates_ref[k : k + 1, :], gate)
    mix = (gate * sel_ref[...].astype(F32)).T
    hi, lo = split(mix)
    hi_ref[...] = hi
    lo_ref[...] = lo


def copy_half(home_ref, own, far, targets, sem):
    def copies(sources):
        return [pltpu.make_async_copy(s.at[0], t, sem.at[k]) for k, (s, t) in enumerate(zip(sources, targets))]

    @pl.when(home_ref[0] == 1)
    def _():
        for c in copies(own):
            c.start()

    @pl.when(home_ref[0] == 0)
    def _():
        for c in copies(far):
            c.start()

    return copies(own)


def weights_kernel(home_ref, *refs):
    own, far, cat_ref, cat_t_ref, sem = refs[:4], refs[4:8], refs[8], refs[9], refs[10]
    half = cat_ref.shape[1] // 4
    targets = [cat_ref.at[:, pl.ds(k * half, half)] for k in range(4)]
    for k, c in enumerate(copy_half(home_ref, own, far, targets, sem)):
        c.wait()
        cat_t_ref[k * half : (k + 1) * half, :] = cat_ref[:, k * half : (k + 1) * half].T


def acts_kernel(x_ref, w_ref, out_ref):
    act = dot(x_ref[...], w_ref[...], NN)
    hidden = act.shape[1] // 2
    gate, up = act[:, :hidden], act[:, hidden:]
    sig = jax.nn.sigmoid(gate)
    out_ref[:, :hidden] = up * sig * (1.0 + gate * (1.0 - sig))
    out_ref[:, hidden:] = gate * sig


def back_kernel(home_ref, g_ref, act_ref, cat_ref, *refs):
    own, far, out_ref, down_buf, cat_buf, sem, cat_sem = refs[:2], refs[2:4], *refs[4:]
    first = pl.program_id(0) == 0
    half = down_buf.shape[0] // 2
    targets = [down_buf.at[pl.ds(k * half, half)] for k in range(2)]
    cat_copy = pltpu.make_async_copy(cat_ref, cat_buf, cat_sem)

    @pl.when(first)
    def _():
        waits = copy_half(home_ref, own, far, targets, sem)
        cat_copy.start()
        for c in waits:
            c.wait()

    grad = dot(g_ref[...], down_buf[...], NT)
    hidden = grad.shape[1]
    both = jnp.concatenate(
        [(grad * act_ref[:, :hidden]).astype(BF16), (grad * act_ref[:, hidden:]).astype(BF16)], axis=1
    )

    @pl.when(first)
    def _():
        cat_copy.wait()

    out_ref[...] = dot(both, cat_buf[...], NN).astype(BF16)


def combine_kernel(hi_ref, lo_ref, rows_ref, grad_ref, out_ref, first_ref, second_ref, acc_ref):
    rows = rows_ref[...]
    part = dot(hi_ref[...], rows, NN) + dot(lo_ref[...], rows, NN)

    @pl.when(pl.program_id(0) == 0)
    def _():
        acc_ref[...] = grad_ref[...].astype(F32) + part

    @pl.when(pl.program_id(0) > 0)
    def _():
        acc_ref[...] = acc_ref[...] + part

    @pl.when(pl.program_id(0) == pl.num_programs(0) - 1)
    def _():
        resid = acc_ref[...].astype(BF16)
        out_ref[...] = resid
        half = first_ref.shape[0]
        first_ref[...] = resid[:half]
        second_ref[...] = resid[half:]


def project_kernel(y_ref, *refs):
    resids, projs, outs, toks_ref, buf_ref, sem = refs[:7], refs[7:12], refs[12:16], refs[16], refs[17], refs[18]
    copies = []
    at = 0
    for k, source in enumerate(projs):
        n = source.shape[0]
        copies.append(pltpu.make_async_copy(source, buf_ref.at[pl.ds(at, n)], sem.at[k]))
        at += n
    for c in copies:
        c.start()
    toks = resids[0].shape[0]
    half = toks // 2
    for source, (dy, at) in zip(resids, ((0, 0), (3, 0), (3, half), (1, 0), (1, half), (2, 0), (2, half))):
        place = ((y_ref[0] + dy) & 3) * toks + at
        toks_ref[pl.ds(pl.multiple_of(place, half), source.shape[0]), :] = source[...]
    line = toks_ref[...]
    rows = outs[0].shape[1]
    for k, waits in enumerate(((0, 1), (2, 3, 4))):
        for w in waits:
            copies[w].wait()
        g = dot(buf_ref[2 * k * rows : 2 * (k + 1) * rows, :], line, NT).astype(BF16)
        for i in range(2):
            for q in range(4):
                outs[2 * k + i][q] = g[i * rows : (i + 1) * rows, q * toks : (q + 1) * toks]


def block_grads(g_ref, k):
    return jnp.concatenate([g_ref[2 * k], g_ref[2 * k + 1]], axis=1)


def head_rows(rows, heads, dim):
    n = rows.shape[1]
    return jnp.concatenate([jnp.broadcast_to(rows[h : h + 1, :], (dim, n)) for h in range(heads)], axis=0)


def prepare_kernel(
    d_ref, b_ref, c_ref, x_ref, wh_ref, wl_ref, ts_ref, te_ref, tt_ref, xh_ref, xl_ref, eh_ref, el_ref, th_ref, tl_ref,
    bs_ref, tot_ref,
):
    heads, n = d_ref.shape
    dim = x_ref.shape[0] // heads
    row = lax.broadcasted_iota(jnp.int32, (n, n), 0)
    col = lax.broadcasted_iota(jnp.int32, (n, n), 1)
    tri = jnp.where(col <= row, 1.0, 0.0)
    d = jnp.concatenate([d_ref[...], jnp.zeros((8 - heads, n), F32)], axis=0)
    across = dot_high(d, tri, NT)
    down = dot_high(tri, d, NT)
    scores = dot_high(b_ref[...], c_ref[...], NT)
    later = col >= row
    for h in range(heads):
        gap = across[h : h + 1, :] - down[:, h : h + 1]
        w = jnp.where(later, jnp.exp(jnp.where(later, gap, 0.0)), 0.0) * scores
        wh_ref[0, h], wl_ref[0, h] = split(w)

    @pl.when(pl.program_id(0) == 0)
    def _():
        tot_ref[...] = jnp.zeros_like(tot_ref)

    last = across[:, n - 1 : n]
    te = jnp.exp(last - across)
    tt = jnp.exp(last - across + tot_ref[:, 0:1])
    ts_ref[...] = jnp.exp(across)
    te_ref[...] = te
    tt_ref[...] = tt
    x = x_ref[...]
    xh_ref[...], xl_ref[...] = split(x.T)
    eh_ref[...], el_ref[...] = split((x * head_rows(te, heads, dim)).T)
    th_ref[...], tl_ref[...] = split((x * head_rows(tt, heads, dim)).T)
    block_sum = jnp.broadcast_to(last, tot_ref.shape)
    bs_ref[0] = block_sum
    tot_ref[...] = tot_ref[...] + block_sum


def state_kernel(heads, z_ref, g0_ref, g1_ref, g2_ref, g3_ref, c_ref, ts_ref, bs_ref, tot_ref, fut_ref, pay_ref, g_ref):
    blocks, rows, lanes = fut_ref.shape
    dim = rows // heads
    n = c_ref.shape[0] // blocks
    for dz, source in enumerate((g0_ref, g1_ref, g2_ref, g3_ref)):
        g_ref[pl.ds(((z_ref[0] + dz) & 3) * 4, 4)] = source[...]
    states = []
    for k in range(blocks):
        at = slice(k * n, (k + 1) * n)
        g = block_grads(g_ref, k).astype(F32)
        ghi, glo = split(g * head_rows(ts_ref[:, at], heads, dim))
        chi, clo = split(c_ref[at, :])
        wide = dot(ghi, jnp.concatenate([chi, clo], axis=1), NN)
        states.append(wide[:, :lanes] + wide[:, lanes:] + dot(glo, chi, NN))
    carry = jnp.zeros((rows, lanes), F32)
    for k in reversed(range(blocks)):
        fut_ref[k] = carry
        carry = head_rows(jnp.exp(bs_ref[k]), heads, dim) * carry + states[k]
    first = tot_ref[...]
    hi, _ = split(first)
    mid, low = split(first - hi.astype(F32))
    sent = jnp.concatenate([carry.astype(BF16), hi, mid, low, low], axis=0)
    for j in range(pay_ref.shape[0]):
        pay_ref[j] = sent


def intra_kernel(
    heads, skip_ref, wh_ref, wl_ref, g_ref, xh_ref, xl_ref, eh_ref, el_ref, te_ref, b_ref, c_ref, fut_ref, gx_ref, pb_ref
):
    n = wh_ref.shape[2]
    rows = gx_ref.shape[0]
    dim = rows // heads
    for k in range(wh_ref.shape[0]):
        at = slice(k * n, (k + 1) * n)
        fhi, flo = split(fut_ref[k])
        bhi, blo = split(b_ref[at, :])
        cross = dot(fhi, bhi, NT) + dot(flo, bhi, NT) + dot(fhi, blo, NT)
        cross = cross * head_rows(te_ref[:, at], heads, dim)
        acc = None
        grads = block_grads(g_ref, k)
        for h in range(heads):
            w = wh_ref[k, h]
            cols = slice(h * dim, (h + 1) * dim)
            g = grads[cols]
            gx_ref[cols, at] = dot(g, w, NT) + cross[cols] + skip_ref[h] * g.astype(F32)
            inner = dot(xh_ref[at, cols], g, NN) + dot(xl_ref[at, cols], g, NN)
            term = (w.astype(F32) + wl_ref[k, h].astype(F32)) * inner
            acc = term if acc is None else acc + term
        ahi, alo = split(acc)
        chi, clo = split(c_ref[at, :])
        eh = eh_ref[at, :]
        pb_ref[at, :] = (
            dot(ahi, chi, NN)
            + dot(alo, chi, NN)
            + dot(ahi, clo, NN)
            + dot(eh, fhi, NN)
            + dot(eh, flo, NN)
            + dot(el_ref[at, :], fhi, NN)
        )


def finish_b_kernel(heads, seq_ref, pay_ref, th_ref, tl_ref, pb_ref, out_ref, hi_ref, lo_ref):
    rows, lanes = hi_ref.shape
    dim = rows // heads

    @pl.when(pl.program_id(0) == 0)
    def _():
        place = seq_ref[0]
        acc = jnp.zeros((rows, lanes), F32)
        log = jnp.zeros((8, lanes), F32)
        for j in range(pay_ref.shape[0]):
            ahead = j > place
            factor = jnp.where(ahead, jnp.exp(log), 0.0)
            acc = acc + head_rows(factor, heads, dim) * pay_ref[j, 0:rows, :].astype(F32)
            tots = pay_ref[j, rows : rows + 32, :].astype(F32)
            log = log + jnp.where(ahead, tots[0:8] + tots[8:16] + tots[16:24], 0.0)
        hi_ref[...], lo_ref[...] = split(acc)

    hi = hi_ref[...]
    th = th_ref[...]
    wide = dot(th, jnp.concatenate([hi, lo_ref[...]], axis=1), NN)
    total = pb_ref[...] + wide[:, :lanes] + wide[:, lanes:] + dot(tl_ref[...], hi, NN)
    out_ref[...] = total.astype(out_ref.dtype)


def finish_x_kernel(heads, hi_ref, lo_ref, tt_ref, b_ref, gx_ref, out_ref):
    bhi, blo = split(b_ref[...])
    hi = hi_ref[...]
    tt = head_rows(tt_ref[...], heads, out_ref.shape[0] // heads)
    out_ref[...] = gx_ref[...] + tt * (dot(hi, bhi, NT) + dot(lo_ref[...], bhi, NT) + dot(hi, blo, NT))


def whole(shape):
    zeros = (0,) * len(shape)
    return pl.BlockSpec(shape, lambda *_: zeros)


def shards(
    moe_input,
    out_grad,
    route_ids,
    route_gates,
    gate_halves,
    up_halves,
    down_halves,
    out_proj,
    ssd_x,
    b_proj,
    c_proj,
    log_decay,
    skip_gain,
):
    sds = jax.ShapeDtypeStruct
    toks, width = moe_input.shape
    seq_axes = ("x", "core")
    n_seq, n_head = lax.axis_size(seq_axes), lax.axis_size("head")
    devices = n_seq * n_head
    slots = devices * SLOTS
    both = ("x", "core", "head")
    smem_spec = pl.BlockSpec(memory_space=pltpu.SMEM)
    any_spec = pl.BlockSpec(memory_space=pl.ANY)
    heads = skip_gain.shape[0]
    inner = out_proj.shape[0]
    seq_rows, state = b_proj.shape
    blocks = seq_rows // BLOCK
    seq, head = lax.axis_index(seq_axes), lax.axis_index("head")
    core = lax.axis_index("core")

    home = core == (head & 1)
    over_y, over_core = [], []
    for s in range(n_seq):
        for h in range(n_head):
            if (s & 1) != (h & 1):
                over_y.append((s * n_head + h, s * n_head + (h ^ 1)))
            else:
                over_core.append((s * n_head + h, (s ^ 1) * n_head + h))
    halves = (gate_halves, up_halves, down_halves)
    y_halves, far_own = [], []
    for a in halves:
        y_halves.append(lax.ppermute(a, both, over_y))
    for a in halves:
        far_own.append(lax.ppermute(a, both, over_core))
    far_y = []
    for a in y_halves:
        far_y.append(lax.ppermute(a, both, over_core))
    own = [a for o, y in zip(halves, y_halves) for a in (o, y)]
    far = [a for o, y in zip(far_own, far_y) for a in (o, y)]
    _, width, half = gate_halves.shape
    hidden = 2 * half
    home_flag = home.astype(jnp.int32).reshape(1)
    expert_cat, expert_cat_t = pl.pallas_call(
        weights_kernel,
        in_specs=[smem_spec] + [any_spec] * 8,
        out_shape=(sds((width, 2 * hidden), BF16), sds((2 * hidden, width), BF16)),
        scratch_shapes=[pltpu.SemaphoreType.DMA((4,))],
        compiler_params=params(),
        cost_estimate=cost(1e9, 9 << 20),
        name="expert_weights",
    )(home_flag, *own[:4], *far[:4])
    strip = lambda columns: pl.BlockSpec((slots // 4, columns), lambda i: (i, 0))
    ids_t, gates_t = route_ids.T, route_gates.T
    sel, send_input = pl.pallas_call(
        select_kernel,
        grid=(4,),
        in_specs=[whole(ids_t.shape), whole((toks, width))],
        out_specs=(strip(toks), strip(width)),
        out_shape=(sds((slots, toks), BF16), sds((slots, width), BF16)),
        compiler_params=params(),
        cost_estimate=cost(2 * slots * toks * width, 4 << 20),
        name="select_rows",
    )(ids_t, moe_input)
    send_grad, mix_hi, mix_lo = pl.pallas_call(
        second_kernel,
        out_shape=(sds((slots, width), BF16), sds((toks, slots), BF16), sds((toks, slots), BF16)),
        compiler_params=params(),
        cost_estimate=cost(2 * slots * toks * width, 4 << 20),
        name="select_grads",
    )(ids_t, gates_t, sel, out_grad)

    def exchange(rows):
        shaped = rows.reshape(devices, SLOTS, width)
        return lax.all_to_all(shaped, both, split_axis=0, concat_axis=0, tiled=True).reshape(slots, width)

    recv_input = exchange(send_input)
    recv_grad = exchange(send_grad)

    def shift(rows, dz, dy):
        pairs = [(z * 4 + y, (z + dz) % 4 * 4 + (y + dy) % 4) for z in range(4) for y in range(4)]
        return lax.ppermute(rows, "head", pairs)

    proj_up, proj_dn = shift(out_proj, 1, 0), shift(out_proj, -1, 0)
    proj_far_up = shift(proj_up[: inner // 2], 1, 0)
    proj_far_dn = shift(proj_dn[inner // 2 :], -1, 0)

    flip = lambda i: blocks - 1 - i
    row_in = pl.BlockSpec((inner, BLOCK), lambda i: (0, flip(i)))
    tok_in = pl.BlockSpec((BLOCK, inner), lambda i: (flip(i), 0))
    tok_st = pl.BlockSpec((BLOCK, state), lambda i: (flip(i), 0))
    row_8 = pl.BlockSpec((8, BLOCK), lambda i: (0, flip(i)))
    blk_st = pl.BlockSpec((1, inner, state), lambda i: (flip(i), 0, 0))
    blk_8 = pl.BlockSpec((1, 8, state), lambda i: (flip(i), 0, 0))
    blk_w = pl.BlockSpec((1, heads, BLOCK, BLOCK), lambda i: (flip(i), 0, 0, 0))
    x_shape = sds((seq_rows, inner), BF16)
    w_shape = sds((blocks, heads, BLOCK, BLOCK), BF16)
    r_shape = sds((8, seq_rows), F32)
    w_hi, w_lo, to_start, to_end, to_last, x_hi, x_lo, e_hi, e_lo, t_hi, t_lo, block_sum, total = pl.pallas_call(
        prepare_kernel,
        grid=(blocks,),
        in_specs=[pl.BlockSpec((heads, BLOCK), lambda i: (0, flip(i))), tok_st, tok_st, row_in],
        out_specs=(blk_w,) * 2 + (row_8,) * 3 + (tok_in,) * 6 + (blk_8, whole((8, state))),
        out_shape=(w_shape,) * 2
        + (r_shape,) * 3
        + (x_shape,) * 6
        + (sds((blocks, 8, state), F32), sds((8, state), F32)),
        compiler_params=params(),
        cost_estimate=cost(4e9, 20 << 20),
        name="scan_prepare",
    )(log_decay, b_proj, c_proj, ssd_x.T)

    tile = 512
    row_spec = pl.BlockSpec((tile, width), lambda i: (i, 0))
    act_spec = pl.BlockSpec((tile, 2 * hidden), lambda i: (i, 0))
    factors = pl.pallas_call(
        acts_kernel,
        grid=(slots // tile,),
        in_specs=[row_spec, whole((width, 2 * hidden))],
        out_specs=act_spec,
        out_shape=sds((slots, 2 * hidden), F32),
        compiler_params=params(),
        cost_estimate=cost(4 * slots * width * hidden, 10 << 20),
        name="expert_acts",
    )(recv_input, expert_cat)
    expert_rows = pl.pallas_call(
        back_kernel,
        grid=(slots // tile,),
        in_specs=[smem_spec, row_spec, act_spec] + [any_spec] * 5,
        out_specs=row_spec,
        out_shape=sds((slots, width), BF16),
        scratch_shapes=[
            pltpu.VMEM((hidden, width), BF16),
            pltpu.VMEM((2 * hidden, width), BF16),
            pltpu.SemaphoreType.DMA((2,)),
            pltpu.SemaphoreType.DMA,
        ],
        compiler_params=params(),
        cost_estimate=cost(6 * slots * width * hidden, 14 << 20),
        name="expert_back",
    )(home_flag, recv_grad, factors, expert_cat_t, *own[4:], *far[4:])
    returned = exchange(expert_rows)

    resid_grad, first, second = pl.pallas_call(
        combine_kernel,
        grid=(2,),
        in_specs=[pl.BlockSpec((toks, slots // 2), lambda i: (0, i))] * 2
        + [pl.BlockSpec((slots // 2, width), lambda i: (i, 0)), whole((toks, width))],
        out_specs=(whole((toks, width)),) + (whole((toks // 2, width)),) * 2,
        out_shape=(sds((toks, width), BF16),) + (sds((toks // 2, width), BF16),) * 2,
        scratch_shapes=[pltpu.VMEM((toks, width), F32)],
        compiler_params=params(),
        cost_estimate=cost(4 * slots * toks * width, 4 << 20),
        name="combine_rows",
    )(mix_hi, mix_lo, returned, out_grad)
    up_first = shift(first, 0, 1)
    dn_second = shift(second, 0, -1)
    up_second = shift(second, 0, 1)
    dn_first = shift(first, 0, -1)
    far_first = shift(up_first, 0, 1)
    far_second = shift(dn_second, 0, -1)
    part_spec = whole((n_head // 4, inner, toks))
    part_shape = sds((n_head // 4, inner, toks), BF16)
    halves_spec = whole((toks // 2, width))
    to_0, to_3, to_2, to_1 = pl.pallas_call(
        project_kernel,
        grid=(1,),
        in_specs=[smem_spec, whole((toks, width))] + [halves_spec] * 6 + [any_spec] * 5,
        out_specs=(part_spec,) * 4,
        out_shape=(part_shape,) * 4,
        scratch_shapes=[
            pltpu.VMEM((4 * toks, width), BF16),
            pltpu.VMEM((4 * inner, width), BF16),
            pltpu.SemaphoreType.DMA((5,)),
        ],
        compiler_params=params(24 << 20),
        cost_estimate=cost(32 * inner * toks * width, 7 << 20),
        name="project_rows",
    )(
        (head & 3).reshape(1),
        resid_grad,
        up_first,
        up_second,
        dn_first,
        dn_second,
        far_first,
        far_second,
        out_proj,
        proj_up,
        proj_far_up,
        proj_far_dn,
        proj_dn,
    )
    from_2 = shift(to_2, 2, 0)
    from_3 = shift(to_1, 1, 0)
    from_1 = shift(to_3, -1, 0)

    pay_rows = inner + 32
    future, payload, grads = pl.pallas_call(
        functools.partial(state_kernel, heads),
        out_shape=(
            sds((blocks, inner, state), F32),
            sds((n_seq, pay_rows, state), BF16),
            sds((n_head, inner, toks), BF16),
        ),
        grid=(1,),
        in_specs=[smem_spec]
        + [part_spec] * 4
        + [
            whole((seq_rows, state)),
            whole((8, seq_rows)),
            whole((blocks, 8, state)),
            whole((8, state)),
        ],
        out_specs=(
            whole((blocks, inner, state)),
            whole((n_seq, pay_rows, state)),
            whole((n_head, inner, toks)),
        ),
        compiler_params=params(66000000),
        cost_estimate=cost(1e9, 4 << 20),
        name="scan_state",
    )((head >> 2).reshape(1), to_0, from_1, from_2, from_3, c_proj, to_start, block_sum, total)
    pays = lax.all_to_all(payload, seq_axes, split_axis=0, concat_axis=0, tiled=True)
    pair = 2
    spec = lambda *shape: pl.BlockSpec(shape, lambda i: (i,) + (0,) * (len(shape) - 1))
    cols = lambda *shape: pl.BlockSpec(shape, lambda i: (0, i))
    tok_in2, tok_st2 = spec(pair * BLOCK, inner), spec(pair * BLOCK, state)
    row_in2, row_82 = cols(inner, pair * BLOCK), cols(8, pair * BLOCK)
    w_spec = spec(pair, heads, BLOCK, BLOCK)
    part_x, part_b = pl.pallas_call(
        functools.partial(intra_kernel, heads),
        grid=(blocks // pair,),
        in_specs=[smem_spec, w_spec, w_spec, spec(pair * BLOCK // toks, inner, toks)]
        + [tok_in2] * 4
        + [row_82, tok_st2, tok_st2, spec(pair, inner, state)],
        out_specs=(row_in2, tok_st2),
        out_shape=(sds((inner, seq_rows), F32), sds((seq_rows, state), F32)),
        compiler_params=params(),
        cost_estimate=cost(4e9, 16 << 20),
        name="scan_intra",
    )(skip_gain, w_hi, w_lo, grads, x_hi, x_lo, e_hi, e_lo, to_end, b_proj, c_proj, future)
    partial_b, in_hi, in_lo = pl.pallas_call(
        functools.partial(finish_b_kernel, heads),
        grid=(2,),
        in_specs=[
            smem_spec,
            whole((n_seq, pay_rows, state)),
            spec(seq_rows // 2, inner),
            spec(seq_rows // 2, inner),
            spec(seq_rows // 2, state),
        ],
        out_specs=(spec(seq_rows // 2, state), whole((inner, state)), whole((inner, state))),
        out_shape=(sds((seq_rows, state), BF16), sds((inner, state), BF16), sds((inner, state), BF16)),
        compiler_params=params(),
        cost_estimate=cost(4e8, 6 << 20),
        name="scan_finish_b",
    )(seq.reshape(1), pays, t_hi, t_lo, part_b)
    shares = lax.all_to_all(
        partial_b.reshape(n_head, seq_rows // n_head, state), "head", split_axis=0, concat_axis=0, tiled=True
    )
    grad_x = pl.pallas_call(
        functools.partial(finish_x_kernel, heads),
        grid=(blocks // pair,),
        in_specs=[whole((inner, state)), whole((inner, state)), row_82, tok_st2, row_in2],
        out_specs=row_in2,
        out_shape=sds((inner, seq_rows), F32),
        compiler_params=params(),
        cost_estimate=cost(4e8, 6 << 20),
        name="scan_finish_x",
    )(in_hi, in_lo, to_last, b_proj, part_x)
    b_grad = jnp.sum(shares.astype(F32), axis=0)
    return (resid_grad, grad_x.T, b_grad)


def solution(mesh):
    n_seq, n_head = mesh.shape["seq"], mesh.shape["head"]
    fine = jax.sharding.Mesh(mesh.devices.reshape(n_seq // 2, 2, n_head), ("x", "core", "head"))

    seq, every = ("x", "core"), ("x", "core", "head")
    return jax.shard_map(
        shards,
        mesh=fine,
        in_specs=(
            P(every, None),
            P(every, None),
            P(every, None),
            P(every, None),
            P(every, None, None),
            P(every, None, None),
            P(every, None, None),
            P("head", None),
            P(seq, "head"),
            P(seq, None),
            P(seq, None),
            P("head", seq),
            P("head"),
        ),
        out_specs=(P(every, None), P(seq, "head"), P(every, None)),
        check_vma=False,
    )
```

```python
import functools

import jax
import jax.numpy as jnp
from jax import lax
from jax.experimental import pallas as pl
from jax.experimental.pallas import tpu as pltpu
from jax.sharding import PartitionSpec as P


BLOCK = 256
SLOTS = 8
F32 = jnp.float32
BF16 = jnp.bfloat16
HIGHEST = lax.Precision.HIGHEST
NT = (((1,), (1,)), ((), ()))
NN = (((1,), (0,)), ((), ()))


def params(limit=67043328):
    return pltpu.CompilerParams(vmem_limit_bytes=limit)


def cost(flops, bytes_accessed):
    return pl.CostEstimate(flops=int(flops), bytes_accessed=int(bytes_accessed), transcendentals=0)


def split(a):
    hi = a.astype(BF16)
    return hi, (a - hi.astype(F32)).astype(BF16)


def dot(a, b, dims):
    return lax.dot_general(a, b, dims, preferred_element_type=F32)


def dot_high(a, b, dims):
    return lax.dot_general(a, b, dims, precision=HIGHEST, preferred_element_type=F32)


def slot_experts(rows, toks):
    row = lax.broadcasted_iota(jnp.int32, (rows, toks), 0)
    dev, slot = row >> 3, row & 7
    x, core, z, y = dev >> 5, (dev >> 4) & 1, (dev >> 2) & 3, dev & 3
    expert = (2 * x + (y & 1)) * 8 + 2 * z + (y >> 1)
    return expert, 2 * slot + core


def select_kernel(ids_ref, rows_ref, sel_ref, out_ref):
    slots, toks = sel_ref.shape
    expert, rank = slot_experts(slots, toks)
    named = ids_ref[0:1, :] == expert
    for k in range(1, ids_ref.shape[0]):
        named = jnp.logical_or(named, ids_ref[k : k + 1, :] == expert)
    named = jnp.where(named, 1.0, 0.0)
    earlier = jnp.where(
        lax.broadcasted_iota(jnp.int32, (toks, toks), 0)
        < lax.broadcasted_iota(jnp.int32, (toks, toks), 1),
        1.0,
        0.0,
    )
    before = dot(named.astype(BF16), earlier.astype(BF16), NN)
    sel = jnp.where(before == rank.astype(F32), named, 0.0).astype(BF16)
    sel_ref[...] = sel
    out_ref[...] = dot(sel, rows_ref[...], NN).astype(BF16)


def second_kernel(ids_ref, gates_ref, sel_ref, rows_ref, out_ref, hi_ref, lo_ref):
    slots, toks = sel_ref.shape
    out_ref[...] = dot(sel_ref[...], rows_ref[...], NN).astype(BF16)
    expert, _ = slot_experts(slots, toks)
    gate = jnp.zeros((slots, toks), F32)
    for k in range(ids_ref.shape[0]):
        gate = jnp.where(ids_ref[k : k + 1, :] == expert, gates_ref[k : k + 1, :], gate)
    mix = (gate * sel_ref[...].astype(F32)).T
    hi, lo = split(mix)
    hi_ref[...] = hi
    lo_ref[...] = lo


def copy_half(home_ref, own, far, targets, sem):
    def copies(sources):
        return [pltpu.make_async_copy(s.at[0], t, sem.at[k]) for k, (s, t) in enumerate(zip(sources, targets))]

    @pl.when(home_ref[0] == 1)
    def _():
        for c in copies(own):
            c.start()

    @pl.when(home_ref[0] == 0)
    def _():
        for c in copies(far):
            c.start()

    return copies(own)


def weights_kernel(home_ref, *refs):
    own, far, cat_ref, cat_t_ref, sem = refs[:4], refs[4:8], refs[8], refs[9], refs[10]
    half = cat_ref.shape[1] // 4
    targets = [cat_ref.at[:, pl.ds(k * half, half)] for k in range(4)]
    for k, c in enumerate(copy_half(home_ref, own, far, targets, sem)):
        c.wait()
        cat_t_ref[k * half : (k + 1) * half, :] = cat_ref[:, k * half : (k + 1) * half].T


def acts_kernel(x_ref, w_ref, out_ref):
    act = dot(x_ref[...], w_ref[...], NN)
    hidden = act.shape[1] // 2
    gate, up = act[:, :hidden], act[:, hidden:]
    sig = jax.nn.sigmoid(gate)
    out_ref[:, :hidden] = up * sig * (1.0 + gate * (1.0 - sig))
    out_ref[:, hidden:] = gate * sig


def back_kernel(home_ref, g_ref, act_ref, cat_ref, *refs):
    own, far, out_ref, down_buf, cat_buf, sem, cat_sem = refs[:2], refs[2:4], *refs[4:]
    first = pl.program_id(0) == 0
    half = down_buf.shape[0] // 2
    targets = [down_buf.at[pl.ds(k * half, half)] for k in range(2)]
    cat_copy = pltpu.make_async_copy(cat_ref, cat_buf, cat_sem)

    @pl.when(first)
    def _():
        waits = copy_half(home_ref, own, far, targets, sem)
        cat_copy.start()
        for c in waits:
            c.wait()

    grad = dot(g_ref[...], down_buf[...], NT)
    hidden = grad.shape[1]
    both = jnp.concatenate(
        [(grad * act_ref[:, :hidden]).astype(BF16), (grad * act_ref[:, hidden:]).astype(BF16)], axis=1
    )

    @pl.when(first)
    def _():
        cat_copy.wait()

    out_ref[...] = dot(both, cat_buf[...], NN).astype(BF16)


def combine_kernel(hi_ref, lo_ref, rows_ref, grad_ref, out_ref, first_ref, second_ref, acc_ref):
    rows = rows_ref[...]
    part = dot(hi_ref[...], rows, NN) + dot(lo_ref[...], rows, NN)

    @pl.when(pl.program_id(0) == 0)
    def _():
        acc_ref[...] = grad_ref[...].astype(F32) + part

    @pl.when(pl.program_id(0) > 0)
    def _():
        acc_ref[...] = acc_ref[...] + part

    @pl.when(pl.program_id(0) == pl.num_programs(0) - 1)
    def _():
        resid = acc_ref[...].astype(BF16)
        out_ref[...] = resid
        half = first_ref.shape[0]
        first_ref[...] = resid[:half]
        second_ref[...] = resid[half:]


def project_kernel(y_ref, *refs):
    resids, projs, outs, toks_ref, buf_ref, sem = refs[:7], refs[7:12], refs[12:16], refs[16], refs[17], refs[18]
    copies = []
    at = 0
    for k, source in enumerate(projs):
        n = source.shape[0]
        copies.append(pltpu.make_async_copy(source, buf_ref.at[pl.ds(at, n)], sem.at[k]))
        at += n
    for c in copies:
        c.start()
    toks = resids[0].shape[0]
    half = toks // 2
    for source, (dy, at) in zip(resids, ((0, 0), (3, 0), (3, half), (1, 0), (1, half), (2, 0), (2, half))):
        place = ((y_ref[0] + dy) & 3) * toks + at
        toks_ref[pl.ds(pl.multiple_of(place, half), source.shape[0]), :] = source[...]
    line = toks_ref[...]
    rows = outs[0].shape[1]
    for k, waits in enumerate(((0, 1), (2, 3, 4))):
        for w in waits:
            copies[w].wait()
        g = dot(buf_ref[2 * k * rows : 2 * (k + 1) * rows, :], line, NT).astype(BF16)
        for i in range(2):
            for q in range(4):
                outs[2 * k + i][q] = g[i * rows : (i + 1) * rows, q * toks : (q + 1) * toks]


def block_grads(g_ref, k):
    return jnp.concatenate([g_ref[2 * k], g_ref[2 * k + 1]], axis=1)


def head_rows(rows, heads, dim):
    n = rows.shape[1]
    return jnp.concatenate([jnp.broadcast_to(rows[h : h + 1, :], (dim, n)) for h in range(heads)], axis=0)


def prepare_kernel(
    d_ref, b_ref, c_ref, x_ref, wh_ref, wl_ref, ts_ref, te_ref, tt_ref, xh_ref, xl_ref, eh_ref, el_ref, th_ref, tl_ref,
    bs_ref, tot_ref,
):
    heads, n = d_ref.shape
    dim = x_ref.shape[0] // heads
    row = lax.broadcasted_iota(jnp.int32, (n, n), 0)
    col = lax.broadcasted_iota(jnp.int32, (n, n), 1)
    tri = jnp.where(col <= row, 1.0, 0.0)
    d = jnp.concatenate([d_ref[...], jnp.zeros((8 - heads, n), F32)], axis=0)
    across = dot_high(d, tri, NT)
    down = dot_high(tri, d, NT)
    scores = dot_high(b_ref[...], c_ref[...], NT)
    later = col >= row
    for h in range(heads):
        gap = across[h : h + 1, :] - down[:, h : h + 1]
        w = jnp.where(later, jnp.exp(jnp.where(later, gap, 0.0)), 0.0) * scores
        wh_ref[0, h], wl_ref[0, h] = split(w)

    @pl.when(pl.program_id(0) == 0)
    def _():
        tot_ref[...] = jnp.zeros_like(tot_ref)

    last = across[:, n - 1 : n]
    te = jnp.exp(last - across)
    tt = jnp.exp(last - across + tot_ref[:, 0:1])
    ts_ref[...] = jnp.exp(across)
    te_ref[...] = te
    tt_ref[...] = tt
    x = x_ref[...]
    xh_ref[...], xl_ref[...] = split(x.T)
    eh_ref[...], el_ref[...] = split((x * head_rows(te, heads, dim)).T)
    th_ref[...], tl_ref[...] = split((x * head_rows(tt, heads, dim)).T)
    block_sum = jnp.broadcast_to(last, tot_ref.shape)
    bs_ref[0] = block_sum
    tot_ref[...] = tot_ref[...] + block_sum


def state_kernel(heads, z_ref, g0_ref, g1_ref, g2_ref, g3_ref, c_ref, ts_ref, bs_ref, tot_ref, fut_ref, pay_ref, g_ref):
    blocks, rows, lanes = fut_ref.shape
    dim = rows // heads
    n = c_ref.shape[0] // blocks
    for dz, source in enumerate((g0_ref, g1_ref, g2_ref, g3_ref)):
        g_ref[pl.ds(((z_ref[0] + dz) & 3) * 4, 4)] = source[...]
    states = []
    for k in range(blocks):
        at = slice(k * n, (k + 1) * n)
        g = block_grads(g_ref, k).astype(F32)
        ghi, glo = split(g * head_rows(ts_ref[:, at], heads, dim))
        chi, clo = split(c_ref[at, :])
        wide = dot(ghi, jnp.concatenate([chi, clo], axis=1), NN)
        states.append(wide[:, :lanes] + wide[:, lanes:] + dot(glo, chi, NN))
    carry = jnp.zeros((rows, lanes), F32)
    for k in reversed(range(blocks)):
        fut_ref[k] = carry
        carry = head_rows(jnp.exp(bs_ref[k]), heads, dim) * carry + states[k]
    first = tot_ref[...]
    hi, _ = split(first)
    mid, low = split(first - hi.astype(F32))
    sent = jnp.concatenate([carry.astype(BF16), hi, mid, low, low], axis=0)
    for j in range(pay_ref.shape[0]):
        pay_ref[j] = sent


def intra_kernel(
    heads, skip_ref, wh_ref, wl_ref, g_ref, xh_ref, xl_ref, eh_ref, el_ref, te_ref, b_ref, c_ref, fut_ref, gx_ref, pb_ref
):
    n = wh_ref.shape[2]
    rows = gx_ref.shape[0]
    dim = rows // heads
    for k in range(wh_ref.shape[0]):
        at = slice(k * n, (k + 1) * n)
        fhi, flo = split(fut_ref[k])
        bhi, blo = split(b_ref[at, :])
        cross = dot(fhi, bhi, NT) + dot(flo, bhi, NT) + dot(fhi, blo, NT)
        cross = cross * head_rows(te_ref[:, at], heads, dim)
        acc = None
        grads = block_grads(g_ref, k)
        for h in range(heads):
            w = wh_ref[k, h]
            cols = slice(h * dim, (h + 1) * dim)
            g = grads[cols]
            gx_ref[cols, at] = dot(g, w, NT) + cross[cols] + skip_ref[h] * g.astype(F32)
            inner = dot(xh_ref[at, cols], g, NN) + dot(xl_ref[at, cols], g, NN)
            term = (w.astype(F32) + wl_ref[k, h].astype(F32)) * inner
            acc = term if acc is None else acc + term
        ahi, alo = split(acc)
        chi, clo = split(c_ref[at, :])
        eh = eh_ref[at, :]
        pb_ref[at, :] = (
            dot(ahi, chi, NN)
            + dot(alo, chi, NN)
            + dot(ahi, clo, NN)
            + dot(eh, fhi, NN)
            + dot(eh, flo, NN)
            + dot(el_ref[at, :], fhi, NN)
        )


def finish_b_kernel(heads, seq_ref, pay_ref, th_ref, tl_ref, pb_ref, out_ref, hi_ref, lo_ref):
    rows, lanes = hi_ref.shape
    dim = rows // heads

    @pl.when(pl.program_id(0) == 0)
    def _():
        place = seq_ref[0]
        acc = jnp.zeros((rows, lanes), F32)
        log = jnp.zeros((8, lanes), F32)
        for j in range(pay_ref.shape[0]):
            ahead = j > place
            factor = jnp.where(ahead, jnp.exp(log), 0.0)
            acc = acc + head_rows(factor, heads, dim) * pay_ref[j, 0:rows, :].astype(F32)
            tots = pay_ref[j, rows : rows + 32, :].astype(F32)
            log = log + jnp.where(ahead, tots[0:8] + tots[8:16] + tots[16:24], 0.0)
        hi_ref[...], lo_ref[...] = split(acc)

    hi = hi_ref[...]
    th = th_ref[...]
    wide = dot(th, jnp.concatenate([hi, lo_ref[...]], axis=1), NN)
    total = pb_ref[...] + wide[:, :lanes] + wide[:, lanes:] + dot(tl_ref[...], hi, NN)
    out_ref[...] = total.astype(out_ref.dtype)


def finish_x_kernel(heads, hi_ref, lo_ref, tt_ref, b_ref, gx_ref, out_ref):
    bhi, blo = split(b_ref[...])
    hi = hi_ref[...]
    tt = head_rows(tt_ref[...], heads, out_ref.shape[0] // heads)
    out_ref[...] = gx_ref[...] + tt * (dot(hi, bhi, NT) + dot(lo_ref[...], bhi, NT) + dot(hi, blo, NT))


def whole(shape):
    zeros = (0,) * len(shape)
    return pl.BlockSpec(shape, lambda *_: zeros)


def shards(
    moe_input,
    out_grad,
    route_ids,
    route_gates,
    gate_halves,
    up_halves,
    down_halves,
    out_proj,
    ssd_x,
    b_proj,
    c_proj,
    log_decay,
    skip_gain,
):
    sds = jax.ShapeDtypeStruct
    toks, width = moe_input.shape
    seq_axes = ("x", "core")
    n_seq, n_head = lax.axis_size(seq_axes), lax.axis_size("head")
    devices = n_seq * n_head
    slots = devices * SLOTS
    both = ("x", "core", "head")
    smem_spec = pl.BlockSpec(memory_space=pltpu.SMEM)
    any_spec = pl.BlockSpec(memory_space=pl.ANY)
    heads = skip_gain.shape[0]
    inner = out_proj.shape[0]
    seq_rows, state = b_proj.shape
    blocks = seq_rows // BLOCK
    seq, head = lax.axis_index(seq_axes), lax.axis_index("head")
    core = lax.axis_index("core")

    home = core == (head & 1)
    over_y, over_core = [], []
    for s in range(n_seq):
        for h in range(n_head):
            if (s & 1) != (h & 1):
                over_y.append((s * n_head + h, s * n_head + (h ^ 1)))
            else:
                over_core.append((s * n_head + h, (s ^ 1) * n_head + h))
    halves = (gate_halves, up_halves, down_halves)
    y_halves, far_own = [], []
    for a in halves:
        y_halves.append(lax.ppermute(a, both, over_y))
    for a in halves:
        far_own.append(lax.ppermute(a, both, over_core))
    far_y = []
    for a in y_halves:
        far_y.append(lax.ppermute(a, both, over_core))
    own = [a for o, y in zip(halves, y_halves) for a in (o, y)]
    far = [a for o, y in zip(far_own, far_y) for a in (o, y)]
    _, width, half = gate_halves.shape
    hidden = 2 * half
    home_flag = home.astype(jnp.int32).reshape(1)
    expert_cat, expert_cat_t = pl.pallas_call(
        weights_kernel,
        in_specs=[smem_spec] + [any_spec] * 8,
        out_shape=(sds((width, 2 * hidden), BF16), sds((2 * hidden, width), BF16)),
        scratch_shapes=[pltpu.SemaphoreType.DMA((4,))],
        compiler_params=params(),
        cost_estimate=cost(1e9, 9 << 20),
        name="expert_weights",
    )(home_flag, *own[:4], *far[:4])
    ids_t, gates_t = route_ids.T, route_gates.T
    sel, send_input = pl.pallas_call(
        select_kernel,
        out_shape=(sds((slots, toks), BF16), sds((slots, width), BF16)),
        compiler_params=params(),
        cost_estimate=cost(2 * slots * toks * width, 4 << 20),
        name="select_rows",
    )(ids_t, moe_input)
    send_grad, mix_hi, mix_lo = pl.pallas_call(
        second_kernel,
        out_shape=(sds((slots, width), BF16), sds((toks, slots), BF16), sds((toks, slots), BF16)),
        compiler_params=params(),
        cost_estimate=cost(2 * slots * toks * width, 4 << 20),
        name="select_grads",
    )(ids_t, gates_t, sel, out_grad)

    def exchange(rows):
        shaped = rows.reshape(devices, SLOTS, width)
        return lax.all_to_all(shaped, both, split_axis=0, concat_axis=0, tiled=True).reshape(slots, width)

    recv_input = exchange(send_input)
    recv_grad = exchange(send_grad)

    def shift(rows, dz, dy):
        pairs = [(z * 4 + y, (z + dz) % 4 * 4 + (y + dy) % 4) for z in range(4) for y in range(4)]
        return lax.ppermute(rows, "head", pairs)

    proj_up, proj_dn = shift(out_proj, 1, 0), shift(out_proj, -1, 0)
    proj_far_up = shift(proj_up[: inner // 2], 1, 0)
    proj_far_dn = shift(proj_dn[inner // 2 :], -1, 0)

    flip = lambda i: blocks - 1 - i
    row_in = pl.BlockSpec((inner, BLOCK), lambda i: (0, flip(i)))
    tok_in = pl.BlockSpec((BLOCK, inner), lambda i: (flip(i), 0))
    tok_st = pl.BlockSpec((BLOCK, state), lambda i: (flip(i), 0))
    row_8 = pl.BlockSpec((8, BLOCK), lambda i: (0, flip(i)))
    blk_st = pl.BlockSpec((1, inner, state), lambda i: (flip(i), 0, 0))
    blk_8 = pl.BlockSpec((1, 8, state), lambda i: (flip(i), 0, 0))
    blk_w = pl.BlockSpec((1, heads, BLOCK, BLOCK), lambda i: (flip(i), 0, 0, 0))
    x_shape = sds((seq_rows, inner), BF16)
    w_shape = sds((blocks, heads, BLOCK, BLOCK), BF16)
    r_shape = sds((8, seq_rows), F32)
    w_hi, w_lo, to_start, to_end, to_last, x_hi, x_lo, e_hi, e_lo, t_hi, t_lo, block_sum, total = pl.pallas_call(
        prepare_kernel,
        grid=(blocks,),
        in_specs=[pl.BlockSpec((heads, BLOCK), lambda i: (0, flip(i))), tok_st, tok_st, row_in],
        out_specs=(blk_w,) * 2 + (row_8,) * 3 + (tok_in,) * 6 + (blk_8, whole((8, state))),
        out_shape=(w_shape,) * 2
        + (r_shape,) * 3
        + (x_shape,) * 6
        + (sds((blocks, 8, state), F32), sds((8, state), F32)),
        compiler_params=params(),
        cost_estimate=cost(4e9, 20 << 20),
        name="scan_prepare",
    )(log_decay, b_proj, c_proj, ssd_x.T)

    tile = 512
    row_spec = pl.BlockSpec((tile, width), lambda i: (i, 0))
    act_spec = pl.BlockSpec((tile, 2 * hidden), lambda i: (i, 0))
    factors = pl.pallas_call(
        acts_kernel,
        grid=(slots // tile,),
        in_specs=[row_spec, whole((width, 2 * hidden))],
        out_specs=act_spec,
        out_shape=sds((slots, 2 * hidden), F32),
        compiler_params=params(),
        cost_estimate=cost(4 * slots * width * hidden, 10 << 20),
        name="expert_acts",
    )(recv_input, expert_cat)
    expert_rows = pl.pallas_call(
        back_kernel,
        grid=(slots // tile,),
        in_specs=[smem_spec, row_spec, act_spec] + [any_spec] * 5,
        out_specs=row_spec,
        out_shape=sds((slots, width), BF16),
        scratch_shapes=[
            pltpu.VMEM((hidden, width), BF16),
            pltpu.VMEM((2 * hidden, width), BF16),
            pltpu.SemaphoreType.DMA((2,)),
            pltpu.SemaphoreType.DMA,
        ],
        compiler_params=params(),
        cost_estimate=cost(6 * slots * width * hidden, 14 << 20),
        name="expert_back",
    )(home_flag, recv_grad, factors, expert_cat_t, *own[4:], *far[4:])
    returned = exchange(expert_rows)

    resid_grad, first, second = pl.pallas_call(
        combine_kernel,
        grid=(2,),
        in_specs=[pl.BlockSpec((toks, slots // 2), lambda i: (0, i))] * 2
        + [pl.BlockSpec((slots // 2, width), lambda i: (i, 0)), whole((toks, width))],
        out_specs=(whole((toks, width)),) + (whole((toks // 2, width)),) * 2,
        out_shape=(sds((toks, width), BF16),) + (sds((toks // 2, width), BF16),) * 2,
        scratch_shapes=[pltpu.VMEM((toks, width), F32)],
        compiler_params=params(),
        cost_estimate=cost(4 * slots * toks * width, 4 << 20),
        name="combine_rows",
    )(mix_hi, mix_lo, returned, out_grad)
    up_first = shift(first, 0, 1)
    dn_second = shift(second, 0, -1)
    up_second = shift(second, 0, 1)
    dn_first = shift(first, 0, -1)
    far_first = shift(up_first, 0, 1)
    far_second = shift(dn_second, 0, -1)
    part_spec = whole((n_head // 4, inner, toks))
    part_shape = sds((n_head // 4, inner, toks), BF16)
    halves_spec = whole((toks // 2, width))
    to_0, to_3, to_2, to_1 = pl.pallas_call(
        project_kernel,
        grid=(1,),
        in_specs=[smem_spec, whole((toks, width))] + [halves_spec] * 6 + [any_spec] * 5,
        out_specs=(part_spec,) * 4,
        out_shape=(part_shape,) * 4,
        scratch_shapes=[
            pltpu.VMEM((4 * toks, width), BF16),
            pltpu.VMEM((4 * inner, width), BF16),
            pltpu.SemaphoreType.DMA((5,)),
        ],
        compiler_params=params(54000000),
        cost_estimate=cost(32 * inner * toks * width, 7 << 20),
        name="project_rows",
    )(
        (head & 3).reshape(1),
        resid_grad,
        up_first,
        up_second,
        dn_first,
        dn_second,
        far_first,
        far_second,
        out_proj,
        proj_up,
        proj_far_up,
        proj_far_dn,
        proj_dn,
    )
    from_2 = shift(to_2, 2, 0)
    from_3 = shift(to_1, 1, 0)
    from_1 = shift(to_3, -1, 0)

    pay_rows = inner + 32
    future, payload, grads = pl.pallas_call(
        functools.partial(state_kernel, heads),
        out_shape=(
            sds((blocks, inner, state), F32),
            sds((n_seq, pay_rows, state), BF16),
            sds((n_head, inner, toks), BF16),
        ),
        grid=(1,),
        in_specs=[smem_spec]
        + [part_spec] * 4
        + [
            whole((seq_rows, state)),
            whole((8, seq_rows)),
            whole((blocks, 8, state)),
            whole((8, state)),
        ],
        out_specs=(
            whole((blocks, inner, state)),
            whole((n_seq, pay_rows, state)),
            whole((n_head, inner, toks)),
        ),
        compiler_params=params(55500000),
        cost_estimate=cost(1e9, 4 << 20),
        name="scan_state",
    )((head >> 2).reshape(1), to_0, from_1, from_2, from_3, c_proj, to_start, block_sum, total)
    pays = lax.all_to_all(payload, seq_axes, split_axis=0, concat_axis=0, tiled=True)
    pair = 2
    spec = lambda *shape: pl.BlockSpec(shape, lambda i: (i,) + (0,) * (len(shape) - 1))
    cols = lambda *shape: pl.BlockSpec(shape, lambda i: (0, i))
    tok_in2, tok_st2 = spec(pair * BLOCK, inner), spec(pair * BLOCK, state)
    row_in2, row_82 = cols(inner, pair * BLOCK), cols(8, pair * BLOCK)
    w_spec = spec(pair, heads, BLOCK, BLOCK)
    part_x, part_b = pl.pallas_call(
        functools.partial(intra_kernel, heads),
        grid=(blocks // pair,),
        in_specs=[smem_spec, w_spec, w_spec, spec(pair * BLOCK // toks, inner, toks)]
        + [tok_in2] * 4
        + [row_82, tok_st2, tok_st2, spec(pair, inner, state)],
        out_specs=(row_in2, tok_st2),
        out_shape=(sds((inner, seq_rows), F32), sds((seq_rows, state), F32)),
        compiler_params=params(),
        cost_estimate=cost(4e9, 16 << 20),
        name="scan_intra",
    )(skip_gain, w_hi, w_lo, grads, x_hi, x_lo, e_hi, e_lo, to_end, b_proj, c_proj, future)
    partial_b, in_hi, in_lo = pl.pallas_call(
        functools.partial(finish_b_kernel, heads),
        grid=(2,),
        in_specs=[
            smem_spec,
            whole((n_seq, pay_rows, state)),
            spec(seq_rows // 2, inner),
            spec(seq_rows // 2, inner),
            spec(seq_rows // 2, state),
        ],
        out_specs=(spec(seq_rows // 2, state), whole((inner, state)), whole((inner, state))),
        out_shape=(sds((seq_rows, state), BF16), sds((inner, state), BF16), sds((inner, state), BF16)),
        compiler_params=params(),
        cost_estimate=cost(4e8, 6 << 20),
        name="scan_finish_b",
    )(seq.reshape(1), pays, t_hi, t_lo, part_b)
    shares = lax.all_to_all(
        partial_b.reshape(n_head, seq_rows // n_head, state), "head", split_axis=0, concat_axis=0, tiled=True
    )
    grad_x = pl.pallas_call(
        functools.partial(finish_x_kernel, heads),
        grid=(blocks // pair,),
        in_specs=[whole((inner, state)), whole((inner, state)), row_82, tok_st2, row_in2],
        out_specs=row_in2,
        out_shape=sds((inner, seq_rows), F32),
        compiler_params=params(),
        cost_estimate=cost(4e8, 6 << 20),
        name="scan_finish_x",
    )(in_hi, in_lo, to_last, b_proj, part_x)
    b_grad = jnp.sum(shares.astype(F32), axis=0)
    return (resid_grad, grad_x.T, b_grad)


def solution(mesh):
    n_seq, n_head = mesh.shape["seq"], mesh.shape["head"]
    fine = jax.sharding.Mesh(mesh.devices.reshape(n_seq // 2, 2, n_head), ("x", "core", "head"))

    seq, every = ("x", "core"), ("x", "core", "head")
    return jax.shard_map(
        shards,
        mesh=fine,
        in_specs=(
            P(every, None),
            P(every, None),
            P(every, None),
            P(every, None),
            P(every, None, None),
            P(every, None, None),
            P(every, None, None),
            P("head", None),
            P(seq, "head"),
            P(seq, None),
            P(seq, None),
            P("head", seq),
            P("head"),
        ),
        out_specs=(P(every, None), P(seq, "head"), P(every, None)),
        check_vma=False,
    )
```
